32 devices in a mesh: slab: 2 (over y), gx: 4 (over z), gy: 4 (over x, core).
Axes of the slice: x: 2, y: 2, z: 4, core: 2. Of those that a mesh axis runs over, the one named last changes fastest.
Arguments:
- charge: float32 [32, 512, 512], P(None, ('slab', 'gx'), 'gy'), parts along dimension 1, may hold values from -6 to 6
- surface_charge: float32 [2, 512, 512], P(None, ('slab', 'gx'), 'gy'), parts along dimension 1, may hold values from -6 to 6
Outputs:
- potential: float32 [32, 512, 512], P(None, ('slab', 'gx'), 'gy'), parts along dimension 1
- interface_residual: float32 [32, 512, 512], P(None, ('slab', 'gx'), 'gy'), parts along dimension 1
The draws below stay inside these ranges and needn't reach their ends.
There are 2 independent parts, one for each index of `slab`. The reference program is written for one: setup_inputs(seed, part) draws one part's arguments, and reference() takes and returns one part's arrays. A program takes and returns all parts, laid end to end along the dimension named above; each array names one. Nothing has to cross between parts.
All inputs are finite; a program needn't handle non-finite values.
Results may differ from the reference program's by a relative error of at most 0.0003.
Values sent between devices are 32-bit elements; how exact they have to be, the bound alone decides.
No kernel may reach another device: no remote copies, remote signals or barrier semaphores. Data moves between devices by JAX's collectives and lax.ppermute only.
A program may use at most 64 MiB of HBM per device.

```python
import jax
import jax.numpy as jnp
from jax import lax

BLOCK_X = 64
BLOCK_Y = 128
DEPTH = 32
ITERS = 2
NX = 256
NY = 512
N_GX = 4
N_GY = 4


def levels(key, dims, pieces, least, largest):
    level, own = 1.0, jax.random.fold_in(key, 6)
    for axis_at, blocks in pieces:
        heights = jnp.exp(jax.random.uniform(jax.random.fold_in(own, axis_at), (blocks,), jnp.float32, least / len(pieces), largest / len(pieces)))
        level = level * jnp.repeat(heights, dims[axis_at] // blocks).reshape([-1 if axis == axis_at else 1 for axis in range(len(dims))])
    return level


def noise(rng, extent, width, most, split=(), dtype=jnp.bfloat16):
    loudness = levels(rng, extent, split, -0.22, 0.18) if split else 1.0
    result = jax.random.normal(rng, extent, jnp.float32) * width * loudness
    return jnp.minimum(jnp.maximum(result, -most), most).astype(dtype)


def setup_inputs(seed: int = 0, part: int = 0) -> dict:
    key_of = jax.random.split(jax.random.key(seed), 3)
    own_keys = jax.random.split(jax.random.fold_in(key_of[2], part), 3)
    return {
        "charge": noise(own_keys[0], (DEPTH, NX, NY), 1.0, 6.0, ((1, 4), (2, 4)), jnp.float32),
        "surface_charge": noise(own_keys[1], (2, NX, NY), 1.0, 6.0, ((1, 4), (2, 4)), jnp.float32),
    }


SCREEN = 0.02

def sine_table(count):
    index = jnp.arange(1, count).astype(jnp.float32)
    return jnp.sqrt(2.0 / count) * jnp.sin(jnp.pi * jnp.outer(index, index) / count)

def cosine_table(count):
    place = jnp.arange(count).astype(jnp.float32) + 0.5
    order = jnp.arange(count).astype(jnp.float32)
    factor = jnp.where(order == 0.0, jnp.sqrt(1.0 / count), jnp.sqrt(2.0 / count))
    return factor[None, :] * jnp.cos(jnp.pi * jnp.outer(place, order) / count)

def spectrum_table():
    across = 2.0 - 2.0 * jnp.cos(jnp.pi * jnp.arange(1, BLOCK_X).astype(jnp.float32) / BLOCK_X)
    along = 2.0 - 2.0 * jnp.cos(jnp.pi * jnp.arange(1, BLOCK_Y).astype(jnp.float32) / BLOCK_Y)
    vertical = 2.0 - 2.0 * jnp.cos(jnp.pi * jnp.arange(DEPTH).astype(jnp.float32) / DEPTH)
    return SCREEN + vertical[:, None, None] + across[None, :, None] + along[None, None, :]

def apply_full(field):
    beside = jnp.roll(field, -1, 1) + jnp.roll(field, 1, 1) + jnp.roll(field, -1, 2) + jnp.roll(field, 1, 2)
    upper = jnp.concatenate([field[1:], field[-1:]], 0)
    lower = jnp.concatenate([field[:1], field[:-1]], 0)
    return (6.0 + SCREEN) * field - beside - upper - lower

def solve_interior(field):
    high = lax.Precision.HIGHEST
    sines_x = sine_table(BLOCK_X)
    sines_y = sine_table(BLOCK_Y)
    cosines = cosine_table(DEPTH)
    spectrum = spectrum_table()
    blocks = field.reshape(DEPTH, N_GX, BLOCK_X, N_GY, BLOCK_Y)[:, :, 1:, :, 1:]
    hat = jnp.einsum('zk,zgxhy->kgxhy', cosines, blocks, precision=high)
    hat = jnp.einsum('xa,kgxhy->kgahy', sines_x, hat, precision=high)
    hat = jnp.einsum('yb,kgahy->kgahb', sines_y, hat, precision=high)
    hat = hat / spectrum[:, None, :, None, :]
    back = jnp.einsum('yb,kgahb->kgahy', sines_y, hat, precision=high)
    back = jnp.einsum('xa,kgahy->kgxhy', sines_x, back, precision=high)
    back = jnp.einsum('zk,kgxhy->zgxhy', cosines, back, precision=high)
    back = jnp.pad(back, ((0, 0), (0, 0), (1, 0), (0, 0), (1, 0)))
    return back.reshape(DEPTH, N_GX * BLOCK_X, N_GY * BLOCK_Y)

def reference(charge, surface_charge):
    size_x = charge.shape[1]
    size_y = charge.shape[2]
    edge_x = jnp.arange(size_x) % BLOCK_X == 0
    edge_y = jnp.arange(size_y) % BLOCK_Y == 0
    gamma = jnp.where(edge_x[:, None] | edge_y[None, :], 1.0, 0.0).astype(jnp.float32)[None]
    source = charge.at[0].add(surface_charge[0]).at[-1].add(surface_charge[1])
    base = solve_interior(source)
    reduced = gamma * (source - apply_full(base))

    def schur(probe):
        lifted = -solve_interior(apply_full(probe))
        return gamma * apply_full(probe + lifted)
    iterate = jnp.zeros_like(reduced)
    residual = reduced
    direction = reduced
    norm_now = jnp.sum(residual * residual)
    for step in range(ITERS):
        image = schur(direction)
        alpha = norm_now / jnp.sum(direction * image)
        iterate = iterate + alpha * direction
        residual = residual - alpha * image
        norm_next = jnp.sum(residual * residual)
        direction = residual + norm_next / norm_now * direction
        norm_now = norm_next
    potential = iterate + base - solve_interior(apply_full(iterate))
    return (potential, residual)
```

```python
import numpy as np
import jax
import jax.numpy as jnp
from jax import lax
from jax.experimental import pallas as pl
from jax.experimental.pallas import tpu as pltpu
from jax.sharding import PartitionSpec as P
import ml_dtypes

SCREEN = 0.02
BF16 = jnp.bfloat16
F32 = jnp.float32


def sine_ext(n):
    i = np.arange(n)
    table = np.sqrt(2.0 / n) * np.sin(np.pi * np.outer(i, i) / n)
    table[0, 0] = 1.0
    return table


def split_bf16(table):
    hi = table.astype(np.float32).astype(ml_dtypes.bfloat16)
    lo = (table - hi.astype(np.float64)).astype(np.float32).astype(ml_dtypes.bfloat16)
    return hi, lo


def make_tables(depth, width, height):
    lanes = 128
    groups = lanes // depth
    rows = height // groups
    tab = {}
    hi, lo = split_bf16(sine_ext(height))
    tab["eyw"] = np.block([[hi, lo], [hi, np.zeros_like(lo)]])
    hi, lo = split_bf16(sine_ext(width))
    tab["exw"] = np.concatenate([hi, lo, hi], 1)
    z = np.arange(depth)
    cos = np.cos(np.pi * np.outer(z + 0.5, z) / depth) * np.sqrt(2.0 / depth)
    cos[:, 0] = np.sqrt(1.0 / depth)
    tab["cz"] = cos.astype(np.float32)
    czt = np.zeros((lanes, lanes))
    czt[:depth, :depth] = cos.T
    tab["czt"] = czt.astype(np.float32)
    lz = SCREEN + 2.0 - 2.0 * np.cos(np.pi * z / depth)
    a = np.arange(width)
    b = np.arange(height)
    lx = 2.0 - 2.0 * np.cos(np.pi * a / width)
    ly = 2.0 - 2.0 * np.cos(np.pi * b / height)
    sx = np.sqrt(2.0 / width) * np.sin(np.pi * a / width)
    sy = np.sqrt(2.0 / height) * np.sin(np.pi * b / height)
    sga = np.where(a % 2 == 1, 1.0, -1.0)
    sgb = np.where(b % 2 == 1, 1.0, -1.0)
    inside = (a[:, None] > 0) & (b[None, :] > 0)
    inv = np.where(inside[None], 1.0 / (lz[:, None, None] + lx[None, :, None] + ly[None, None, :]), 0.0)
    tab["inv"] = inv.astype(np.float32)

    def to_rows(kb):
        return kb.T.reshape(groups, rows, depth).transpose(1, 0, 2).reshape(rows, lanes)

    def to_cols(ka):
        return np.tile(ka.T, (1, groups))

    inv2 = inv.transpose(2, 1, 0).reshape(groups, rows, width, depth)
    tab["inv2"] = inv2.transpose(1, 2, 0, 3).reshape(rows, width, lanes).astype(np.float32)
    ones = np.ones((depth, 1))
    odd_a, odd_b = sga > 0, sgb > 0
    sx2, sy2 = (sx**2)[None, :, None] * inv, (sy**2)[None, None, :] * inv
    tab["rowt"] = np.stack([
        to_rows(ones * sy),
        to_rows(ones * (sy * sgb)),
        to_rows(sx2[:, odd_a].sum(1)),
        to_rows(sx2[:, ~odd_a].sum(1)),
        to_rows((lz[:, None] + 2.0 + ly) * (b > 0)),
    ]).astype(np.float32)
    tab["colt"] = np.stack([
        to_cols(ones * sx),
        to_cols(ones * (sx * sga)),
        to_cols(sy2[:, :, odd_b].sum(2)),
        to_cols(sy2[:, :, ~odd_b].sum(2)),
        to_cols((lz[:, None] + 2.0 + lx) * (a > 0)),
    ]).astype(np.float32)
    tab["crnt"] = np.tile(np.tile(lz + 4.0, groups)[None], (8, 1)).astype(np.float32)
    tab["sx0"] = np.tile(sx[:, None], (1, height)).astype(np.float32)
    lane = np.zeros((8, height))
    lane[0], lane[1] = sy, sy * sgb
    lane[2], lane[3] = np.where(b > 0, sy, 1.0), sy * sgb
    tab["sy0"] = lane.astype(np.float32)
    return tab


def cosine_fwd(xs, scale):
    n = len(xs)
    if n == 1:
        return [xs[0] * (scale / np.sqrt(2.0))]
    half = n // 2
    even = cosine_fwd([xs[j] + xs[n - 1 - j] for j in range(half)], scale)
    diff = [xs[j] - xs[n - 1 - j] for j in range(half)]
    out = [None] * n
    for m in range(half):
        out[2 * m] = even[m]
        acc = None
        for j in range(half):
            term = diff[j] * float(scale * np.cos(np.pi * (2 * m + 1) * (2 * j + 1) / (2 * n)))
            acc = term if acc is None else acc + term
        out[2 * m + 1] = acc
    return out


def cosine_back(ys, scale):
    n = len(ys)
    if n == 1:
        return [ys[0] * (scale / np.sqrt(2.0))]
    half = n // 2
    even = cosine_back(ys[0::2], scale)
    out = [None] * n
    for j in range(half):
        acc = None
        for m in range(half):
            term = ys[2 * m + 1] * float(scale * np.cos(np.pi * (2 * m + 1) * (2 * j + 1) / (2 * n)))
            acc = term if acc is None else acc + term
        out[j] = even[j] + acc
        out[n - 1 - j] = even[j] - acc
    return out


def halves(x):
    hi = x.astype(BF16)
    return hi, (x - hi.astype(F32)).astype(BF16)


def times_sy(x, eyw):
    hi, lo = halves(x)
    n = x.shape[1]
    out = jnp.dot(jnp.concatenate([hi, lo], 1), eyw, preferred_element_type=F32)
    return out[:, :n] + out[:, n:]


def sx_times(exw, x):
    hi, lo = halves(x)
    return jnp.dot(exw, jnp.concatenate([hi, hi, lo], 0), preferred_element_type=F32)


def lane_id(shape):
    return lax.broadcasted_iota(jnp.int32, shape, 1)


def by_group(pieces, depth):
    group = lane_id(pieces[0].shape) // depth
    out = pieces[0]
    for h in range(1, len(pieces)):
        out = jnp.where(group == h, pieces[h], out)
    return out


def spread(x, depth):
    width = x.shape[1] // 2
    while width >= depth:
        x = x + pltpu.roll(x, width, 1)
        width //= 2
    return x


def pack(col, depth):
    groups = 128 // depth
    size = col.shape[0] // groups
    return by_group([col[h * size:(h + 1) * size] for h in range(groups)], depth)


def unpack(packed, depth):
    groups = 128 // depth
    group = lane_id(packed.shape) // depth
    return jnp.concatenate(
        [spread(jnp.where(group == h, packed, 0.0), depth) for h in range(groups)], 0
    )


def copies_t(kb):
    groups = 128 // kb.shape[0]
    return jnp.concatenate([kb] * groups, 0).T


def rows_from(kbt, depth):
    groups = 128 // depth
    size = kbt.shape[0] // groups
    return by_group([kbt[h * size:(h + 1) * size] for h in range(groups)], depth)


def rows_back(row, depth):
    groups = 128 // depth
    parts = [row] + [pltpu.roll(row, 128 - h * depth, 1) for h in range(1, groups)]
    return jnp.concatenate(parts, 0).T[:depth]


def total(x):
    return jnp.sum(x, 0, keepdims=True)


def sub_sums(ref):
    plus = minus = None
    for s in range(8):
        part = ref[:, s, :]
        if s % 2 == 1:
            plus = part if plus is None else plus + part
        else:
            minus = part if minus is None else minus + part
    return plus + minus, plus - minus


def with_tail(body, tails):
    width = body.shape[1]
    rows = list(tails) + [jnp.zeros((8 - len(tails), width), F32)]
    return jnp.concatenate([body, jnp.concatenate(rows, 0)], 0)


def front_kernel(charge, surf, eyw, exw, inv, sx0, sy0, base, px, nx, py, ny, work, part, first):
    depth, width, height = charge.shape
    scale = np.sqrt(2.0 / depth)

    def columns(i, carry):
        at = pl.ds(pl.multiple_of(i * 8, 8), 8)
        xs = [charge[z, at, :] for z in range(depth)]
        xs[0] = xs[0] + surf[0, at, :]
        xs[-1] = xs[-1] + surf[1, at, :]
        for k, value in enumerate(cosine_fwd(xs, scale)):
            work[k, at, :] = value
        return carry

    lax.fori_loop(0, width // 8, columns, 0)
    step = 4
    for c in range(0, depth, step):
        block = work[c:c + step].reshape(step * width, height)
        work[c:c + step] = times_sy(block, eyw[...]).reshape(step, width, height)
    lane = lane_id((width, 128))
    zero = jnp.zeros((width, 128), F32)
    near, far, own = zero, zero, zero
    for c in range(0, depth, 2):
        pair = sx_times(exw[...], jnp.concatenate([work[c], work[c + 1]], 1))
        for k in (c, c + 1):
            spec = pair[:, (k - c) * height:(k - c + 1) * height]
            inner = spec * inv[k]
            base[k] = inner
            first[k] = spec[0:8]
            part[k] = jnp.sum((inner * sx0[...]).reshape(width // 8, 8, height), 0)
            here = lane % depth == k
            near = jnp.where(here, jnp.sum(inner * sy0[0:1, :], 1, keepdims=True), near)
            far = jnp.where(here, jnp.sum(inner * sy0[1:2, :], 1, keepdims=True), far)
            own = jnp.where(here, spec[:, 0:1], own)
    row_near, row_far = sub_sums(part)
    own_t = copies_t(first[:, 0, :])
    corner = own_t[0:1]
    row = rows_from(own_t + copies_t(row_near), depth)
    at_zero = (lax.broadcasted_iota(jnp.int32, row.shape, 0) == 0) & (lane_id(row.shape) < depth)
    row = jnp.where(at_zero, 0.0, row)
    col = jnp.where(lax.broadcasted_iota(jnp.int32, own.shape, 0) == 0, 0.0, own + near)
    px[...] = with_tail(row, [corner])
    nx[...] = with_tail(rows_from(copies_t(row_far), depth), [])
    py[...] = with_tail(pack(col, depth), [corner])
    ny[...] = with_tail(pack(far, depth), [])


def assemble(depth, own, got):
    (px, nx, py, ny), (from_nx, from_px, from_ny, from_py) = own, got
    rows, cols = px.shape[0] - 8, py.shape[0] - 8
    row = px[:rows] + from_px[:rows]
    row_n = from_nx[:rows] + nx[:rows]
    col = unpack(py[:cols] + from_py[:cols], depth)
    col_n = unpack(from_ny[:cols] + ny[:cols], depth)
    c00 = px[rows:rows + 1] + from_px[rows:rows + 1] + from_py[cols:cols + 1]
    cx0 = from_nx[rows:rows + 1] + nx[rows:rows + 1] + from_py[cols + 1:cols + 2]
    c0y = from_ny[cols:cols + 1] + ny[cols:cols + 1] + from_px[rows + 1:rows + 2]
    return row, row_n, col, col_n, c00, cx0, c0y


def sizes(rows, cols):
    offs = np.cumsum([0, rows, rows, cols, cols])
    return [slice(int(offs[i]), int(offs[i + 1])) for i in range(4)] + [int(offs[4])]


def unpacked_state(state, rows, cols):
    s = sizes(rows, cols)
    at = s[4]
    return tuple(state[s[i], :] for i in range(4)) + tuple(state[at + i:at + i + 1, :] for i in range(3))


def schur_kernel(depth, want_moments, *refs):
    own, got = [r[...] for r in refs[0:4]], [r[...] for r in refs[4:8]]
    inv2, rowt, colt, crnt = refs[8:12]
    rest = list(refs[12:])
    before = rest.pop(0) if want_moments else None
    state, px, nx, py, ny = rest[:5]
    moments = rest[5] if want_moments else None
    part, odd_rows, even_rows = rest[-3:]
    row, row_n, col, col_n, c00, cx0, c0y = assemble(depth, own, got)
    rows, cols = row.shape[0], col.shape[0]
    s = sizes(rows, cols)
    for i, piece in enumerate((row, row_n, col, col_n)):
        state[s[i], :] = piece
    state[s[4]:s[4] + 8, :] = jnp.concatenate([c00, cx0, c0y, jnp.zeros((5, 128), F32)], 0)
    sy, sys, g_odd, g_even, d_row = (rowt[i] for i in range(5))
    sx, sxs, h_odd, h_even, d_col = (colt[i] for i in range(5))
    row_p, row_m, col_p, col_m = row + row_n, row - row_n, col + col_n, col - col_n
    odd_rows[...] = row_p * sy
    even_rows[...] = row_m * sy
    col_w = (col_m * sx, col_p * sx)
    odd = lax.broadcasted_iota(jnp.int32, (8, 128), 0) % 2 == 1
    acc = [None, None]
    for r in range(rows):
        table = inv2[r].reshape(cols // 8, 8, 128)
        part[r] = jnp.sum(table * col_w[r % 2].reshape(cols // 8, 8, 128), 0)
        pick = jnp.where(odd, odd_rows[r:r + 1, :], even_rows[r:r + 1, :])
        term = table * pick[None]
        acc[r % 2] = term if acc[r % 2] is None else acc[r % 2] + term
    row_s, row_d = sub_sums(part)
    acc_s = spread((acc[1] + acc[0]).reshape(cols, 128), depth)
    acc_d = spread((acc[1] - acc[0]).reshape(cols, 128), depth)
    diag_o, diag_e = g_odd * row_p, g_even * row_m
    x_near = sy * row_s + (diag_o + diag_e)
    x_far = sy * row_d + (diag_o - diag_e)
    diag_o, diag_e = h_odd * col_p, h_even * col_m
    y_near = sx * acc_s + (diag_o + diag_e)
    y_far = sx * acc_d + (diag_o - diag_e)
    row_img = d_row * row - sy * c00 - sys * c0y - x_near
    col_img = d_col * col - sx * c00 - sxs * cx0 - y_near
    row_end0 = spread(total(sy * row), depth)
    row_end1 = spread(total(sys * row), depth)
    row_end1n = spread(total(sys * row_n), depth)
    col_end0 = total(sx * col)
    col_end1 = total(sxs * col)
    col_end1n = total(sxs * col_n)
    q00 = crnt[0:1, :] * c00 - row_end0 - col_end0
    px[...] = with_tail(row_img, [q00])
    nx[...] = with_tail(-x_far, [-col_end1, -col_end1n])
    py[...] = with_tail(pack(col_img, depth), [q00])
    ny[...] = with_tail(pack(-y_far, depth), [-row_end1, -row_end1n])
    if want_moments:
        row0, _, col0, _, c000, _, _ = unpacked_state(before, rows, cols)
        share = depth / 128.0

        def dot(x, y):
            return total(x[0] * y[0]) + share * (total(x[1] * y[1]) + x[2] * y[2])

        v0, v1 = (row0, col0, c000), (row, col, c00)
        m3 = total(row * row_img - row_n * x_far) + share * (
            total(col * col_img - col_n * y_far) + c00 * q00 - c0y * row_end1 - cx0 * col_end1
        )
        moments[...] = jnp.concatenate([dot(v0, v0), dot(v0, v1), dot(v1, v1), m3, jnp.zeros((4, 128), F32)], 0)


def back_kernel(depth, n_moments, *refs):
    base, s0, s1, px, py, from_px, from_py = refs[:7]
    moms = refs[7:7 + n_moments]
    eyw, exw, inv, sx0, sy0, cz, czt = refs[7 + n_moments:14 + n_moments]
    potential, residual, work = refs[14 + n_moments:]
    _, width, height = base.shape
    rows, cols = px.shape[0] - 8, width
    packed = py.shape[0] - 8
    m = moms[0][...]
    for other in moms[1:]:
        m = m + other[...]
    m = jnp.broadcast_to(jnp.sum(m, 1, keepdims=True), (8, 128))
    m0 = m[0:1]
    n1, n2, n3 = m[1:2] / m0, m[2:3] / m0, m[3:4] / m0
    det = n1 * n3 - n2 * n2
    fine = det > 1e-6 * (n1 * n3)
    safe = jnp.where(fine, det, 1.0)
    c0 = jnp.where(fine, (n3 - n1 * n2) / safe, 1.0 / n1)
    c1 = jnp.where(fine, (n1 * n1 - n2) / safe, 0.0)
    v0 = unpacked_state(s0, rows, cols)
    v1 = unpacked_state(s1, rows, cols)
    row, row_n, col, col_n, c00 = (c0 * v0[i] + c1 * v1[i] for i in range(5))
    row2 = px[:rows, :] + from_px[:rows, :]
    col2 = unpack(py[:packed, :] + from_py[:packed, :], depth)
    c2 = px[rows:rows + 1, :] + from_px[rows:rows + 1, :] + from_py[packed:packed + 1, :]
    res_row = v0[0] - c0 * v1[0] - c1 * row2
    res_col = v0[2] - c0 * v1[2] - c1 * col2
    res_c = v0[4] - c0 * v1[4] - c1 * c2
    at_zero = (lax.broadcasted_iota(jnp.int32, row.shape, 0) == 0) & (lane_id(row.shape) < depth)
    row_p = rows_back(row + row_n, depth)
    row_m = rows_back(row - row_n, depth)
    row_full = rows_back(jnp.where(at_zero, c00, row), depth)
    res_row = rows_back(jnp.where(at_zero, res_c, res_row), depth)
    odd = lax.broadcasted_iota(jnp.int32, (8, height), 0) % 2 == 1
    top = lax.broadcasted_iota(jnp.int32, (width, height), 0) == 0
    lane0 = lane_id((width, height)) == 0
    for c in range(0, depth, 2):
        pieces = []
        for k in (c, c + 1):
            pick = jnp.where(odd, row_p[k:k + 1], row_m[k:k + 1])
            pick = jnp.broadcast_to(pick[None], (width // 8, 8, height)).reshape(width, height)
            rim = sx0[...] * pick + col[:, k:k + 1] * sy0[2:3, :] + col_n[:, k:k + 1] * sy0[3:4, :]
            weight = jnp.where(lane0, 1.0, inv[k])
            pieces.append(jnp.where(top, row_full[k:k + 1], base[k] + weight * rim))
        pair = sx_times(exw[...], jnp.concatenate(pieces, 1))
        work[c] = pair[:, :height]
        work[c + 1] = pair[:, height:]
    step = 4
    for c in range(0, depth, step):
        block = work[c:c + step].reshape(step * width, height)
        work[c:c + step] = times_sy(block, eyw[...]).reshape(step, width, height)
    scale = np.sqrt(2.0 / depth)

    def columns(i, carry):
        at = pl.ds(pl.multiple_of(i * 8, 8), 8)
        for z, value in enumerate(cosine_back([work[k, at, :] for k in range(depth)], scale)):
            potential[z, at, :] = value
        return carry

    lax.fori_loop(0, width // 8, columns, 0)
    high = lax.Precision.HIGHEST
    rim_row = jnp.dot(cz[...], times_sy(res_row, eyw[...]), precision=high, preferred_element_type=F32)
    res_col = sx_times(exw[...], res_col)
    rim_col = jnp.dot(res_col, czt[...], precision=high, preferred_element_type=F32)
    for z in range(depth):
        residual[z] = jnp.where(top, rim_row[z:z + 1], jnp.where(lane0, rim_col[:, z:z + 1], 0.0))


def shifted(value, axis, by):
    n = lax.axis_size(axis)
    return lax.ppermute(value, axis, [(i, (i + by) % n) for i in range(n)])


def exchange(px, nx, py, ny):
    return (shifted(px, "gx", -1), shifted(nx, "gx", 1), shifted(py, "gy", -1), shifted(ny, "gy", 1))


def pieces_over(value, axis):
    n, stride = lax.axis_size(axis), 1
    while True:
        radix = 4 if n % 4 == 0 else 2 if n % 2 == 0 else n
        parts = [value] + [shifted(value, axis, stride * j) for j in range(1, radix)]
        n, stride = n // radix, stride * radix
        if n == 1:
            return parts
        value = sum(parts[1:], parts[0])


def call(kernel, outs, scratch):
    return pl.pallas_call(
        kernel,
        out_shape=[jax.ShapeDtypeStruct(shape, F32) for shape in outs],
        scratch_shapes=[pltpu.VMEM(shape, F32) for shape in scratch],
        compiler_params=pltpu.CompilerParams(vmem_limit_bytes=48 * 1024 * 1024),
    )


def on_device(charge, surface_charge):
    depth, width, height = charge.shape
    tab = {name: jnp.asarray(value) for name, value in make_tables(depth, width, height).items()}
    rows, packed = height * depth // 128, width * depth // 128
    msgs = [(rows + 8, 128)] * 2 + [(packed + 8, 128)] * 2
    state = (2 * rows + 2 * width + 8, 128)
    block = (depth, width, height)
    base, *own = call(front_kernel, [block] + msgs, [block, (depth, 8, height), (depth, 8, height)])(
        charge, surface_charge, tab["eyw"], tab["exw"], tab["inv"], tab["sx0"], tab["sy0"]
    )
    got = exchange(*own)
    tables = (tab["inv2"], tab["rowt"], tab["colt"], tab["crnt"])
    scratch = [(rows, 8, 128), (rows, 128), (rows, 128)]
    s0, *own = call(lambda *r: schur_kernel(depth, False, *r), [state] + msgs, scratch)(*own, *got, *tables)
    got = exchange(*own)
    s1, px, nx, py, ny, moments = call(
        lambda *r: schur_kernel(depth, True, *r), [state] + msgs + [(8, 128)], scratch
    )(*own, *got, *tables, s0)
    parts = pieces_over(moments, "gx")
    from_px, from_py = shifted(nx, "gx", 1), shifted(ny, "gy", 1)
    parts = pieces_over(sum(parts[1:], parts[0]), "gy")
    return call(lambda *r: back_kernel(depth, len(parts), *r), [block, block], [block])(
        base, s0, s1, px, py, from_px, from_py, *parts,
        tab["eyw"], tab["exw"], tab["inv"], tab["sx0"], tab["sy0"], tab["cz"], tab["czt"],
    )


def solution(mesh):
    spec = P(None, ("slab", "gx"), "gy")
    return jax.shard_map(
        on_device, mesh=mesh, in_specs=(spec, spec), out_specs=(spec, spec), check_vma=False
    )
```

```python
import numpy as np
import jax
import jax.numpy as jnp
from jax import lax
from jax.experimental import pallas as pl
from jax.experimental.pallas import tpu as pltpu
from jax.sharding import PartitionSpec as P
import ml_dtypes

SCREEN = 0.02
BF16 = jnp.bfloat16
F32 = jnp.float32


def sine_ext(n):
    i = np.arange(n)
    table = np.sqrt(2.0 / n) * np.sin(np.pi * np.outer(i, i) / n)
    table[0, 0] = 1.0
    return table


def split_bf16(table):
    hi = table.astype(np.float32).astype(ml_dtypes.bfloat16)
    lo = (table - hi.astype(np.float64)).astype(np.float32).astype(ml_dtypes.bfloat16)
    return hi, lo


def make_tables(depth, width, height):
    lanes = 128
    groups = lanes // depth
    rows = height // groups
    tab = {}
    hi, lo = split_bf16(sine_ext(height))
    tab["eyw"] = np.block([[hi, lo], [hi, np.zeros_like(lo)]])
    hi, lo = split_bf16(sine_ext(width))
    tab["exw"] = np.concatenate([hi, lo, hi], 1)
    z = np.arange(depth)
    cos = np.cos(np.pi * np.outer(z + 0.5, z) / depth) * np.sqrt(2.0 / depth)
    cos[:, 0] = np.sqrt(1.0 / depth)
    tab["cz"] = cos.astype(np.float32)
    czt = np.zeros((lanes, lanes))
    czt[:depth, :depth] = cos.T
    tab["czt"] = czt.astype(np.float32)
    lz = SCREEN + 2.0 - 2.0 * np.cos(np.pi * z / depth)
    a = np.arange(width)
    b = np.arange(height)
    lx = 2.0 - 2.0 * np.cos(np.pi * a / width)
    ly = 2.0 - 2.0 * np.cos(np.pi * b / height)
    sx = np.sqrt(2.0 / width) * np.sin(np.pi * a / width)
    sy = np.sqrt(2.0 / height) * np.sin(np.pi * b / height)
    sga = np.where(a % 2 == 1, 1.0, -1.0)
    sgb = np.where(b % 2 == 1, 1.0, -1.0)
    inside = (a[:, None] > 0) & (b[None, :] > 0)
    inv = np.where(inside[None], 1.0 / (lz[:, None, None] + lx[None, :, None] + ly[None, None, :]), 0.0)
    tab["inv"] = inv.astype(np.float32)

    def to_rows(kb):
        return kb.T.reshape(groups, rows, depth).transpose(1, 0, 2).reshape(rows, lanes)

    def to_cols(ka):
        return np.tile(ka.T, (1, groups))

    inv2 = inv.transpose(2, 1, 0).reshape(groups, rows, width, depth)
    tab["inv2"] = inv2.transpose(1, 2, 0, 3).reshape(rows, width, lanes).astype(np.float32)
    ones = np.ones((depth, 1))
    odd_a, odd_b = sga > 0, sgb > 0
    sx2, sy2 = (sx**2)[None, :, None] * inv, (sy**2)[None, None, :] * inv
    tab["rowt"] = np.stack([
        to_rows(ones * sy),
        to_rows(ones * (sy * sgb)),
        to_rows(sx2[:, odd_a].sum(1)),
        to_rows(sx2[:, ~odd_a].sum(1)),
        to_rows((lz[:, None] + 2.0 + ly) * (b > 0)),
    ]).astype(np.float32)
    tab["colt"] = np.stack([
        to_cols(ones * sx),
        to_cols(ones * (sx * sga)),
        to_cols(sy2[:, :, odd_b].sum(2)),
        to_cols(sy2[:, :, ~odd_b].sum(2)),
        to_cols((lz[:, None] + 2.0 + lx) * (a > 0)),
    ]).astype(np.float32)
    tab["crnt"] = np.tile(np.tile(lz + 4.0, groups)[None], (8, 1)).astype(np.float32)
    tab["sx0"] = np.tile(sx[:, None], (1, height)).astype(np.float32)
    lane = np.zeros((8, height))
    lane[0], lane[1] = sy, sy * sgb
    lane[2], lane[3] = np.where(b > 0, sy, 1.0), sy * sgb
    tab["sy0"] = lane.astype(np.float32)
    return tab


def cosine_fwd(xs, scale):
    n = len(xs)
    if n == 1:
        return [xs[0] * (scale / np.sqrt(2.0))]
    half = n // 2
    even = cosine_fwd([xs[j] + xs[n - 1 - j] for j in range(half)], scale)
    diff = [xs[j] - xs[n - 1 - j] for j in range(half)]
    out = [None] * n
    for m in range(half):
        out[2 * m] = even[m]
        acc = None
        for j in range(half):
            term = diff[j] * float(scale * np.cos(np.pi * (2 * m + 1) * (2 * j + 1) / (2 * n)))
            acc = term if acc is None else acc + term
        out[2 * m + 1] = acc
    return out


def cosine_back(ys, scale):
    n = len(ys)
    if n == 1:
        return [ys[0] * (scale / np.sqrt(2.0))]
    half = n // 2
    even = cosine_back(ys[0::2], scale)
    out = [None] * n
    for j in range(half):
        acc = None
        for m in range(half):
            term = ys[2 * m + 1] * float(scale * np.cos(np.pi * (2 * m + 1) * (2 * j + 1) / (2 * n)))
            acc = term if acc is None else acc + term
        out[j] = even[j] + acc
        out[n - 1 - j] = even[j] - acc
    return out


def halves(x):
    hi = x.astype(BF16)
    return hi, (x - hi.astype(F32)).astype(BF16)


def times_sy(x, eyw):
    hi, lo = halves(x)
    n = x.shape[1]
    out = jnp.dot(jnp.concatenate([hi, lo], 1), eyw, preferred_element_type=F32)
    return out[:, :n] + out[:, n:]


def sx_times(exw, x):
    hi, lo = halves(x)
    return jnp.dot(exw, jnp.concatenate([hi, hi, lo], 0), preferred_element_type=F32)


def lane_id(shape):
    return lax.broadcasted_iota(jnp.int32, shape, 1)


def by_group(pieces, depth):
    group = lane_id(pieces[0].shape) // depth
    out = pieces[0]
    for h in range(1, len(pieces)):
        out = jnp.where(group == h, pieces[h], out)
    return out


def spread(x, depth):
    width = x.shape[1] // 2
    while width >= depth:
        x = x + pltpu.roll(x, width, 1)
        width //= 2
    return x


def pack(col, depth):
    groups = 128 // depth
    size = col.shape[0] // groups
    return by_group([col[h * size:(h + 1) * size] for h in range(groups)], depth)


def unpack(packed, depth):
    groups = 128 // depth
    group = lane_id(packed.shape) // depth
    return jnp.concatenate(
        [spread(jnp.where(group == h, packed, 0.0), depth) for h in range(groups)], 0
    )


def copies_t(kb):
    groups = 128 // kb.shape[0]
    return jnp.concatenate([kb] * groups, 0).T


def rows_from(kbt, depth):
    groups = 128 // depth
    size = kbt.shape[0] // groups
    return by_group([kbt[h * size:(h + 1) * size] for h in range(groups)], depth)


def rows_back(row, depth):
    groups = 128 // depth
    parts = [row] + [pltpu.roll(row, 128 - h * depth, 1) for h in range(1, groups)]
    return jnp.concatenate(parts, 0).T[:depth]


def total(x):
    return jnp.sum(x, 0, keepdims=True)


def sub_sums(ref):
    plus = minus = None
    for s in range(8):
        part = ref[:, s, :]
        if s % 2 == 1:
            plus = part if plus is None else plus + part
        else:
            minus = part if minus is None else minus + part
    return plus + minus, plus - minus


def with_tail(body, tails, size=8):
    width = body.shape[1]
    rows = list(tails) + [jnp.zeros((size - len(tails), width), F32)]
    return jnp.concatenate([body, jnp.concatenate(rows, 0)], 0)


def front_kernel(charge_h, surf_h, eyw_h, exw_h, inv_h, sx0_h, sy0_h, base, px, nx, py, ny,
                 charge, surf, eyw, exw, inv, sx0, sy0, work, part, first, sems):
    depth, width, height = charge.shape
    scale = np.sqrt(2.0 / depth)
    tiles = width // 8
    pairs = [(surf_h, surf)]
    pairs += [(charge_h.at[:, 8 * i:8 * i + 8, :], charge.at[:, 8 * i:8 * i + 8, :]) for i in range(tiles)]
    pairs += [(eyw_h, eyw), (exw_h, exw), (sx0_h, sx0), (sy0_h, sy0), (inv_h, inv)]
    copies = [pltpu.make_async_copy(src, dst, sems.at[i]) for i, (src, dst) in enumerate(pairs)]
    for copy in copies:
        copy.start()
    copies[0].wait()
    for i in range(tiles):
        copies[1 + i].wait()
        at = slice(8 * i, 8 * i + 8)
        xs = [charge[z, at, :] for z in range(depth)]
        xs[0] = xs[0] + surf[0, at, :]
        xs[-1] = xs[-1] + surf[1, at, :]
        for k, value in enumerate(cosine_fwd(xs, scale)):
            work[k, at, :] = value
    for copy in copies[1 + tiles:]:
        copy.wait()
    step = 4
    for c in range(0, depth, step):
        block = work[c:c + step].reshape(step * width, height)
        work[c:c + step] = times_sy(block, eyw[...]).reshape(step, width, height)
    lane = lane_id((width, 128))
    zero = jnp.zeros((width, 128), F32)
    near, far, own = zero, zero, zero
    for c in range(0, depth, 2):
        pair = sx_times(exw[...], jnp.concatenate([work[c], work[c + 1]], 1))
        for k in (c, c + 1):
            spec = pair[:, (k - c) * height:(k - c + 1) * height]
            inner = spec * inv[k]
            base[k] = inner
            first[k] = spec[0:8]
            part[k] = jnp.sum((inner * sx0[...]).reshape(width // 8, 8, height), 0)
            here = lane % depth == k
            near = jnp.where(here, jnp.sum(inner * sy0[0:1, :], 1, keepdims=True), near)
            far = jnp.where(here, jnp.sum(inner * sy0[1:2, :], 1, keepdims=True), far)
            own = jnp.where(here, spec[:, 0:1], own)
    row_near, row_far = sub_sums(part)
    own_t = copies_t(first[:, 0, :])
    corner = own_t[0:1]
    row = rows_from(own_t + copies_t(row_near), depth)
    at_zero = (lax.broadcasted_iota(jnp.int32, row.shape, 0) == 0) & (lane_id(row.shape) < depth)
    row = jnp.where(at_zero, 0.0, row)
    col = jnp.where(lax.broadcasted_iota(jnp.int32, own.shape, 0) == 0, 0.0, own + near)
    px[...] = with_tail(row, [corner])
    nx[...] = with_tail(rows_from(copies_t(row_far), depth), [])
    py[...] = with_tail(pack(col, depth), [corner])
    ny[...] = with_tail(pack(far, depth), [])


def assemble(depth, own, got):
    (px, nx, py, ny), (from_nx, from_px, from_ny, from_py) = own, got
    rows, cols = px.shape[0] - 8, py.shape[0] - 8
    row = px[:rows] + from_px[:rows]
    row_n = from_nx[:rows] + nx[:rows]
    col = unpack(py[:cols] + from_py[:cols], depth)
    col_n = unpack(from_ny[:cols] + ny[:cols], depth)
    c00 = px[rows:rows + 1] + from_px[rows:rows + 1] + from_py[cols:cols + 1]
    cx0 = from_nx[rows:rows + 1] + nx[rows:rows + 1] + from_py[cols + 1:cols + 2]
    c0y = from_ny[cols:cols + 1] + ny[cols:cols + 1] + from_px[rows + 1:rows + 2]
    return row, row_n, col, col_n, c00, cx0, c0y


def sizes(rows, cols):
    offs = np.cumsum([0, rows, rows, cols, cols])
    return [slice(int(offs[i]), int(offs[i + 1])) for i in range(4)] + [int(offs[4])]


def unpacked_state(state, rows, cols):
    s = sizes(rows, cols)
    at = s[4]
    return tuple(state[s[i], :] for i in range(4)) + tuple(state[at + i:at + i + 1, :] for i in range(3))


def schur_kernel(depth, want_moments, *refs):
    own, got = [r[...] for r in refs[0:4]], [r[...] for r in refs[4:8]]
    inv2, rowt, colt, crnt = refs[8:12]
    rest = list(refs[12:])
    before = rest.pop(0) if want_moments else None
    state, px, nx, py, ny = rest[:5]
    moments = rest[5] if want_moments else None
    part, odd_rows, even_rows = rest[-3:]
    row, row_n, col, col_n, c00, cx0, c0y = assemble(depth, own, got)
    rows, cols = row.shape[0], col.shape[0]
    s = sizes(rows, cols)
    for i, piece in enumerate((row, row_n, col, col_n)):
        state[s[i], :] = piece
    state[s[4]:s[4] + 8, :] = jnp.concatenate([c00, cx0, c0y, jnp.zeros((5, 128), F32)], 0)
    sy, sys, g_odd, g_even, d_row = (rowt[i] for i in range(5))
    sx, sxs, h_odd, h_even, d_col = (colt[i] for i in range(5))
    row_p, row_m, col_p, col_m = row + row_n, row - row_n, col + col_n, col - col_n
    odd_rows[...] = row_p * sy
    even_rows[...] = row_m * sy
    col_w = (col_m * sx, col_p * sx)
    odd = lax.broadcasted_iota(jnp.int32, (8, 128), 0) % 2 == 1
    acc = [None, None]
    for r in range(rows):
        table = inv2[r].reshape(cols // 8, 8, 128)
        part[r] = jnp.sum(table * col_w[r % 2].reshape(cols // 8, 8, 128), 0)
        pick = jnp.where(odd, odd_rows[r:r + 1, :], even_rows[r:r + 1, :])
        term = table * pick[None]
        acc[r % 2] = term if acc[r % 2] is None else acc[r % 2] + term
    row_s, row_d = sub_sums(part)
    acc_s = spread((acc[1] + acc[0]).reshape(cols, 128), depth)
    acc_d = spread((acc[1] - acc[0]).reshape(cols, 128), depth)
    diag_o, diag_e = g_odd * row_p, g_even * row_m
    x_near = sy * row_s + (diag_o + diag_e)
    x_far = sy * row_d + (diag_o - diag_e)
    diag_o, diag_e = h_odd * col_p, h_even * col_m
    y_near = sx * acc_s + (diag_o + diag_e)
    y_far = sx * acc_d + (diag_o - diag_e)
    row_img = d_row * row - sy * c00 - sys * c0y - x_near
    col_img = d_col * col - sx * c00 - sxs * cx0 - y_near
    row_end0 = spread(total(sy * row), depth)
    row_end1 = spread(total(sys * row), depth)
    row_end1n = spread(total(sys * row_n), depth)
    col_end0 = total(sx * col)
    col_end1 = total(sxs * col)
    col_end1n = total(sxs * col_n)
    q00 = crnt[0:1, :] * c00 - row_end0 - col_end0
    px[...] = with_tail(row_img, [q00])
    nx[...] = with_tail(-x_far, [-col_end1, -col_end1n])
    py[...] = with_tail(pack(col_img, depth), [q00])
    ny[...] = with_tail(pack(-y_far, depth), [-row_end1, -row_end1n])
    if want_moments:
        row0, _, col0, _, c000, _, _ = unpacked_state(before, rows, cols)
        share = depth / 128.0

        def dot(x, y):
            return total(x[0] * y[0]) + share * (total(x[1] * y[1]) + x[2] * y[2])

        v0, v1 = (row0, col0, c000), (row, col, c00)
        m3 = total(row * row_img - row_n * x_far) + share * (
            total(col * col_img - col_n * y_far) + c00 * q00 - c0y * row_end1 - cx0 * col_end1
        )
        moments[...] = jnp.concatenate([dot(v0, v0), dot(v0, v1), dot(v1, v1), m3, jnp.zeros((4, 128), F32)], 0)


def cells_from(out, work, spectrum, exw, eyw):
    depth, width, height = work.shape
    for c in range(0, depth, 2):
        pair = sx_times(exw, jnp.concatenate([spectrum(c), spectrum(c + 1)], 1))
        work[c] = pair[:, :height]
        work[c + 1] = pair[:, height:]
    step = 4
    for c in range(0, depth, step):
        block = work[c:c + step].reshape(step * width, height)
        work[c:c + step] = times_sy(block, eyw).reshape(step, width, height)
    scale = np.sqrt(2.0 / depth)
    for i in range(width // 8):
        at = slice(8 * i, 8 * i + 8)
        for z, value in enumerate(cosine_back([work[k, at, :] for k in range(depth)], scale)):
            out[z, at, :] = value


def base_kernel(base, eyw, exw, out, work):
    cells_from(out, work, lambda k: base[k], exw[...], eyw[...])


def extend_kernel(state, eyw, exw, inv, sx0, sy0, out, work):
    depth, width, height = work.shape
    rows = height * depth // 128
    row, row_n, col, col_n, c00 = unpacked_state(state, rows, width)[:5]
    at_zero = (lax.broadcasted_iota(jnp.int32, row.shape, 0) == 0) & (lane_id(row.shape) < depth)
    row_p = rows_back(row + row_n, depth)
    row_m = rows_back(row - row_n, depth)
    row_full = rows_back(jnp.where(at_zero, c00, row), depth)
    odd = lax.broadcasted_iota(jnp.int32, (8, height), 0) % 2 == 1
    top = lax.broadcasted_iota(jnp.int32, (width, height), 0) == 0
    lane0 = lane_id((width, height)) == 0

    def spectrum(k):
        pick = jnp.where(odd, row_p[k:k + 1], row_m[k:k + 1])
        pick = jnp.broadcast_to(pick[None], (width // 8, 8, height)).reshape(width, height)
        rim = sx0[...] * pick + col[:, k:k + 1] * sy0[2:3, :] + col_n[:, k:k + 1] * sy0[3:4, :]
        return jnp.where(top, row_full[k:k + 1], jnp.where(lane0, 1.0, inv[k]) * rim)

    cells_from(out, work, spectrum, exw[...], eyw[...])


def rims_kernel(depth, s0, s1, px, py, from_px, from_py, eyw, exw, cz, czt, out_rows, out_cols):
    packed = py.shape[0] - 8
    rows = px.shape[0] - 8
    width = packed * 128 // depth
    v0 = unpacked_state(s0, rows, width)
    v1 = unpacked_state(s1, rows, width)
    v2 = (
        px[:rows, :] + from_px[:rows, :], None,
        unpack(py[:packed, :] + from_py[:packed, :], depth), None,
        px[rows:rows + 1, :] + from_px[rows:rows + 1, :] + from_py[packed:packed + 1, :],
    )
    at_zero = (lax.broadcasted_iota(jnp.int32, (rows, 128), 0) == 0) & (lane_id((rows, 128)) < depth)
    lines = [rows_back(jnp.where(at_zero, v[4], v[0]), depth) for v in (v0, v1, v2)]
    high = lax.Precision.HIGHEST
    lines = times_sy(jnp.concatenate(lines, 0), eyw[...])
    lines = jnp.concatenate([lines[i * depth:(i + 1) * depth] for i in range(3)], 1)
    lines = jnp.dot(cz[...], lines, precision=high, preferred_element_type=F32)
    for i in range(3):
        out_rows[i] = lines[:, i * 128:(i + 1) * 128]
    sides = sx_times(exw[...], jnp.concatenate([v[2] for v in (v0, v1, v2)], 1))
    sides = jnp.concatenate([sides[:, i * 128:(i + 1) * 128] for i in range(3)], 0)
    sides = jnp.dot(sides, czt[...], precision=high, preferred_element_type=F32)
    for i in range(3):
        out_cols[i] = sides[i * width:(i + 1) * width]


def final_kernel(n_moments, *refs):
    cells_b, cells_0, cells_1, in_rows, in_cols = refs[:5]
    moms = refs[5:5 + n_moments]
    potential_h, residual_h, potential, residual, sems = refs[5 + n_moments:]
    depth, width, height = cells_b.shape
    m = moms[0][...]
    for other in moms[1:]:
        m = m + other[...]
    m = jnp.broadcast_to(jnp.sum(m, 1, keepdims=True), (8, 128))
    m0 = m[0:1]
    n1, n2, n3 = m[1:2] / m0, m[2:3] / m0, m[3:4] / m0
    det = n1 * n3 - n2 * n2
    fine = det > 1e-6 * (n1 * n3)
    safe = jnp.where(fine, det, 1.0)
    c0 = jnp.where(fine, (n3 - n1 * n2) / safe, 1.0 / n1)
    c1 = jnp.where(fine, (n1 * n1 - n2) / safe, 0.0)
    rim_row = in_rows[0] - c0 * in_rows[1] - c1 * in_rows[2]
    rim_col = in_cols[0] - c0 * in_cols[1] - c1 * in_cols[2]
    top = lax.broadcasted_iota(jnp.int32, (width, height), 0) == 0
    lane0 = lane_id((width, height)) == 0
    step = depth // 4
    copies = []
    for c in range(0, depth, step):
        for z in range(c, c + step):
            potential[z] = cells_b[z] + c0 * cells_0[z] + c1 * cells_1[z]
        copies.append((potential.at[c:c + step], potential_h.at[c:c + step]))
        copies[-1] = pltpu.make_async_copy(*copies[-1], sems.at[len(copies) - 1])
        copies[-1].start()
    for c in range(0, depth, step):
        for z in range(c, c + step):
            residual[z] = jnp.where(top, rim_row[z:z + 1], jnp.where(lane0, rim_col[:, z:z + 1], 0.0))
        copies.append((residual.at[c:c + step], residual_h.at[c:c + step]))
        copies[-1] = pltpu.make_async_copy(*copies[-1], sems.at[len(copies) - 1])
        copies[-1].start()
    for copy in copies:
        copy.wait()


def shifted(value, axis, by):
    n = lax.axis_size(axis)
    return lax.ppermute(value, axis, [(i, (i + by) % n) for i in range(n)])


def exchange(px, nx, py, ny):
    from_py = shifted(ny, "gy", 1)
    from_ny = shifted(py, "gy", -1)
    from_px = shifted(nx, "gx", 1)
    from_nx = shifted(px, "gx", -1)
    return from_nx, from_px, from_ny, from_py


def pieces_over(value, axis):
    n, stride = lax.axis_size(axis), 1
    while True:
        radix = 4 if n % 4 == 0 else 2 if n % 2 == 0 else n
        parts = [value] + [shifted(value, axis, stride * j) for j in range(1, radix)]
        n, stride = n // radix, stride * radix
        if n == 1:
            return parts
        value = sum(parts[1:], parts[0])


def call(kernel, outs, scratch, in_specs=None, out_specs=None):
    specs = {}
    if in_specs is not None:
        specs["in_specs"] = in_specs
    if out_specs is not None:
        specs["out_specs"] = out_specs
    return pl.pallas_call(
        kernel,
        out_shape=[jax.ShapeDtypeStruct(shape, F32) for shape in outs],
        scratch_shapes=[pltpu.VMEM(s, F32) if isinstance(s, tuple) else s for s in scratch],
        compiler_params=pltpu.CompilerParams(vmem_limit_bytes=48 * 1024 * 1024),
        **specs,
    )


def on_device(charge, surface_charge):
    depth, width, height = charge.shape
    tab = {name: jnp.asarray(value) for name, value in make_tables(depth, width, height).items()}
    rows, packed = height * depth // 128, width * depth // 128
    msgs = [(rows + 8, 128)] * 2 + [(packed + 8, 128)] * 2
    state = (2 * rows + 2 * width + 8, 128)
    block = (depth, width, height)
    anywhere = pl.BlockSpec(memory_space=pltpu.HBM)
    whole = pl.BlockSpec(memory_space=pltpu.VMEM)
    fronts = (charge, surface_charge) + tuple(tab[n] for n in ("eyw", "exw", "inv", "sx0", "sy0"))
    landing = [pltpu.VMEM(x.shape, x.dtype) for x in fronts]
    fronts = [pltpu.with_memory_space_constraint(x, pltpu.HBM) for x in fronts]
    base, *own = call(
        front_kernel, [block] + msgs,
        landing + [block, (depth, 8, height), (depth, 8, height), pltpu.SemaphoreType.DMA((6 + width // 8,))],
        in_specs=[anywhere] * 7,
    )(*fronts)
    got = exchange(*own)
    cells_b = call(base_kernel, [block], [block])(base, tab["eyw"], tab["exw"])[0]
    *got, cells_b = lax.optimization_barrier((*got, cells_b))
    tables = (tab["inv2"], tab["rowt"], tab["colt"], tab["crnt"])
    scratch = [(rows, 8, 128), (rows, 128), (rows, 128)]
    s0, *own = call(lambda *r: schur_kernel(depth, False, *r), [state] + msgs, scratch)(*own, *got, *tables)
    got = exchange(*own)
    extend = call(extend_kernel, [block], [block])
    backs = tuple(tab[n] for n in ("eyw", "exw", "inv", "sx0", "sy0"))
    cells_0 = extend(s0, *backs)[0]
    *got, cells_0 = lax.optimization_barrier((*got, cells_0))
    s1, px, nx, py, ny, moments = call(
        lambda *r: schur_kernel(depth, True, *r), [state] + msgs + [(8, 128)], scratch
    )(*own, *got, *tables, s0)
    parts = pieces_over(moments, "gx")
    from_py, from_px = shifted(ny, "gy", 1), shifted(nx, "gx", 1)
    cells_1 = extend(s1, *backs)[0]
    *parts, cells_1 = lax.optimization_barrier((*parts, cells_1))
    parts = pieces_over(sum(parts[1:], parts[0]), "gy")
    rim = call(lambda *r: rims_kernel(depth, *r), [(3, depth, height), (3, width, 128)], [])(
        s0, s1, px, py, from_px, from_py, tab["eyw"], tab["exw"], tab["cz"], tab["czt"]
    )
    return call(
        lambda *r: final_kernel(len(parts), *r), [block, block], [block, block, pltpu.SemaphoreType.DMA((8,))],
        in_specs=[whole] * (5 + len(parts)), out_specs=[anywhere, anywhere],
    )(cells_b, cells_0, cells_1, *rim, *parts)


def solution(mesh):
    spec = P(None, ("slab", "gx"), "gy")
    return jax.shard_map(
        on_device, mesh=mesh, in_specs=(spec, spec), out_specs=(spec, spec), check_vma=False
    )
```

```python
import numpy as np
import jax
import jax.numpy as jnp
from jax import lax
from jax.experimental import pallas as pl
from jax.experimental.pallas import tpu as pltpu
from jax.sharding import PartitionSpec as P
import ml_dtypes

SCREEN = 0.02
BF16 = jnp.bfloat16
F32 = jnp.float32


def sine_ext(n):
    i = np.arange(n)
    table = np.sqrt(2.0 / n) * np.sin(np.pi * np.outer(i, i) / n)
    table[0, 0] = 1.0
    return table


def split_bf16(table):
    hi = table.astype(np.float32).astype(ml_dtypes.bfloat16)
    lo = (table - hi.astype(np.float64)).astype(np.float32).astype(ml_dtypes.bfloat16)
    return hi, lo


def make_tables(depth, width, height):
    lanes = 128
    groups = lanes // depth
    rows = height // groups
    tab = {}
    hi, lo = split_bf16(sine_ext(height))
    tab["eyw"] = np.block([[hi, lo], [hi, np.zeros_like(lo)]])
    hi, lo = split_bf16(sine_ext(width))
    tab["exw"] = np.concatenate([hi, lo, hi], 1)
    tab["ey"], tab["ex"] = sine_ext(height).astype(np.float32), sine_ext(width).astype(np.float32)
    z = np.arange(depth)
    cos = np.cos(np.pi * np.outer(z + 0.5, z) / depth) * np.sqrt(2.0 / depth)
    cos[:, 0] = np.sqrt(1.0 / depth)
    tab["cz"] = cos.astype(np.float32)
    czt = np.zeros((lanes, lanes))
    czt[:depth, :depth] = cos.T
    tab["czt"] = czt.astype(np.float32)
    lz = SCREEN + 2.0 - 2.0 * np.cos(np.pi * z / depth)
    a = np.arange(width)
    b = np.arange(height)
    lx = 2.0 - 2.0 * np.cos(np.pi * a / width)
    ly = 2.0 - 2.0 * np.cos(np.pi * b / height)
    sx = np.sqrt(2.0 / width) * np.sin(np.pi * a / width)
    sy = np.sqrt(2.0 / height) * np.sin(np.pi * b / height)
    sga = np.where(a % 2 == 1, 1.0, -1.0)
    sgb = np.where(b % 2 == 1, 1.0, -1.0)
    inside = (a[:, None] > 0) & (b[None, :] > 0)
    inv = np.where(inside[None], 1.0 / (lz[:, None, None] + lx[None, :, None] + ly[None, None, :]), 0.0)
    tab["inv"] = inv.astype(np.float32)

    def to_rows(kb):
        return kb.T.reshape(groups, rows, depth).transpose(1, 0, 2).reshape(rows, lanes)

    def to_cols(ka):
        return np.tile(ka.T, (1, groups))

    inv2 = inv.transpose(2, 1, 0).reshape(groups, rows, width, depth)
    tab["inv2"] = inv2.transpose(1, 2, 0, 3).reshape(rows, width, lanes).astype(np.float32)
    ones = np.ones((depth, 1))
    odd_a, odd_b = sga > 0, sgb > 0
    sx2, sy2 = (sx**2)[None, :, None] * inv, (sy**2)[None, None, :] * inv
    tab["rowt"] = np.stack([
        to_rows(ones * sy),
        to_rows(ones * (sy * sgb)),
        to_rows(sx2[:, odd_a].sum(1)),
        to_rows(sx2[:, ~odd_a].sum(1)),
        to_rows((lz[:, None] + 2.0 + ly) * (b > 0)),
    ]).astype(np.float32)
    tab["colt"] = np.stack([
        to_cols(ones * sx),
        to_cols(ones * (sx * sga)),
        to_cols(sy2[:, :, odd_b].sum(2)),
        to_cols(sy2[:, :, ~odd_b].sum(2)),
        to_cols((lz[:, None] + 2.0 + lx) * (a > 0)),
    ]).astype(np.float32)
    tab["crnt"] = np.tile(np.tile(lz + 4.0, groups)[None], (8, 1)).astype(np.float32)
    tab["sx0"] = np.tile(sx[:, None], (1, height)).astype(np.float32)
    lane = np.zeros((8, height))
    lane[0], lane[1] = sy, sy * sgb
    lane[2], lane[3] = np.where(b > 0, sy, 1.0), sy * sgb
    tab["sy0"] = lane.astype(np.float32)
    return tab


def cosine_fwd(xs, scale):
    n = len(xs)
    if n == 1:
        return [xs[0] * (scale / np.sqrt(2.0))]
    half = n // 2
    even = cosine_fwd([xs[j] + xs[n - 1 - j] for j in range(half)], scale)
    diff = [xs[j] - xs[n - 1 - j] for j in range(half)]
    out = [None] * n
    for m in range(half):
        out[2 * m] = even[m]
        acc = None
        for j in range(half):
            term = diff[j] * float(scale * np.cos(np.pi * (2 * m + 1) * (2 * j + 1) / (2 * n)))
            acc = term if acc is None else acc + term
        out[2 * m + 1] = acc
    return out


def cosine_back(ys, scale):
    n = len(ys)
    if n == 1:
        return [ys[0] * (scale / np.sqrt(2.0))]
    half = n // 2
    even = cosine_back(ys[0::2], scale)
    out = [None] * n
    for j in range(half):
        acc = None
        for m in range(half):
            term = ys[2 * m + 1] * float(scale * np.cos(np.pi * (2 * m + 1) * (2 * j + 1) / (2 * n)))
            acc = term if acc is None else acc + term
        out[j] = even[j] + acc
        out[n - 1 - j] = even[j] - acc
    return out


def halves(x):
    hi = x.astype(BF16)
    return hi, (x - hi.astype(F32)).astype(BF16)


def times_sy(x, eyw):
    hi, lo = halves(x)
    n = x.shape[1]
    out = jnp.dot(jnp.concatenate([hi, lo], 1), eyw, preferred_element_type=F32)
    return out[:, :n] + out[:, n:]


def sx_times(exw, x):
    hi, lo = halves(x)
    return jnp.dot(exw, jnp.concatenate([hi, hi, lo], 0), preferred_element_type=F32)


def lane_id(shape):
    return lax.broadcasted_iota(jnp.int32, shape, 1)


def by_group(pieces, depth):
    group = lane_id(pieces[0].shape) // depth
    out = pieces[0]
    for h in range(1, len(pieces)):
        out = jnp.where(group == h, pieces[h], out)
    return out


def spread(x, depth):
    width = x.shape[1] // 2
    while width >= depth:
        x = x + pltpu.roll(x, width, 1)
        width //= 2
    return x


def pack(col, depth):
    groups = 128 // depth
    size = col.shape[0] // groups
    return by_group([col[h * size:(h + 1) * size] for h in range(groups)], depth)


def unpack(packed, depth):
    groups = 128 // depth
    group = lane_id(packed.shape) // depth
    return jnp.concatenate(
        [spread(jnp.where(group == h, packed, 0.0), depth) for h in range(groups)], 0
    )


def copies_t(kb):
    groups = 128 // kb.shape[0]
    return jnp.concatenate([kb] * groups, 0).T


def rows_from(kbt, depth):
    groups = 128 // depth
    size = kbt.shape[0] // groups
    return by_group([kbt[h * size:(h + 1) * size] for h in range(groups)], depth)


def rows_back(row, depth):
    groups = 128 // depth
    parts = [row] + [pltpu.roll(row, 128 - h * depth, 1) for h in range(1, groups)]
    return jnp.concatenate(parts, 0).T[:depth]


def total(x):
    return jnp.sum(x, 0, keepdims=True)


def sub_sums(ref):
    plus = minus = None
    for s in range(8):
        part = ref[:, s, :]
        if s % 2 == 1:
            plus = part if plus is None else plus + part
        else:
            minus = part if minus is None else minus + part
    return plus + minus, plus - minus


def with_tail(body, tails, size=8):
    width = body.shape[1]
    rows = list(tails)
    if len(rows) < size:
        rows.append(jnp.zeros((size - len(rows), width), F32))
    return jnp.concatenate([body, jnp.concatenate(rows, 0)], 0)


def front_kernel(charge_h, surf_h, eyw_h, exw_h, inv_h, sx0_h, sy0_h, base, *rest):
    msgs = rest[:4]
    charge, surf, eyw, exw, inv, sx0, sy0, work, part, first, sems = rest[4:]
    depth, width, height = charge.shape
    scale = np.sqrt(2.0 / depth)
    tiles = width // 8
    pairs = [(surf_h, surf)]
    pairs += [(charge_h.at[:, 8 * i:8 * i + 8, :], charge.at[:, 8 * i:8 * i + 8, :]) for i in range(tiles)]
    pairs += [(eyw_h, eyw), (exw_h, exw), (sx0_h, sx0), (sy0_h, sy0), (inv_h, inv)]
    copies = [pltpu.make_async_copy(src, dst, sems.at[i]) for i, (src, dst) in enumerate(pairs)]
    for copy in copies:
        copy.start()
    copies[0].wait()
    for i in range(tiles):
        copies[1 + i].wait()
        at = slice(8 * i, 8 * i + 8)
        xs = [charge[z, at, :] for z in range(depth)]
        xs[0] = xs[0] + surf[0, at, :]
        xs[-1] = xs[-1] + surf[1, at, :]
        for k, value in enumerate(cosine_fwd(xs, scale)):
            work[k, at, :] = value
    for copy in copies[1 + tiles:]:
        copy.wait()
    step = 4
    for c in range(0, depth, step):
        block = work[c:c + step].reshape(step * width, height)
        work[c:c + step] = times_sy(block, eyw[...]).reshape(step, width, height)
    lane = lane_id((width, 128))
    zero = jnp.zeros((width, 128), F32)
    near, far, own = zero, zero, zero
    for c in range(0, depth, 2):
        pair = sx_times(exw[...], jnp.concatenate([work[c], work[c + 1]], 1))
        for k in (c, c + 1):
            spec = pair[:, (k - c) * height:(k - c + 1) * height]
            inner = spec * inv[k]
            base[k] = inner
            first[k] = spec[0:8]
            part[k] = jnp.sum((inner * sx0[...]).reshape(width // 8, 8, height), 0)
            here = lane % depth == k
            near = jnp.where(here, jnp.sum(inner * sy0[0:1, :], 1, keepdims=True), near)
            far = jnp.where(here, jnp.sum(inner * sy0[1:2, :], 1, keepdims=True), far)
            own = jnp.where(here, spec[:, 0:1], own)
    row_near, row_far = sub_sums(part)
    own_t = copies_t(first[:, 0, :])
    corner = own_t[0:1]
    row = rows_from(own_t + copies_t(row_near), depth)
    at_zero = (lax.broadcasted_iota(jnp.int32, row.shape, 0) == 0) & (lane_id(row.shape) < depth)
    row = jnp.where(at_zero, 0.0, row)
    col = jnp.where(lax.broadcasted_iota(jnp.int32, own.shape, 0) == 0, 0.0, own + near)
    px = with_tail(row, [corner])
    nx = with_tail(rows_from(copies_t(row_far), depth), [])
    py = with_tail(pack(col, depth), [corner])
    ny = with_tail(pack(far, depth), [])
    for ref, value in zip(msgs, swapped("gx", nx, px) + swapped("gy", ny, py)):
        ref[...] = value


def swapped(axis, after, before):
    even = lax.axis_index(axis) % 2 == 0
    return jnp.where(even, before, after), jnp.where(even, after, before)


def assemble(depth, own, got):
    (nx, px), (ny, py) = swapped("gx", *own[:2]), swapped("gy", *own[2:])
    (from_nx, from_px), (from_ny, from_py) = swapped("gx", *got[:2]), swapped("gy", *got[2:])
    rows, cols = px.shape[0] - 8, py.shape[0] - 8
    row = px[:rows] + from_px[:rows]
    row_n = from_nx[:rows] + nx[:rows]
    col = unpack(py[:cols] + from_py[:cols], depth)
    col_n = unpack(from_ny[:cols] + ny[:cols], depth)
    c00 = px[rows:rows + 1] + from_px[rows:rows + 1] + from_py[cols:cols + 1]
    cx0 = from_nx[rows:rows + 1] + nx[rows:rows + 1] + from_py[cols + 1:cols + 2]
    c0y = from_ny[cols:cols + 1] + ny[cols:cols + 1] + from_px[rows + 1:rows + 2]
    return row, row_n, col, col_n, c00, cx0, c0y


def sizes(rows, cols):
    offs = np.cumsum([0, rows, rows, cols, cols])
    return [slice(int(offs[i]), int(offs[i + 1])) for i in range(4)] + [int(offs[4])]


def unpacked_state(state, rows, cols):
    s = sizes(rows, cols)
    at = s[4]
    return tuple(state[s[i], :] for i in range(4)) + tuple(state[at + i:at + i + 1, :] for i in range(3))


def schur_kernel(depth, want_moments, *refs):
    own, got = [r[...] for r in refs[0:4]], [r[...] for r in refs[4:8]]
    inv2, rowt, colt, crnt = refs[8:12]
    rest = list(refs[12:])
    before = rest.pop(0) if want_moments else None
    state, *outs = rest[:5]
    moments = rest[5] if want_moments else None
    part, odd_rows, even_rows = rest[-3:]
    row, row_n, col, col_n, c00, cx0, c0y = assemble(depth, own, got)
    rows, cols = row.shape[0], col.shape[0]
    s = sizes(rows, cols)
    for i, piece in enumerate((row, row_n, col, col_n)):
        state[s[i], :] = piece
    state[s[4]:s[4] + 8, :] = jnp.concatenate([c00, cx0, c0y, jnp.zeros((5, 128), F32)], 0)
    sy, sys, g_odd, g_even, d_row = (rowt[i] for i in range(5))
    sx, sxs, h_odd, h_even, d_col = (colt[i] for i in range(5))
    row_p, row_m, col_p, col_m = row + row_n, row - row_n, col + col_n, col - col_n
    odd_rows[...] = row_p * sy
    even_rows[...] = row_m * sy
    col_w = (col_m * sx, col_p * sx)
    odd = lax.broadcasted_iota(jnp.int32, (8, 128), 0) % 2 == 1
    acc = [None, None]
    for r in range(rows):
        table = inv2[r].reshape(cols // 8, 8, 128)
        part[r] = jnp.sum(table * col_w[r % 2].reshape(cols // 8, 8, 128), 0)
        pick = jnp.where(odd, odd_rows[r:r + 1, :], even_rows[r:r + 1, :])
        term = table * pick[None]
        acc[r % 2] = term if acc[r % 2] is None else acc[r % 2] + term
    row_s, row_d = sub_sums(part)
    acc_s = spread((acc[1] + acc[0]).reshape(cols, 128), depth)
    acc_d = spread((acc[1] - acc[0]).reshape(cols, 128), depth)
    diag_o, diag_e = g_odd * row_p, g_even * row_m
    x_near = sy * row_s + (diag_o + diag_e)
    x_far = sy * row_d + (diag_o - diag_e)
    diag_o, diag_e = h_odd * col_p, h_even * col_m
    y_near = sx * acc_s + (diag_o + diag_e)
    y_far = sx * acc_d + (diag_o - diag_e)
    row_img = d_row * row - sy * c00 - sys * c0y - x_near
    col_img = d_col * col - sx * c00 - sxs * cx0 - y_near
    row_end0 = spread(total(sy * row), depth)
    row_end1 = spread(total(sys * row), depth)
    row_end1n = spread(total(sys * row_n), depth)
    col_end0 = total(sx * col)
    col_end1 = total(sxs * col)
    col_end1n = total(sxs * col_n)
    q00 = crnt[0:1, :] * c00 - row_end0 - col_end0
    px = with_tail(row_img, [q00])
    nx = with_tail(-x_far, [-col_end1, -col_end1n])
    py = with_tail(pack(col_img, depth), [q00])
    ny = with_tail(pack(-y_far, depth), [-row_end1, -row_end1n])
    if not want_moments:
        for ref, value in zip(outs, swapped("gx", nx, px) + swapped("gy", ny, py)):
            ref[...] = value
        return
    row0, _, col0, _, c000, _, _ = unpacked_state(before, rows, cols)
    share = depth / 128.0

    def dot(x, y):
        return total(x[0] * y[0]) + share * (total(x[1] * y[1]) + x[2] * y[2])

    v0, v1 = (row0, col0, c000), (row, col, c00)
    m3 = total(row * row_img - row_n * x_far) + share * (
        total(col * col_img - col_n * y_far) + c00 * q00 - c0y * row_end1 - cx0 * col_end1
    )
    tail = [-col_end1, -col_end1n, c00, c00, dot(v0, v0), dot(v0, v1), dot(v1, v1), m3]
    nx = with_tail(-x_far, tail)
    moments[...] = nx[rows:]
    for ref, value in zip(outs, (px, nx, py, ny)):
        ref[...] = value


def cells_from(out, work, spectrum, exw, eyw):
    depth, width, height = work.shape
    for c in range(0, depth, 2):
        pair = sx_times(exw, jnp.concatenate([spectrum(c), spectrum(c + 1)], 1))
        work[c] = pair[:, :height]
        work[c + 1] = pair[:, height:]
    step = 4
    for c in range(0, depth, step):
        block = work[c:c + step].reshape(step * width, height)
        work[c:c + step] = times_sy(block, eyw).reshape(step, width, height)
    scale = np.sqrt(2.0 / depth)
    for i in range(width // 8):
        at = slice(8 * i, 8 * i + 8)
        for z, value in enumerate(cosine_back([work[k, at, :] for k in range(depth)], scale)):
            out[z, at, :] = value


def base_kernel(base, eyw, exw, out, work):
    cells_from(out, work, lambda k: base[k], exw[...], eyw[...])


def extend_kernel(state, eyw, exw, inv, sx0, sy0, out, work):
    depth, width, height = work.shape
    rows = height * depth // 128
    row, row_n, col, col_n, c00 = unpacked_state(state, rows, width)[:5]
    at_zero = (lax.broadcasted_iota(jnp.int32, row.shape, 0) == 0) & (lane_id(row.shape) < depth)
    row_p = rows_back(row + row_n, depth)
    row_m = rows_back(row - row_n, depth)
    row_full = rows_back(jnp.where(at_zero, c00, row), depth)
    odd = lax.broadcasted_iota(jnp.int32, (8, height), 0) % 2 == 1
    top = lax.broadcasted_iota(jnp.int32, (width, height), 0) == 0
    lane0 = lane_id((width, height)) == 0

    def spectrum(k):
        pick = jnp.where(odd, row_p[k:k + 1], row_m[k:k + 1])
        pick = jnp.broadcast_to(pick[None], (width // 8, 8, height)).reshape(width, height)
        rim = sx0[...] * pick + col[:, k:k + 1] * sy0[2:3, :] + col_n[:, k:k + 1] * sy0[3:4, :]
        return jnp.where(top, row_full[k:k + 1], jnp.where(lane0, 1.0, inv[k]) * rim)

    cells_from(out, work, spectrum, exw[...], eyw[...])


def rims_kernel(depth, s0, s1, px, py, from_px, from_py, ey, ex, cz, czt, out_rows, out_cols):
    packed = py.shape[0] - 8
    rows = px.shape[0] - 8
    width = packed * 128 // depth
    v0 = unpacked_state(s0, rows, width)
    v1 = unpacked_state(s1, rows, width)
    v2 = (
        px[:rows, :] + from_px[:rows, :], None,
        unpack(py[:packed, :] + from_py[:packed, :], depth), None,
        px[rows:rows + 1, :] + from_px[rows:rows + 1, :] + from_py[packed:packed + 1, :],
    )
    at_zero = (lax.broadcasted_iota(jnp.int32, (rows, 128), 0) == 0) & (lane_id((rows, 128)) < depth)
    lines = [rows_back(jnp.where(at_zero, v[4], v[0]), depth) for v in (v0, v1, v2)]
    high = lax.Precision.HIGHEST
    lines = jnp.dot(jnp.concatenate(lines, 0), ey[...], precision=high, preferred_element_type=F32)
    lines = jnp.concatenate([lines[i * depth:(i + 1) * depth] for i in range(3)], 1)
    lines = jnp.dot(cz[...], lines, precision=high, preferred_element_type=F32)
    for i in range(3):
        out_rows[i] = lines[:, i * 128:(i + 1) * 128]
    sides = jnp.concatenate([v[2] for v in (v0, v1, v2)], 1)
    sides = jnp.dot(ex[...], sides, precision=high, preferred_element_type=F32)
    sides = jnp.concatenate([sides[:, i * 128:(i + 1) * 128] for i in range(3)], 0)
    sides = jnp.dot(sides, czt[...], precision=high, preferred_element_type=F32)
    for i in range(3):
        out_cols[i] = sides[i * width:(i + 1) * width]


def final_kernel(n_moments, *refs):
    cells_b, cells_0, cells_1, in_rows, in_cols = refs[:5]
    moms = refs[5:5 + n_moments]
    potential_h, residual_h, potential, residual, sems = refs[5 + n_moments:]
    depth, width, height = cells_b.shape
    m = moms[0][...]
    for other in moms[1:]:
        m = m + other[...]
    m = jnp.broadcast_to(jnp.sum(m, 1, keepdims=True), (8, 128))
    m0 = m[4:5]
    n1, n2, n3 = m[5:6] / m0, m[6:7] / m0, m[7:8] / m0
    det = n1 * n3 - n2 * n2
    fine = det > 1e-6 * (n1 * n3)
    safe = jnp.where(fine, det, 1.0)
    c0 = jnp.where(fine, (n3 - n1 * n2) / safe, 1.0 / n1)
    c1 = jnp.where(fine, (n1 * n1 - n2) / safe, 0.0)
    rim_row = in_rows[0] - c0 * in_rows[1] - c1 * in_rows[2]
    rim_col = in_cols[0] - c0 * in_cols[1] - c1 * in_cols[2]
    top = lax.broadcasted_iota(jnp.int32, (width, height), 0) == 0
    lane0 = lane_id((width, height)) == 0
    step = depth // 4
    copies = []
    for c in range(0, depth, step):
        for z in range(c, c + step):
            potential[z] = cells_b[z] + c0 * cells_0[z] + c1 * cells_1[z]
        copies.append((potential.at[c:c + step], potential_h.at[c:c + step]))
        copies[-1] = pltpu.make_async_copy(*copies[-1], sems.at[len(copies) - 1])
        copies[-1].start()
    for c in range(0, depth, step):
        for z in range(c, c + step):
            residual[z] = jnp.where(top, rim_row[z:z + 1], jnp.where(lane0, rim_col[:, z:z + 1], 0.0))
        copies.append((residual.at[c:c + step], residual_h.at[c:c + step]))
        copies[-1] = pltpu.make_async_copy(*copies[-1], sems.at[len(copies) - 1])
        copies[-1].start()
    for copy in copies:
        copy.wait()


def shifted(value, axis, by):
    n = lax.axis_size(axis)
    return lax.ppermute(value, axis, [(i, (i + by) % n) for i in range(n)])


def swap(value, axis, odd):
    n = lax.axis_size(axis)
    pairs = [(i, (i + 1) % n) for i in range(odd, n, 2)]
    return lax.ppermute(value, axis, pairs + [(j, i) for i, j in pairs])


def exchange(bx, ax, by, ay):
    return swap(bx, "gx", 1), swap(ax, "gx", 0), swap(by, "gy", 1), swap(ay, "gy", 0)


def pieces_over(value, axis, first=None):
    n, stride, kept = lax.axis_size(axis), 1, None
    while True:
        radix = 4 if n % 4 == 0 else 2 if n % 2 == 0 else n
        parts = [value]
        for j in range(1, radix):
            if first is not None and stride * j == 1:
                kept = shifted(first, axis, 1)
                parts.append(kept[-value.shape[0]:])
            else:
                parts.append(shifted(value, axis, stride * j))
        n, stride = n // radix, stride * radix
        if n == 1:
            return parts, kept
        value = sum(parts[1:], parts[0])


def call(kernel, outs, scratch, in_specs=None, out_specs=None):
    specs = {}
    if in_specs is not None:
        specs["in_specs"] = in_specs
    if out_specs is not None:
        specs["out_specs"] = out_specs
    return pl.pallas_call(
        kernel,
        out_shape=[jax.ShapeDtypeStruct(shape, F32) for shape in outs],
        scratch_shapes=[pltpu.VMEM(s, F32) if isinstance(s, tuple) else s for s in scratch],
        compiler_params=pltpu.CompilerParams(vmem_limit_bytes=48 * 1024 * 1024),
        **specs,
    )


def on_device(charge, surface_charge):
    depth, width, height = charge.shape
    tab = {name: jnp.asarray(value) for name, value in make_tables(depth, width, height).items()}
    rows, packed = height * depth // 128, width * depth // 128
    msgs = [(rows + 8, 128)] * 2 + [(packed + 8, 128)] * 2
    state = (2 * rows + 2 * width + 8, 128)
    block = (depth, width, height)
    anywhere = pl.BlockSpec(memory_space=pltpu.HBM)
    whole = pl.BlockSpec(memory_space=pltpu.VMEM)
    fronts = (charge, surface_charge) + tuple(tab[n] for n in ("eyw", "exw", "inv", "sx0", "sy0"))
    landing = [pltpu.VMEM(x.shape, x.dtype) for x in fronts]
    fronts = [pltpu.with_memory_space_constraint(x, pltpu.HBM) for x in fronts]
    base, *own = call(
        front_kernel, [block] + msgs,
        landing + [block, (depth, 8, height), (depth, 8, height), pltpu.SemaphoreType.DMA((6 + width // 8,))],
        in_specs=[anywhere] * 7,
    )(*fronts)
    got = exchange(*own)
    cells_b = call(base_kernel, [block], [block])(base, tab["eyw"], tab["exw"])[0]
    *got, cells_b = lax.optimization_barrier((*got, cells_b))
    tables = (tab["inv2"], tab["rowt"], tab["colt"], tab["crnt"])
    scratch = [(rows, 8, 128), (rows, 128), (rows, 128)]
    s0, *own = call(lambda *r: schur_kernel(depth, False, *r), [state] + msgs, scratch)(*own, *got, *tables)
    got = exchange(*own)
    extend = call(extend_kernel, [block], [block])
    backs = tuple(tab[n] for n in ("eyw", "exw", "inv", "sx0", "sy0"))
    cells_0 = extend(s0, *backs)[0]
    *got, cells_0 = lax.optimization_barrier((*got, cells_0))
    s1, px, nx, py, ny, moments = call(
        lambda *r: schur_kernel(depth, True, *r), [state] + msgs + [(8, 128)], scratch
    )(*own, *got, *tables, s0)
    parts, from_px = pieces_over(moments, "gx", nx)
    from_py = shifted(ny, "gy", 1)
    cells_1 = extend(s1, *backs)[0]
    *parts, cells_1 = lax.optimization_barrier((*parts, cells_1))
    parts, _ = pieces_over(sum(parts[1:], parts[0]), "gy")
    rim = call(lambda *r: rims_kernel(depth, *r), [(3, depth, height), (3, width, 128)], [])(
        s0, s1, px, py, from_px, from_py, tab["ey"], tab["ex"], tab["cz"], tab["czt"]
    )
    return call(
        lambda *r: final_kernel(len(parts), *r), [block, block], [block, block, pltpu.SemaphoreType.DMA((8,))],
        in_specs=[whole] * (5 + len(parts)), out_specs=[anywhere, anywhere],
    )(cells_b, cells_0, cells_1, *rim, *parts)


def solution(mesh):
    spec = P(None, ("slab", "gx"), "gy")
    return jax.shard_map(
        on_device, mesh=mesh, in_specs=(spec, spec), out_specs=(spec, spec), check_vma=False
    )
```

```python
import numpy as np
import jax
import jax.numpy as jnp
from jax import lax
from jax.experimental import pallas as pl
from jax.experimental.pallas import tpu as pltpu
from jax.sharding import PartitionSpec as P
import ml_dtypes

SCREEN = 0.02
BF16 = jnp.bfloat16
F32 = jnp.float32


def sine_ext(n):
    i = np.arange(n)
    table = np.sqrt(2.0 / n) * np.sin(np.pi * np.outer(i, i) / n)
    table[0, 0] = 1.0
    return table


def split_bf16(table):
    hi = table.astype(np.float32).astype(ml_dtypes.bfloat16)
    lo = (table - hi.astype(np.float64)).astype(np.float32).astype(ml_dtypes.bfloat16)
    return hi, lo


def make_tables(depth, width, height):
    lanes = 128
    groups = lanes // depth
    rows = height // groups
    tab = {}
    hi, lo = split_bf16(sine_ext(height))
    tab["eyw"] = np.block([[hi, lo], [hi, np.zeros_like(lo)]])
    hi, lo = split_bf16(sine_ext(width))
    tab["exw"] = np.concatenate([hi, lo, hi], 1)
    tab["ey"], tab["ex"] = sine_ext(height).astype(np.float32), sine_ext(width).astype(np.float32)
    z = np.arange(depth)
    cos = np.cos(np.pi * np.outer(z + 0.5, z) / depth) * np.sqrt(2.0 / depth)
    cos[:, 0] = np.sqrt(1.0 / depth)
    tab["cz"] = cos.astype(np.float32)
    czt = np.zeros((lanes, lanes))
    czt[:depth, :depth] = cos.T
    tab["czt"] = czt.astype(np.float32)
    lz = SCREEN + 2.0 - 2.0 * np.cos(np.pi * z / depth)
    a = np.arange(width)
    b = np.arange(height)
    lx = 2.0 - 2.0 * np.cos(np.pi * a / width)
    ly = 2.0 - 2.0 * np.cos(np.pi * b / height)
    sx = np.sqrt(2.0 / width) * np.sin(np.pi * a / width)
    sy = np.sqrt(2.0 / height) * np.sin(np.pi * b / height)
    sga = np.where(a % 2 == 1, 1.0, -1.0)
    sgb = np.where(b % 2 == 1, 1.0, -1.0)
    inside = (a[:, None] > 0) & (b[None, :] > 0)
    inv = np.where(inside[None], 1.0 / (lz[:, None, None] + lx[None, :, None] + ly[None, None, :]), 0.0)
    tab["inv"] = inv.astype(np.float32)

    def to_rows(kb):
        return kb.T.reshape(groups, rows, depth).transpose(1, 0, 2).reshape(rows, lanes)

    def to_cols(ka):
        return np.tile(ka.T, (1, groups))

    inv2 = inv.transpose(2, 1, 0).reshape(groups, rows, width, depth)
    tab["inv2"] = inv2.transpose(1, 2, 0, 3).reshape(rows, width, lanes).astype(np.float32)
    ones = np.ones((depth, 1))
    odd_a, odd_b = sga > 0, sgb > 0
    sx2, sy2 = (sx**2)[None, :, None] * inv, (sy**2)[None, None, :] * inv
    tab["rowt"] = np.stack([
        to_rows(ones * sy),
        to_rows(ones * (sy * sgb)),
        to_rows(sx2[:, odd_a].sum(1)),
        to_rows(sx2[:, ~odd_a].sum(1)),
        to_rows((lz[:, None] + 2.0 + ly) * (b > 0)),
    ]).astype(np.float32)
    tab["colt"] = np.stack([
        to_cols(ones * sx),
        to_cols(ones * (sx * sga)),
        to_cols(sy2[:, :, odd_b].sum(2)),
        to_cols(sy2[:, :, ~odd_b].sum(2)),
        to_cols((lz[:, None] + 2.0 + lx) * (a > 0)),
    ]).astype(np.float32)
    tab["crnt"] = np.tile(np.tile(lz + 4.0, groups)[None], (8, 1)).astype(np.float32)
    tab["sx0"] = np.tile(sx[:, None], (1, height)).astype(np.float32)
    lane = np.zeros((8, height))
    lane[0], lane[1] = sy, sy * sgb
    lane[2], lane[3] = np.where(b > 0, sy, 1.0), sy * sgb
    tab["sy0"] = lane.astype(np.float32)
    return tab


def cosine_fwd(xs, scale):
    n = len(xs)
    if n == 1:
        return [xs[0] * (scale / np.sqrt(2.0))]
    half = n // 2
    even = cosine_fwd([xs[j] + xs[n - 1 - j] for j in range(half)], scale)
    diff = [xs[j] - xs[n - 1 - j] for j in range(half)]
    out = [None] * n
    for m in range(half):
        out[2 * m] = even[m]
        acc = None
        for j in range(half):
            term = diff[j] * float(scale * np.cos(np.pi * (2 * m + 1) * (2 * j + 1) / (2 * n)))
            acc = term if acc is None else acc + term
        out[2 * m + 1] = acc
    return out


def cosine_back(ys, scale):
    n = len(ys)
    if n == 1:
        return [ys[0] * (scale / np.sqrt(2.0))]
    half = n // 2
    even = cosine_back(ys[0::2], scale)
    out = [None] * n
    for j in range(half):
        acc = None
        for m in range(half):
            term = ys[2 * m + 1] * float(scale * np.cos(np.pi * (2 * m + 1) * (2 * j + 1) / (2 * n)))
            acc = term if acc is None else acc + term
        out[j] = even[j] + acc
        out[n - 1 - j] = even[j] - acc
    return out


def halves(x):
    hi = x.astype(BF16)
    return hi, (x - hi.astype(F32)).astype(BF16)


def times_sy(x, eyw):
    hi, lo = halves(x)
    n = x.shape[1]
    out = jnp.dot(jnp.concatenate([hi, lo], 1), eyw, preferred_element_type=F32)
    return out[:, :n] + out[:, n:]


def sx_times(exw, x):
    hi, lo = halves(x)
    return jnp.dot(exw, jnp.concatenate([hi, hi, lo], 0), preferred_element_type=F32)


def lane_id(shape):
    return lax.broadcasted_iota(jnp.int32, shape, 1)


def by_group(pieces, depth):
    group = lane_id(pieces[0].shape) // depth
    out = pieces[0]
    for h in range(1, len(pieces)):
        out = jnp.where(group == h, pieces[h], out)
    return out


def spread(x, depth):
    width = x.shape[1] // 2
    while width >= depth:
        x = x + pltpu.roll(x, width, 1)
        width //= 2
    return x


def pack(col, depth):
    groups = 128 // depth
    size = col.shape[0] // groups
    return by_group([col[h * size:(h + 1) * size] for h in range(groups)], depth)


def unpack(packed, depth):
    groups = 128 // depth
    group = lane_id(packed.shape) // depth
    return jnp.concatenate(
        [spread(jnp.where(group == h, packed, 0.0), depth) for h in range(groups)], 0
    )


def copies_t(kb):
    groups = 128 // kb.shape[0]
    return jnp.concatenate([kb] * groups, 0).T


def rows_from(kbt, depth):
    groups = 128 // depth
    size = kbt.shape[0] // groups
    return by_group([kbt[h * size:(h + 1) * size] for h in range(groups)], depth)


def rows_back(row, depth):
    groups = 128 // depth
    parts = [row] + [pltpu.roll(row, 128 - h * depth, 1) for h in range(1, groups)]
    return jnp.concatenate(parts, 0).T[:depth]


def total(x):
    return jnp.sum(x, 0, keepdims=True)


def sub_sums(ref):
    plus = minus = None
    for s in range(8):
        part = ref[:, s, :]
        if s % 2 == 1:
            plus = part if plus is None else plus + part
        else:
            minus = part if minus is None else minus + part
    return plus + minus, plus - minus


def with_tail(body, tails, size=8):
    width = body.shape[1]
    rows = list(tails)
    if len(rows) < size:
        rows.append(jnp.zeros((size - len(rows), width), F32))
    return jnp.concatenate([body, jnp.concatenate(rows, 0)], 0)


def front_kernel(charge_h, surf_h, eyw_h, exw_h, inv_h, sx0_h, sy0_h, base, *rest):
    msgs = rest[:4]
    charge, surf, eyw, exw, inv, sx0, sy0, work, part, first, sems = rest[4:]
    depth, width, height = charge.shape
    scale = np.sqrt(2.0 / depth)
    tiles = width // 8
    pairs = [(surf_h, surf)]
    pairs += [(charge_h.at[:, 8 * i:8 * i + 8, :], charge.at[:, 8 * i:8 * i + 8, :]) for i in range(tiles)]
    pairs += [(eyw_h, eyw), (exw_h, exw), (sx0_h, sx0), (sy0_h, sy0), (inv_h, inv)]
    copies = [pltpu.make_async_copy(src, dst, sems.at[i]) for i, (src, dst) in enumerate(pairs)]
    for copy in copies:
        copy.start()
    copies[0].wait()
    for i in range(tiles):
        copies[1 + i].wait()
        at = slice(8 * i, 8 * i + 8)
        xs = [charge[z, at, :] for z in range(depth)]
        xs[0] = xs[0] + surf[0, at, :]
        xs[-1] = xs[-1] + surf[1, at, :]
        for k, value in enumerate(cosine_fwd(xs, scale)):
            work[k, at, :] = value
    for copy in copies[1 + tiles:]:
        copy.wait()
    step = 4
    for c in range(0, depth, step):
        block = work[c:c + step].reshape(step * width, height)
        work[c:c + step] = times_sy(block, eyw[...]).reshape(step, width, height)
    lane = lane_id((width, 128))
    zero = jnp.zeros((width, 128), F32)
    near, far, own = zero, zero, zero
    for c in range(0, depth, 2):
        pair = sx_times(exw[...], jnp.concatenate([work[c], work[c + 1]], 1))
        for k in (c, c + 1):
            spec = pair[:, (k - c) * height:(k - c + 1) * height]
            inner = spec * inv[k]
            base[k] = inner
            first[k] = spec[0:8]
            part[k] = jnp.sum((inner * sx0[...]).reshape(width // 8, 8, height), 0)
            here = lane % depth == k
            near = jnp.where(here, jnp.sum(inner * sy0[0:1, :], 1, keepdims=True), near)
            far = jnp.where(here, jnp.sum(inner * sy0[1:2, :], 1, keepdims=True), far)
            own = jnp.where(here, spec[:, 0:1], own)
    row_near, row_far = sub_sums(part)
    own_t = copies_t(first[:, 0, :])
    corner = own_t[0:1]
    row = rows_from(own_t + copies_t(row_near), depth)
    at_zero = (lax.broadcasted_iota(jnp.int32, row.shape, 0) == 0) & (lane_id(row.shape) < depth)
    row = jnp.where(at_zero, 0.0, row)
    col = jnp.where(lax.broadcasted_iota(jnp.int32, own.shape, 0) == 0, 0.0, own + near)
    px = with_tail(row, [corner])
    nx = with_tail(rows_from(copies_t(row_far), depth), [])
    py = with_tail(pack(col, depth), [corner])
    ny = with_tail(pack(far, depth), [])
    for ref, value in zip(msgs, swapped("gx", nx, px) + swapped("gy", ny, py)):
        ref[...] = value


def swapped(axis, after, before):
    even = lax.axis_index(axis) % 2 == 0
    return jnp.where(even, before, after), jnp.where(even, after, before)


def assemble(depth, own, got):
    (nx, px), (ny, py) = swapped("gx", *own[:2]), swapped("gy", *own[2:])
    (from_nx, from_px), (from_ny, from_py) = swapped("gx", *got[:2]), swapped("gy", *got[2:])
    rows, cols = px.shape[0] - 8, py.shape[0] - 8
    row = px[:rows] + from_px[:rows]
    row_n = from_nx[:rows] + nx[:rows]
    col = unpack(py[:cols] + from_py[:cols], depth)
    col_n = unpack(from_ny[:cols] + ny[:cols], depth)
    c00 = px[rows:rows + 1] + from_px[rows:rows + 1] + from_py[cols:cols + 1]
    cx0 = from_nx[rows:rows + 1] + nx[rows:rows + 1] + from_py[cols + 1:cols + 2]
    c0y = from_ny[cols:cols + 1] + ny[cols:cols + 1] + from_px[rows + 1:rows + 2]
    return row, row_n, col, col_n, c00, cx0, c0y


def sizes(rows, cols):
    offs = np.cumsum([0, rows, rows, cols, cols])
    return [slice(int(offs[i]), int(offs[i + 1])) for i in range(4)] + [int(offs[4])]


def unpacked_state(state, rows, cols):
    s = sizes(rows, cols)
    at = s[4]
    return tuple(state[s[i], :] for i in range(4)) + tuple(state[at + i:at + i + 1, :] for i in range(3))


def schur_kernel(depth, want_moments, *refs):
    own, got = [r[...] for r in refs[0:4]], [r[...] for r in refs[4:8]]
    inv2, rowt, colt, crnt = refs[8:12]
    rest = list(refs[12:])
    before = rest.pop(0) if want_moments else None
    state, *outs = rest[:5]
    part, odd_rows, even_rows = rest[-3:]
    row, row_n, col, col_n, c00, cx0, c0y = assemble(depth, own, got)
    rows, cols = row.shape[0], col.shape[0]
    s = sizes(rows, cols)
    for i, piece in enumerate((row, row_n, col, col_n)):
        state[s[i], :] = piece
    state[s[4]:s[4] + 8, :] = jnp.concatenate([c00, cx0, c0y, jnp.zeros((5, 128), F32)], 0)
    sy, sys, g_odd, g_even, d_row = (rowt[i] for i in range(5))
    sx, sxs, h_odd, h_even, d_col = (colt[i] for i in range(5))
    row_p, row_m, col_p, col_m = row + row_n, row - row_n, col + col_n, col - col_n
    odd_rows[...] = row_p * sy
    even_rows[...] = row_m * sy
    col_w = (col_m * sx, col_p * sx)
    odd = lax.broadcasted_iota(jnp.int32, (8, 128), 0) % 2 == 1
    acc = [None, None]
    for r in range(rows):
        table = inv2[r].reshape(cols // 8, 8, 128)
        part[r] = jnp.sum(table * col_w[r % 2].reshape(cols // 8, 8, 128), 0)
        pick = jnp.where(odd, odd_rows[r:r + 1, :], even_rows[r:r + 1, :])
        term = table * pick[None]
        acc[r % 2] = term if acc[r % 2] is None else acc[r % 2] + term
    row_s, row_d = sub_sums(part)
    acc_s = spread((acc[1] + acc[0]).reshape(cols, 128), depth)
    acc_d = spread((acc[1] - acc[0]).reshape(cols, 128), depth)
    diag_o, diag_e = g_odd * row_p, g_even * row_m
    x_near = sy * row_s + (diag_o + diag_e)
    x_far = sy * row_d + (diag_o - diag_e)
    diag_o, diag_e = h_odd * col_p, h_even * col_m
    y_near = sx * acc_s + (diag_o + diag_e)
    y_far = sx * acc_d + (diag_o - diag_e)
    row_img = d_row * row - sy * c00 - sys * c0y - x_near
    col_img = d_col * col - sx * c00 - sxs * cx0 - y_near
    row_end0 = spread(total(sy * row), depth)
    row_end1 = spread(total(sys * row), depth)
    row_end1n = spread(total(sys * row_n), depth)
    col_end0 = total(sx * col)
    col_end1 = total(sxs * col)
    col_end1n = total(sxs * col_n)
    q00 = crnt[0:1, :] * c00 - row_end0 - col_end0
    px = with_tail(row_img, [q00])
    nx = with_tail(-x_far, [-col_end1, -col_end1n])
    py = with_tail(pack(col_img, depth), [q00])
    ny = with_tail(pack(-y_far, depth), [-row_end1, -row_end1n])
    if want_moments:
        row0, _, col0, _, c000, _, _ = unpacked_state(before, rows, cols)
        share = depth / 128.0

        def dot(x, y):
            return total(x[0] * y[0]) + share * (total(x[1] * y[1]) + x[2] * y[2])

        v0, v1 = (row0, col0, c000), (row, col, c00)
        m3 = total(row * row_img - row_n * x_far) + share * (
            total(col * col_img - col_n * y_far) + c00 * q00 - c0y * row_end1 - cx0 * col_end1
        )
        moments = [dot(v0, v0), dot(v0, v1), dot(v1, v1), m3]
        px = with_tail(row_img, [q00, q00, q00, q00] + moments)
        nx = with_tail(-x_far, [-col_end1, -col_end1n, c00, c00] + moments)
    sides = (ny, py) if want_moments else swapped("gy", ny, py)
    for ref, value in zip(outs, swapped("gx", nx, px) + sides):
        ref[...] = value


def cells_from(out, work, spectrum, exw, eyw):
    depth, width, height = work.shape
    for c in range(0, depth, 2):
        pair = sx_times(exw, jnp.concatenate([spectrum(c), spectrum(c + 1)], 1))
        work[c] = pair[:, :height]
        work[c + 1] = pair[:, height:]
    step = 4
    for c in range(0, depth, step):
        block = work[c:c + step].reshape(step * width, height)
        work[c:c + step] = times_sy(block, eyw).reshape(step, width, height)
    scale = np.sqrt(2.0 / depth)
    for i in range(width // 8):
        at = slice(8 * i, 8 * i + 8)
        for z, value in enumerate(cosine_back([work[k, at, :] for k in range(depth)], scale)):
            out[z, at, :] = value


def base_kernel(base, eyw, exw, out, work):
    cells_from(out, work, lambda k: base[k], exw[...], eyw[...])


def extend_kernel(state, eyw, exw, inv, sx0, sy0, out, work):
    depth, width, height = work.shape
    rows = height * depth // 128
    row, row_n, col, col_n, c00 = unpacked_state(state, rows, width)[:5]
    at_zero = (lax.broadcasted_iota(jnp.int32, row.shape, 0) == 0) & (lane_id(row.shape) < depth)
    row_p = rows_back(row + row_n, depth)
    row_m = rows_back(row - row_n, depth)
    row_full = rows_back(jnp.where(at_zero, c00, row), depth)
    odd = lax.broadcasted_iota(jnp.int32, (8, height), 0) % 2 == 1
    top = lax.broadcasted_iota(jnp.int32, (width, height), 0) == 0
    lane0 = lane_id((width, height)) == 0

    def spectrum(k):
        pick = jnp.where(odd, row_p[k:k + 1], row_m[k:k + 1])
        pick = jnp.broadcast_to(pick[None], (width // 8, 8, height)).reshape(width, height)
        rim = sx0[...] * pick + col[:, k:k + 1] * sy0[2:3, :] + col_n[:, k:k + 1] * sy0[3:4, :]
        return jnp.where(top, row_full[k:k + 1], jnp.where(lane0, 1.0, inv[k]) * rim)

    cells_from(out, work, spectrum, exw[...], eyw[...])


def rims_kernel(depth, s0, s1, bx, ax, py, got_bx, got_ax, from_py, ey, ex, cz, czt, out_rows, out_cols):
    packed = py.shape[0] - 8
    rows = bx.shape[0] - 8
    width = packed * 128 // depth
    _, px = swapped("gx", bx[...], ax[...])
    _, from_px = swapped("gx", got_bx[...], got_ax[...])
    v0 = unpacked_state(s0, rows, width)
    v1 = unpacked_state(s1, rows, width)
    v2 = (
        px[:rows, :] + from_px[:rows, :], None,
        unpack(py[:packed, :] + from_py[:packed, :], depth), None,
        px[rows:rows + 1, :] + from_px[rows:rows + 1, :] + from_py[packed:packed + 1, :],
    )
    at_zero = (lax.broadcasted_iota(jnp.int32, (rows, 128), 0) == 0) & (lane_id((rows, 128)) < depth)
    lines = [rows_back(jnp.where(at_zero, v[4], v[0]), depth) for v in (v0, v1, v2)]
    high = lax.Precision.HIGHEST
    lines = jnp.dot(jnp.concatenate(lines, 0), ey[...], precision=high, preferred_element_type=F32)
    lines = jnp.concatenate([lines[i * depth:(i + 1) * depth] for i in range(3)], 1)
    lines = jnp.dot(cz[...], lines, precision=high, preferred_element_type=F32)
    for i in range(3):
        out_rows[i] = lines[:, i * 128:(i + 1) * 128]
    sides = jnp.concatenate([v[2] for v in (v0, v1, v2)], 1)
    sides = jnp.dot(ex[...], sides, precision=high, preferred_element_type=F32)
    sides = jnp.concatenate([sides[:, i * 128:(i + 1) * 128] for i in range(3)], 0)
    sides = jnp.dot(sides, czt[...], precision=high, preferred_element_type=F32)
    for i in range(3):
        out_cols[i] = sides[i * width:(i + 1) * width]


def final_kernel(n_moments, *refs):
    cells_b, cells_0, cells_1, in_rows, in_cols = refs[:5]
    moms = refs[5:5 + n_moments]
    potential_h, residual_h, potential, residual, sems = refs[5 + n_moments:]
    depth, width, height = cells_b.shape
    m = moms[0][...]
    for other in moms[1:]:
        m = m + other[...]
    m = jnp.broadcast_to(jnp.sum(m, 1, keepdims=True), (8, 128))
    m0 = m[4:5]
    n1, n2, n3 = m[5:6] / m0, m[6:7] / m0, m[7:8] / m0
    det = n1 * n3 - n2 * n2
    fine = det > 1e-6 * (n1 * n3)
    safe = jnp.where(fine, det, 1.0)
    c0 = jnp.where(fine, (n3 - n1 * n2) / safe, 1.0 / n1)
    c1 = jnp.where(fine, (n1 * n1 - n2) / safe, 0.0)
    rim_row = in_rows[0] - c0 * in_rows[1] - c1 * in_rows[2]
    rim_col = in_cols[0] - c0 * in_cols[1] - c1 * in_cols[2]
    top = lax.broadcasted_iota(jnp.int32, (width, height), 0) == 0
    lane0 = lane_id((width, height)) == 0
    step = depth // 4
    copies = []
    for c in range(0, depth, step):
        for z in range(c, c + step):
            potential[z] = cells_b[z] + c0 * cells_0[z] + c1 * cells_1[z]
        copies.append((potential.at[c:c + step], potential_h.at[c:c + step]))
        copies[-1] = pltpu.make_async_copy(*copies[-1], sems.at[len(copies) - 1])
        copies[-1].start()
    for c in range(0, depth, step):
        for z in range(c, c + step):
            residual[z] = jnp.where(top, rim_row[z:z + 1], jnp.where(lane0, rim_col[:, z:z + 1], 0.0))
        copies.append((residual.at[c:c + step], residual_h.at[c:c + step]))
        copies[-1] = pltpu.make_async_copy(*copies[-1], sems.at[len(copies) - 1])
        copies[-1].start()
    for copy in copies:
        copy.wait()


def shifted(value, axis, by):
    n = lax.axis_size(axis)
    return lax.ppermute(value, axis, [(i, (i + by) % n) for i in range(n)])


def swap(value, axis, odd):
    n = lax.axis_size(axis)
    pairs = [(i, (i + 1) % n) for i in range(odd, n, 2)]
    return lax.ppermute(value, axis, pairs + [(j, i) for i, j in pairs])


def exchange(bx, ax, by, ay):
    return swap(bx, "gx", 1), swap(ax, "gx", 0), swap(by, "gy", 1), swap(ay, "gy", 0)


def pieces_over(value, axis):
    n, stride = lax.axis_size(axis), 1
    while True:
        radix = 4 if n % 4 == 0 else 2 if n % 2 == 0 else n
        parts = [value] + [shifted(value, axis, stride * j) for j in range(1, radix)]
        n, stride = n // radix, stride * radix
        if n == 1:
            return parts
        value = sum(parts[1:], parts[0])


def reduced_x(bx, ax):
    got_bx, got_ax = swap(bx, "gx", 1), swap(ax, "gx", 0)
    if lax.axis_size("gx") == 4:
        parts = [bx, got_ax, shifted(bx, "gx", 2), got_bx]
        parts = [part[-8:] for part in parts]
    else:
        parts = pieces_over(bx[-8:], "gx")
    return parts, got_bx, got_ax


def reduced_y(value):
    if lax.axis_size("gy") == 4:
        return [value, swap(value, "gy", 0), shifted(value, "gy", 2), swap(value, "gy", 1)]
    return pieces_over(value, "gy")


def call(kernel, outs, scratch, in_specs=None, out_specs=None):
    specs = {}
    if in_specs is not None:
        specs["in_specs"] = in_specs
    if out_specs is not None:
        specs["out_specs"] = out_specs
    return pl.pallas_call(
        kernel,
        out_shape=[jax.ShapeDtypeStruct(shape, F32) for shape in outs],
        scratch_shapes=[pltpu.VMEM(s, F32) if isinstance(s, tuple) else s for s in scratch],
        compiler_params=pltpu.CompilerParams(vmem_limit_bytes=48 * 1024 * 1024),
        **specs,
    )


def on_device(charge, surface_charge):
    depth, width, height = charge.shape
    tab = {name: jnp.asarray(value) for name, value in make_tables(depth, width, height).items()}
    rows, packed = height * depth // 128, width * depth // 128
    msgs = [(rows + 8, 128)] * 2 + [(packed + 8, 128)] * 2
    state = (2 * rows + 2 * width + 8, 128)
    block = (depth, width, height)
    anywhere = pl.BlockSpec(memory_space=pltpu.HBM)
    whole = pl.BlockSpec(memory_space=pltpu.VMEM)
    fronts = (charge, surface_charge) + tuple(tab[n] for n in ("eyw", "exw", "inv", "sx0", "sy0"))
    landing = [pltpu.VMEM(x.shape, x.dtype) for x in fronts]
    fronts = [pltpu.with_memory_space_constraint(x, pltpu.HBM) for x in fronts]
    base, *own = call(
        front_kernel, [block] + msgs,
        landing + [block, (depth, 8, height), (depth, 8, height), pltpu.SemaphoreType.DMA((6 + width // 8,))],
        in_specs=[anywhere] * 7,
    )(*fronts)
    got = exchange(*own)
    cells_b = call(base_kernel, [block], [block])(base, tab["eyw"], tab["exw"])[0]
    *got, cells_b = lax.optimization_barrier((*got, cells_b))
    tables = (tab["inv2"], tab["rowt"], tab["colt"], tab["crnt"])
    scratch = [(rows, 8, 128), (rows, 128), (rows, 128)]
    s0, *own = call(lambda *r: schur_kernel(depth, False, *r), [state] + msgs, scratch)(*own, *got, *tables)
    got = exchange(*own)
    extend = call(extend_kernel, [block], [block])
    backs = tuple(tab[n] for n in ("eyw", "exw", "inv", "sx0", "sy0"))
    cells_0 = extend(s0, *backs)[0]
    *got, cells_0 = lax.optimization_barrier((*got, cells_0))
    s1, *own = call(lambda *r: schur_kernel(depth, True, *r), [state] + msgs, scratch)(*own, *got, *tables, s0)
    parts, got_bx, got_ax = reduced_x(*own[:2])
    from_py = shifted(own[2], "gy", 1)
    cells_1 = extend(s1, *backs)[0]
    *parts, cells_1 = lax.optimization_barrier((*parts, cells_1))
    parts = reduced_y(sum(parts[1:], parts[0]))
    rim = call(lambda *r: rims_kernel(depth, *r), [(3, depth, height), (3, width, 128)], [])(
        s0, s1, own[0], own[1], own[3], got_bx, got_ax, from_py, tab["ey"], tab["ex"], tab["cz"], tab["czt"]
    )
    return call(
        lambda *r: final_kernel(len(parts), *r), [block, block], [block, block, pltpu.SemaphoreType.DMA((8,))],
        in_specs=[whole] * (5 + len(parts)), out_specs=[anywhere, anywhere],
    )(cells_b, cells_0, cells_1, *rim, *parts)


def solution(mesh):
    spec = P(None, ("slab", "gx"), "gy")
    return jax.shard_map(
        on_device, mesh=mesh, in_specs=(spec, spec), out_specs=(spec, spec), check_vma=False
    )
```

```python
import numpy as np
import jax
import jax.numpy as jnp
from jax import lax
from jax.experimental import pallas as pl
from jax.experimental.pallas import tpu as pltpu
from jax.sharding import PartitionSpec as P
import ml_dtypes

SCREEN = 0.02
BF16 = jnp.bfloat16
F32 = jnp.float32


def sine_ext(n):
    i = np.arange(n)
    table = np.sqrt(2.0 / n) * np.sin(np.pi * np.outer(i, i) / n)
    table[0, 0] = 1.0
    return table


def split_bf16(table):
    hi = table.astype(np.float32).astype(ml_dtypes.bfloat16)
    lo = (table - hi.astype(np.float64)).astype(np.float32).astype(ml_dtypes.bfloat16)
    return hi, lo


def make_tables(depth, width, height):
    lanes = 128
    groups = lanes // depth
    rows = height // groups
    tab = {}
    hi, lo = split_bf16(sine_ext(height))
    tab["eyw"] = np.block([[hi, lo], [hi, np.zeros_like(lo)]])
    hi, lo = split_bf16(sine_ext(width) * np.sqrt(2.0 / depth))
    tab["exw"] = np.concatenate([hi, lo, hi], 1)
    sign = np.where(np.arange(height) % 2 == 1, 1.0, -1.0)
    unit = (np.arange(height) == 0) * 1.0
    wide = np.zeros((height, lanes))
    for g, values in enumerate((1.0 - unit, sign * (1.0 - unit), unit)):
        wide[:, g * depth:(g + 1) * depth] = values[:, None]
    tab["rimw"] = np.concatenate([wide, wide], 0).astype(ml_dtypes.bfloat16)
    wide[0, :depth] = 1.0
    wide[:, 2 * depth:] = 0.0
    tab["colw"] = np.concatenate([wide.T, wide.T], 0).astype(ml_dtypes.bfloat16)
    tab["ey"], tab["ex"] = sine_ext(height).astype(np.float32), sine_ext(width).astype(np.float32)
    z = np.arange(depth)
    cos = np.cos(np.pi * np.outer(z + 0.5, z) / depth) * np.sqrt(2.0 / depth)
    cos[:, 0] = np.sqrt(1.0 / depth)
    tab["cz"] = cos.astype(np.float32)
    czt = np.zeros((lanes, lanes))
    czt[:depth, :depth] = cos.T
    tab["czt"] = czt.astype(np.float32)
    lz = SCREEN + 2.0 - 2.0 * np.cos(np.pi * z / depth)
    a = np.arange(width)
    b = np.arange(height)
    lx = 2.0 - 2.0 * np.cos(np.pi * a / width)
    ly = 2.0 - 2.0 * np.cos(np.pi * b / height)
    sx = np.sqrt(2.0 / width) * np.sin(np.pi * a / width)
    sy = np.sqrt(2.0 / height) * np.sin(np.pi * b / height)
    sga = np.where(a % 2 == 1, 1.0, -1.0)
    sgb = np.where(b % 2 == 1, 1.0, -1.0)
    inside = (a[:, None] > 0) & (b[None, :] > 0)
    inv = np.where(inside[None], 1.0 / (lz[:, None, None] + lx[None, :, None] + ly[None, None, :]), 0.0)
    tab["inv"] = inv.astype(np.float32)
    tab["lxy"] = np.where(inside, lx[:, None] + ly[None, :], 1e30).astype(np.float32)

    def to_rows(kb):
        return kb.T.reshape(groups, rows, depth).transpose(1, 0, 2).reshape(rows, lanes)

    def to_cols(ka):
        return np.tile(ka.T, (1, groups))

    inv2 = inv.transpose(2, 1, 0).reshape(groups, rows, width, depth)
    tab["inv2"] = inv2.transpose(1, 2, 0, 3).reshape(rows, width, lanes).astype(np.float32)
    ones = np.ones((depth, 1))
    odd_a, odd_b = sga > 0, sgb > 0
    sx2, sy2 = (sx**2)[None, :, None] * inv, (sy**2)[None, None, :] * inv
    tab["rowt"] = np.stack([
        to_rows(ones * sy),
        to_rows(ones * (sy * sgb)),
        to_rows(sx2[:, odd_a].sum(1)),
        to_rows(sx2[:, ~odd_a].sum(1)),
        to_rows((lz[:, None] + 2.0 + ly) * (b > 0)),
    ]).astype(np.float32)
    tab["colt"] = np.stack([
        to_cols(ones * sx),
        to_cols(ones * (sx * sga)),
        to_cols(sy2[:, :, odd_b].sum(2)),
        to_cols(sy2[:, :, ~odd_b].sum(2)),
        to_cols((lz[:, None] + 2.0 + lx) * (a > 0)),
    ]).astype(np.float32)
    tab["crnt"] = np.tile(np.tile(lz + 4.0, groups)[None], (8, 1)).astype(np.float32)
    line = np.where(b > 0, sy, 1.0)[None]
    tab["line"] = np.tile(line, (8, 1)).astype(np.float32)
    tab["sx0"] = np.tile(sx[:, None], (1, height)).astype(np.float32)
    return tab


def cosine_two(xs):
    n = len(xs)
    if n == 1:
        return list(xs)
    half = n // 2
    out = [None] * n
    out[0::2] = cosine_two([xs[j] + xs[n - 1 - j] for j in range(half)])
    out[1::2] = cosine_four([xs[j] - xs[n - 1 - j] for j in range(half)])
    return out


def cosine_three(ys):
    n = len(ys)
    if n == 1:
        return list(ys)
    half = n // 2
    even, odd = cosine_three(ys[0::2]), cosine_four(ys[1::2])
    return [even[j] + odd[j] for j in range(half)] + [even[j] - odd[j] for j in reversed(range(half))]


def cosine_four(xs):
    n = len(xs)
    if n == 1:
        return [xs[0] * float(np.cos(np.pi / 4))]
    half = n // 2
    plus, minus = [], []
    for j in range(half):
        c, s = (float(f(np.pi * (2 * j + 1) / (4 * n))) for f in (np.cos, np.sin))
        x, y = xs[j], xs[n - 1 - j]
        plus.append(x * c + y * s)
        minus.append(x * s - y * c if j % 2 == 0 else y * c - x * s)
    c, s = cosine_two(plus), cosine_two(minus)[::-1]
    out = [None] * n
    out[0], out[n - 1] = c[0], s[half - 1]
    for k in range(1, half):
        out[2 * k] = c[k] - s[k - 1]
        out[2 * k - 1] = c[k] + s[k - 1]
    return out


ROOT_HALF = float(np.sqrt(0.5))


def halves(x):
    hi = x.astype(BF16)
    return hi, (x - hi.astype(F32)).astype(BF16)


def times_sy(x, eyw):
    hi, lo = halves(x)
    n = x.shape[1]
    out = jnp.dot(jnp.concatenate([hi, lo], 1), eyw, preferred_element_type=F32)
    return out[:, :n] + out[:, n:]


def sx_times(exw, x):
    hi, lo = halves(x)
    return jnp.dot(exw, jnp.concatenate([hi, hi, lo], 0), preferred_element_type=F32)


def lane_id(shape):
    return lax.broadcasted_iota(jnp.int32, shape, 1)


def by_group(pieces, depth):
    group = lane_id(pieces[0].shape) // depth
    out = pieces[0]
    for h in range(1, len(pieces)):
        out = jnp.where(group == h, pieces[h], out)
    return out


def spread(x, depth):
    width = x.shape[1] // 2
    while width >= depth:
        x = x + pltpu.roll(x, width, 1)
        width //= 2
    return x


def pack(col, depth):
    groups = 128 // depth
    size = col.shape[0] // groups
    return by_group([col[h * size:(h + 1) * size] for h in range(groups)], depth)


def unpack(packed, depth):
    groups = 128 // depth
    group = lane_id(packed.shape) // depth
    return jnp.concatenate(
        [spread(jnp.where(group == h, packed, 0.0), depth) for h in range(groups)], 0
    )


def copies_t(kb):
    groups = 128 // kb.shape[0]
    return jnp.concatenate([kb] * groups, 0).T


def rows_from(kbt, depth):
    groups = 128 // depth
    size = kbt.shape[0] // groups
    return by_group([kbt[h * size:(h + 1) * size] for h in range(groups)], depth)


def rows_back(row, depth):
    groups = 128 // depth
    parts = [row] + [pltpu.roll(row, 128 - h * depth, 1) for h in range(1, groups)]
    return jnp.concatenate(parts, 0).T[:depth]


def total(x):
    return jnp.sum(x, 0, keepdims=True)


def sub_sums(ref):
    plus = minus = None
    for s in range(8):
        part = ref[:, s, :]
        if s % 2 == 1:
            plus = part if plus is None else plus + part
        else:
            minus = part if minus is None else minus + part
    return plus + minus, plus - minus


def with_tail(body, tails, size=8):
    width = body.shape[1]
    rows = list(tails)
    if len(rows) < size:
        rows.append(jnp.zeros((size - len(rows), width), F32))
    return jnp.concatenate([body, jnp.concatenate(rows, 0)], 0)


def front_kernel(charge_h, surf_h, eyw_h, exw_h, lxy_h, sx0_h, rimw_h, line_h, base, *rest):
    msgs = rest[:4]
    charge, surf, eyw, exw, lxy, sx0, rimw, line, work, inv, rims, part, first, sems = rest[4:]
    depth, width, height = charge.shape
    tiles = width // 8
    pairs = [(lxy_h, lxy), (surf_h, surf)]
    pairs += [(charge_h.at[:, 8 * i:8 * i + 8, :], charge.at[:, 8 * i:8 * i + 8, :]) for i in range(tiles)]
    pairs += [(eyw_h, eyw), (exw_h, exw), (sx0_h, sx0), (rimw_h, rimw), (line_h, line)]
    copies = [pltpu.make_async_copy(src, dst, sems.at[i]) for i, (src, dst) in enumerate(pairs)]
    for copy in copies:
        copy.start()
    copies[0].wait()
    for k in range(depth):
        inv[k] = 1.0 / (lxy[...] + float(SCREEN + 2.0 - 2.0 * np.cos(np.pi * k / depth)))
    copies[1].wait()

    for i in range(tiles):
        copies[2 + i].wait()
        at = slice(8 * i, 8 * i + 8)
        xs = [charge[z, at, :] for z in range(depth)]
        xs[0] = xs[0] + surf[0, at, :]
        xs[-1] = xs[-1] + surf[1, at, :]
        for k, value in enumerate(cosine_two(xs)):
            work[k, at, :] = value * ROOT_HALF if k == 0 else value
    for copy in copies[2 + tiles:]:
        copy.wait()
    for c in range(0, depth, 4):
        block = work[c:c + 4].reshape(4 * width, height)
        work[c:c + 4] = times_sy(block, eyw[...]).reshape(4, width, height)
    lane = lane_id((width, 128))
    for c in range(0, depth, 2):
        pair = sx_times(exw[...], jnp.concatenate([work[c], work[c + 1]], 1))
        for k in (c, c + 1):
            spec = pair[:, (k - c) * height:(k - c + 1) * height]
            inner = spec * inv[k]
            base[k] = inner
            first[k] = spec[0:8]
            part[k] = jnp.sum((inner * sx0[...]).reshape(width // 8, 8, height), 0)
            hi, lo = halves(jnp.where(lane == 0, spec, inner * line[0:1, :]))
            rims[k * width:(k + 1) * width, :] = jnp.concatenate([hi, lo], 1)
    step = 8
    found = jnp.zeros((width, 128), F32)
    for c in range(0, depth, step):
        out = jnp.dot(rims[c * width:(c + step) * width, :], rimw[...], preferred_element_type=F32)
        for k in range(c, c + step):
            one = out[(k - c) * width:(k - c + 1) * width]
            found = jnp.where(lane % depth == k, one, found)
    near, far, own = (spread(jnp.where(lane // depth == g, found, 0.0), depth) for g in range(3))
    row_near, row_far = sub_sums(part)
    own_t = copies_t(first[:, 0, :])
    corner = own_t[0:1]
    row = rows_from(own_t + copies_t(row_near), depth)
    at_zero = (lax.broadcasted_iota(jnp.int32, row.shape, 0) == 0) & (lane_id(row.shape) < depth)
    row = jnp.where(at_zero, 0.0, row)
    col = jnp.where(lax.broadcasted_iota(jnp.int32, own.shape, 0) == 0, 0.0, own + near)
    px = with_tail(row, [corner])
    nx = with_tail(rows_from(copies_t(row_far), depth), [])
    py = with_tail(pack(col, depth), [corner])
    ny = with_tail(pack(far, depth), [])
    for ref, value in zip(msgs, swapped("gx", nx, px) + swapped("gy", ny, py)):
        ref[...] = value


def swapped(axis, after, before):
    even = lax.axis_index(axis) % 2 == 0
    return jnp.where(even, before, after), jnp.where(even, after, before)


def assemble(depth, own, got):
    (nx, px), (ny, py) = swapped("gx", *own[:2]), swapped("gy", *own[2:])
    (from_nx, from_px), (from_ny, from_py) = swapped("gx", *got[:2]), swapped("gy", *got[2:])
    rows, cols = px.shape[0] - 8, py.shape[0] - 8
    row = px[:rows] + from_px[:rows]
    row_n = from_nx[:rows] + nx[:rows]
    col = unpack(py[:cols] + from_py[:cols], depth)
    col_n = unpack(from_ny[:cols] + ny[:cols], depth)
    c00 = px[rows:rows + 1] + from_px[rows:rows + 1] + from_py[cols:cols + 1]
    cx0 = from_nx[rows:rows + 1] + nx[rows:rows + 1] + from_py[cols + 1:cols + 2]
    c0y = from_ny[cols:cols + 1] + ny[cols:cols + 1] + from_px[rows + 1:rows + 2]
    return row, row_n, col, col_n, c00, cx0, c0y


def sizes(rows, cols):
    offs = np.cumsum([0, rows, rows, cols, cols])
    return [slice(int(offs[i]), int(offs[i + 1])) for i in range(4)] + [int(offs[4])]


def unpacked_state(state, rows, cols):
    s = sizes(rows, cols)
    at = s[4]
    return tuple(state[s[i], :] for i in range(4)) + tuple(state[at + i:at + i + 1, :] for i in range(3))


def schur_kernel(depth, want_moments, *refs):
    own, got = [r[...] for r in refs[0:4]], [r[...] for r in refs[4:8]]
    inv2, rowt, colt, crnt = refs[8:12]
    rest = list(refs[12:])
    before = rest.pop(0) if want_moments else None
    state, *outs = rest[:5]
    part, odd_rows, even_rows = rest[-3:]
    row, row_n, col, col_n, c00, cx0, c0y = assemble(depth, own, got)
    rows, cols = row.shape[0], col.shape[0]
    s = sizes(rows, cols)
    for i, piece in enumerate((row, row_n, col, col_n)):
        state[s[i], :] = piece
    state[s[4]:s[4] + 8, :] = jnp.concatenate([c00, cx0, c0y, jnp.zeros((5, 128), F32)], 0)
    sy, sys, g_odd, g_even, d_row = (rowt[i] for i in range(5))
    sx, sxs, h_odd, h_even, d_col = (colt[i] for i in range(5))
    row_p, row_m, col_p, col_m = row + row_n, row - row_n, col + col_n, col - col_n
    odd_rows[...] = row_p * sy
    even_rows[...] = row_m * sy
    col_w = (col_m * sx, col_p * sx)
    odd = lax.broadcasted_iota(jnp.int32, (8, 128), 0) % 2 == 1
    acc = [None, None]
    for r in range(rows):
        table = inv2[r].reshape(cols // 8, 8, 128)
        part[r] = jnp.sum(table * col_w[r % 2].reshape(cols // 8, 8, 128), 0)
        pick = jnp.where(odd, odd_rows[r:r + 1, :], even_rows[r:r + 1, :])
        term = table * pick[None]
        acc[r % 2] = term if acc[r % 2] is None else acc[r % 2] + term
    row_s, row_d = sub_sums(part)
    acc_s = spread((acc[1] + acc[0]).reshape(cols, 128), depth)
    acc_d = spread((acc[1] - acc[0]).reshape(cols, 128), depth)
    diag_o, diag_e = g_odd * row_p, g_even * row_m
    x_near = sy * row_s + (diag_o + diag_e)
    x_far = sy * row_d + (diag_o - diag_e)
    diag_o, diag_e = h_odd * col_p, h_even * col_m
    y_near = sx * acc_s + (diag_o + diag_e)
    y_far = sx * acc_d + (diag_o - diag_e)
    row_img = d_row * row - sy * c00 - sys * c0y - x_near
    col_img = d_col * col - sx * c00 - sxs * cx0 - y_near
    row_end0 = spread(total(sy * row), depth)
    row_end1 = spread(total(sys * row), depth)
    row_end1n = spread(total(sys * row_n), depth)
    col_end0 = total(sx * col)
    col_end1 = total(sxs * col)
    col_end1n = total(sxs * col_n)
    q00 = crnt[0:1, :] * c00 - row_end0 - col_end0
    px = with_tail(row_img, [q00])
    nx = with_tail(-x_far, [-col_end1, -col_end1n])
    py = with_tail(pack(col_img, depth), [q00])
    ny = with_tail(pack(-y_far, depth), [-row_end1, -row_end1n])
    if want_moments:
        row0, _, col0, _, c000, _, _ = unpacked_state(before, rows, cols)
        share = depth / 128.0

        def dot(x, y):
            return total(x[0] * y[0]) + share * (total(x[1] * y[1]) + x[2] * y[2])

        v0, v1 = (row0, col0, c000), (row, col, c00)
        m3 = total(row * row_img - row_n * x_far) + share * (
            total(col * col_img - col_n * y_far) + c00 * q00 - c0y * row_end1 - cx0 * col_end1
        )
        moments = [dot(v0, v0), dot(v0, v1), dot(v1, v1), m3]
        px = with_tail(row_img, [q00, q00, q00, q00] + moments)
        nx = with_tail(-x_far, [-col_end1, -col_end1n, c00, c00] + moments)
    sides = (ny, py) if want_moments else swapped("gy", ny, py)
    for ref, value in zip(outs, swapped("gx", nx, px) + sides):
        ref[...] = value


def cells_from(out, work, spectrum, exw, eyw):
    depth, width, height = work.shape
    for c in range(0, depth, 2):
        pair = sx_times(exw, jnp.concatenate([spectrum(c), spectrum(c + 1)], 1))
        work[c] = pair[:, :height]
        work[c + 1] = pair[:, height:]
    step = 4
    for c in range(0, depth, step):
        block = work[c:c + step].reshape(step * width, height)
        work[c:c + step] = times_sy(block, eyw).reshape(step, width, height)
    for i in range(width // 8):
        at = slice(8 * i, 8 * i + 8)
        ys = [work[k, at, :] for k in range(depth)]
        for z, value in enumerate(cosine_three([ys[0] * ROOT_HALF] + ys[1:])):
            out[z, at, :] = value


def base_kernel(base, eyw, exw, out, work):
    cells_from(out, work, lambda k: base[k], exw[...], eyw[...])


def extend_kernel(state, eyw, exw, inv, sx0, colw, line, out, work):
    depth, width, height = work.shape
    rows = height * depth // 128
    row, row_n, col, col_n, c00 = unpacked_state(state, rows, width)[:5]
    at_zero = (lax.broadcasted_iota(jnp.int32, row.shape, 0) == 0) & (lane_id(row.shape) < depth)
    row_p = rows_back(row + row_n, depth)
    row_m = rows_back(row - row_n, depth)
    row_full = rows_back(jnp.where(at_zero, c00, row), depth)
    odd = lax.broadcasted_iota(jnp.int32, (8, height), 0) % 2 == 1
    top = lax.broadcasted_iota(jnp.int32, (8, height), 0) == 0
    lane0 = lane_id((width, height)) == 0
    lane = lane_id((width, 256)) % depth
    hi, lo = halves(by_group([col, col_n] + [jnp.zeros_like(col)] * (128 // depth - 2), depth))
    both = jnp.concatenate([hi, lo], 1)
    step = 8
    for c in range(0, depth, step):
        rim = jnp.concatenate([jnp.where(lane == k, both, jnp.zeros_like(both)) for k in range(c, c + step)], 0)
        rim = jnp.dot(rim, colw[...], preferred_element_type=F32)
        for k in range(c, c + step):
            side = rim[(k - c) * width:(k - c + 1) * width]
            pick = jnp.where(odd, row_p[k:k + 1], row_m[k:k + 1])
            pick = jnp.broadcast_to(pick[None], (width // 8, 8, height)).reshape(width, height)
            value = jnp.where(lane0, 1.0, inv[k]) * (sx0[...] * pick + side * line[0:1, :])
            work[k] = value
            work[k, 0:8, :] = jnp.where(top, row_full[k:k + 1], value[0:8])
    cells_from(out, work, lambda k: work[k], exw[...], eyw[...])


def rims_kernel(depth, s0, s1, bx, ax, py, got_bx, got_ax, from_py, ey, ex, cz, czt, out_rows, out_cols):
    packed = py.shape[0] - 8
    rows = bx.shape[0] - 8
    width = packed * 128 // depth
    _, px = swapped("gx", bx[...], ax[...])
    _, from_px = swapped("gx", got_bx[...], got_ax[...])
    v0 = unpacked_state(s0, rows, width)
    v1 = unpacked_state(s1, rows, width)
    v2 = (
        px[:rows, :] + from_px[:rows, :], None,
        unpack(py[:packed, :] + from_py[:packed, :], depth), None,
        px[rows:rows + 1, :] + from_px[rows:rows + 1, :] + from_py[packed:packed + 1, :],
    )
    at_zero = (lax.broadcasted_iota(jnp.int32, (rows, 128), 0) == 0) & (lane_id((rows, 128)) < depth)
    lines = [rows_back(jnp.where(at_zero, v[4], v[0]), depth) for v in (v0, v1, v2)]
    high = lax.Precision.HIGHEST
    lines = jnp.dot(jnp.concatenate(lines, 0), ey[...], precision=high, preferred_element_type=F32)
    lines = jnp.concatenate([lines[i * depth:(i + 1) * depth] for i in range(3)], 1)
    lines = jnp.dot(cz[...], lines, precision=high, preferred_element_type=F32)
    for i in range(3):
        out_rows[i] = lines[:, i * 128:(i + 1) * 128]
    sides = jnp.concatenate([v[2] for v in (v0, v1, v2)], 1)
    sides = jnp.dot(ex[...], sides, precision=high, preferred_element_type=F32)
    sides = jnp.concatenate([sides[:, i * 128:(i + 1) * 128] for i in range(3)], 0)
    sides = jnp.dot(sides, czt[...], precision=high, preferred_element_type=F32)
    for i in range(3):
        out_cols[i] = sides[i * width:(i + 1) * width]


def final_kernel(n_moments, *refs):
    cells_b, cells_0, cells_1, in_rows, in_cols = refs[:5]
    moms = refs[5:5 + n_moments]
    potential_h, residual_h, potential, residual, sems = refs[5 + n_moments:]
    depth, width, height = cells_b.shape
    m = moms[0][...]
    for other in moms[1:]:
        m = m + other[...]
    m = jnp.broadcast_to(jnp.sum(m, 1, keepdims=True), (8, 128))
    m0 = m[4:5]
    n1, n2, n3 = m[5:6] / m0, m[6:7] / m0, m[7:8] / m0
    det = n1 * n3 - n2 * n2
    fine = det > 1e-6 * (n1 * n3)
    safe = jnp.where(fine, det, 1.0)
    c0 = jnp.where(fine, (n3 - n1 * n2) / safe, 1.0 / n1)
    c1 = jnp.where(fine, (n1 * n1 - n2) / safe, 0.0)
    rim_row = in_rows[0] - c0 * in_rows[1] - c1 * in_rows[2]
    rim_col = in_cols[0] - c0 * in_cols[1] - c1 * in_cols[2]
    top = lax.broadcasted_iota(jnp.int32, (width, height), 0) == 0
    lane0 = lane_id((width, height)) == 0
    step = depth // 4
    copies = []
    for c in range(0, depth, step):
        for z in range(c, c + step):
            potential[z] = cells_b[z] + c0 * cells_0[z] + c1 * cells_1[z]
        copies.append((potential.at[c:c + step], potential_h.at[c:c + step]))
        copies[-1] = pltpu.make_async_copy(*copies[-1], sems.at[len(copies) - 1])
        copies[-1].start()
    for c in range(0, depth, step):
        for z in range(c, c + step):
            residual[z] = jnp.where(top, rim_row[z:z + 1], jnp.where(lane0, rim_col[:, z:z + 1], 0.0))
        copies.append((residual.at[c:c + step], residual_h.at[c:c + step]))
        copies[-1] = pltpu.make_async_copy(*copies[-1], sems.at[len(copies) - 1])
        copies[-1].start()
    for copy in copies:
        copy.wait()


def shifted(value, axis, by):
    n = lax.axis_size(axis)
    return lax.ppermute(value, axis, [(i, (i + by) % n) for i in range(n)])


def swap(value, axis, odd):
    n = lax.axis_size(axis)
    pairs = [(i, (i + 1) % n) for i in range(odd, n, 2)]
    return lax.ppermute(value, axis, pairs + [(j, i) for i, j in pairs])


def exchange(bx, ax, by, ay):
    return swap(bx, "gx", 1), swap(ax, "gx", 0), swap(by, "gy", 1), swap(ay, "gy", 0)


def pieces_over(value, axis):
    n, stride = lax.axis_size(axis), 1
    while True:
        radix = 4 if n % 4 == 0 else 2 if n % 2 == 0 else n
        parts = [value] + [shifted(value, axis, stride * j) for j in range(1, radix)]
        n, stride = n // radix, stride * radix
        if n == 1:
            return parts
        value = sum(parts[1:], parts[0])


def reduced_x(bx, ax):
    got_bx, got_ax = swap(bx, "gx", 1), swap(ax, "gx", 0)
    if lax.axis_size("gx") == 4:
        parts = [bx, got_ax, shifted(ax, "gx", 2), got_bx]
        parts = [part[-8:] for part in parts]
    else:
        parts = pieces_over(bx[-8:], "gx")
    return parts, got_bx, got_ax


def reduced_y(value):
    if lax.axis_size("gy") == 4:
        return [value, swap(value, "gy", 0), shifted(value, "gy", 2), swap(value, "gy", 1)]
    return pieces_over(value, "gy")


def call(kernel, outs, scratch, in_specs=None, out_specs=None):
    specs = {}
    if in_specs is not None:
        specs["in_specs"] = in_specs
    if out_specs is not None:
        specs["out_specs"] = out_specs
    return pl.pallas_call(
        kernel,
        out_shape=[jax.ShapeDtypeStruct(shape, F32) for shape in outs],
        scratch_shapes=[pltpu.VMEM(s, F32) if isinstance(s, tuple) else s for s in scratch],
        compiler_params=pltpu.CompilerParams(vmem_limit_bytes=48 * 1024 * 1024),
        **specs,
    )


def on_device(charge, surface_charge):
    depth, width, height = charge.shape
    tab = {name: jnp.asarray(value) for name, value in make_tables(depth, width, height).items()}
    rows, packed = height * depth // 128, width * depth // 128
    msgs = [(rows + 8, 128)] * 2 + [(packed + 8, 128)] * 2
    state = (2 * rows + 2 * width + 8, 128)
    block = (depth, width, height)
    anywhere = pl.BlockSpec(memory_space=pltpu.HBM)
    whole = pl.BlockSpec(memory_space=pltpu.VMEM)
    fronts = (charge, surface_charge) + tuple(tab[n] for n in ("eyw", "exw", "lxy", "sx0", "rimw", "line"))
    landing = [pltpu.VMEM(x.shape, x.dtype) for x in fronts]
    fronts = [pltpu.with_memory_space_constraint(x, pltpu.HBM) for x in fronts]
    base, *own = call(
        front_kernel, [block] + msgs,
        landing + [block, block, pltpu.VMEM((depth * width, 2 * height), BF16), (depth, 8, height), (depth, 8, height),
                   pltpu.SemaphoreType.DMA((7 + width // 8,))],
        in_specs=[anywhere] * 8,
    )(*fronts)
    got = exchange(*own)
    cells_b = call(base_kernel, [block], [block])(base, tab["eyw"], tab["exw"])[0]
    *got, cells_b = lax.optimization_barrier((*got, cells_b))
    tables = (tab["inv2"], tab["rowt"], tab["colt"], tab["crnt"])
    scratch = [(rows, 8, 128), (rows, 128), (rows, 128)]
    s0, *own = call(lambda *r: schur_kernel(depth, False, *r), [state] + msgs, scratch)(*own, *got, *tables)
    got = exchange(*own)
    extend = call(extend_kernel, [block], [block])
    backs = tuple(tab[n] for n in ("eyw", "exw", "inv", "sx0", "colw", "line"))
    cells_0 = extend(s0, *backs)[0]
    *got, cells_0 = lax.optimization_barrier((*got, cells_0))
    s1, *own = call(lambda *r: schur_kernel(depth, True, *r), [state] + msgs, scratch)(*own, *got, *tables, s0)
    parts, got_bx, got_ax = reduced_x(*own[:2])
    from_py = shifted(own[2], "gy", 1)
    cells_1 = extend(s1, *backs)[0]
    *parts, cells_1 = lax.optimization_barrier((*parts, cells_1))
    parts = reduced_y(sum(parts[1:], parts[0]))
    rim = call(lambda *r: rims_kernel(depth, *r), [(3, depth, height), (3, width, 128)], [])(
        s0, s1, own[0], own[1], own[3], got_bx, got_ax, from_py, tab["ey"], tab["ex"], tab["cz"], tab["czt"]
    )
    return call(
        lambda *r: final_kernel(len(parts), *r), [block, block], [block, block, pltpu.SemaphoreType.DMA((8,))],
        in_specs=[whole] * (5 + len(parts)), out_specs=[anywhere, anywhere],
    )(cells_b, cells_0, cells_1, *rim, *parts)


def solution(mesh):
    spec = P(None, ("slab", "gx"), "gy")
    return jax.shard_map(
        on_device, mesh=mesh, in_specs=(spec, spec), out_specs=(spec, spec), check_vma=False
    )
```

```python
import numpy as np
import jax
import jax.numpy as jnp
from jax import lax
from jax.experimental import pallas as pl
from jax.experimental.pallas import tpu as pltpu
from jax.sharding import PartitionSpec as P
import ml_dtypes

SCREEN = 0.02
BF16 = jnp.bfloat16
F32 = jnp.float32


def sine_ext(n):
    i = np.arange(n)
    table = np.sqrt(2.0 / n) * np.sin(np.pi * np.outer(i, i) / n)
    table[0, 0] = 1.0
    return table


def split_bf16(table):
    hi = table.astype(np.float32).astype(ml_dtypes.bfloat16)
    lo = (table - hi.astype(np.float64)).astype(np.float32).astype(ml_dtypes.bfloat16)
    return hi, lo


def make_tables(depth, width, height):
    lanes = 128
    groups = lanes // depth
    rows = height // groups
    tab = {}
    hi, lo = split_bf16(sine_ext(height))
    tab["eyw"] = np.block([[hi, lo], [hi, np.zeros_like(lo)]])
    hi, lo = split_bf16(sine_ext(width) * np.sqrt(2.0 / depth))
    half = np.block([[hi, hi], [lo, np.zeros_like(lo)]])
    tab["exw"] = np.block([[half, np.zeros_like(half)], [np.zeros_like(half), half]])
    sign = np.where(np.arange(height) % 2 == 1, 1.0, -1.0)
    unit = (np.arange(height) == 0) * 1.0
    wide = np.zeros((height, lanes))
    for g, values in enumerate((1.0 - unit, sign * (1.0 - unit), unit)):
        wide[:, g * depth:(g + 1) * depth] = values[:, None]
    tab["rimw"] = np.concatenate([wide, wide], 0).astype(ml_dtypes.bfloat16)
    wide[0, :depth] = 1.0
    wide[:, 2 * depth:] = 0.0
    tab["colw"] = np.concatenate([wide.T, wide.T], 0).astype(ml_dtypes.bfloat16)
    tab["ey"], tab["ex"] = sine_ext(height).astype(np.float32), sine_ext(width).astype(np.float32)
    z = np.arange(depth)
    cos = np.cos(np.pi * np.outer(z + 0.5, z) / depth) * np.sqrt(2.0 / depth)
    cos[:, 0] = np.sqrt(1.0 / depth)
    tab["cz"] = cos.astype(np.float32)
    czt = np.zeros((lanes, lanes))
    czt[:depth, :depth] = cos.T
    tab["czt"] = czt.astype(np.float32)
    lz = SCREEN + 2.0 - 2.0 * np.cos(np.pi * z / depth)
    a = np.arange(width)
    b = np.arange(height)
    lx = 2.0 - 2.0 * np.cos(np.pi * a / width)
    ly = 2.0 - 2.0 * np.cos(np.pi * b / height)
    sx = np.sqrt(2.0 / width) * np.sin(np.pi * a / width)
    sy = np.sqrt(2.0 / height) * np.sin(np.pi * b / height)
    sga = np.where(a % 2 == 1, 1.0, -1.0)
    sgb = np.where(b % 2 == 1, 1.0, -1.0)
    inside = (a[:, None] > 0) & (b[None, :] > 0)
    inv = np.where(inside[None], 1.0 / (lz[:, None, None] + lx[None, :, None] + ly[None, None, :]), 0.0)
    tab["inv"] = inv.astype(np.float32)
    tab["lxy"] = np.where(inside, lx[:, None] + ly[None, :], 1e30).astype(np.float32)

    def to_rows(kb):
        return kb.T.reshape(groups, rows, depth).transpose(1, 0, 2).reshape(rows, lanes)

    def to_cols(ka):
        return np.tile(ka.T, (1, groups))

    inv2 = inv.transpose(2, 1, 0).reshape(groups, rows, width, depth)
    tab["inv2"] = inv2.transpose(1, 2, 0, 3).reshape(rows, width, lanes).astype(np.float32)
    ones = np.ones((depth, 1))
    odd_a, odd_b = sga > 0, sgb > 0
    sx2, sy2 = (sx**2)[None, :, None] * inv, (sy**2)[None, None, :] * inv
    tab["rowt"] = np.stack([
        to_rows(ones * sy),
        to_rows(ones * (sy * sgb)),
        to_rows(sx2[:, odd_a].sum(1)),
        to_rows(sx2[:, ~odd_a].sum(1)),
        to_rows((lz[:, None] + 2.0 + ly) * (b > 0)),
    ]).astype(np.float32)
    tab["colt"] = np.stack([
        to_cols(ones * sx),
        to_cols(ones * (sx * sga)),
        to_cols(sy2[:, :, odd_b].sum(2)),
        to_cols(sy2[:, :, ~odd_b].sum(2)),
        to_cols((lz[:, None] + 2.0 + lx) * (a > 0)),
    ]).astype(np.float32)
    tab["crnt"] = np.tile(np.tile(lz + 4.0, groups)[None], (8, 1)).astype(np.float32)
    line = np.where(b > 0, sy, 1.0)[None]
    tab["line"] = np.tile(line, (8, 1)).astype(np.float32)
    tab["sx0"] = np.tile(sx[:, None], (1, height)).astype(np.float32)
    return tab


def cosine_two(xs):
    n = len(xs)
    if n == 1:
        return list(xs)
    half = n // 2
    out = [None] * n
    out[0::2] = cosine_two([xs[j] + xs[n - 1 - j] for j in range(half)])
    out[1::2] = cosine_four([xs[j] - xs[n - 1 - j] for j in range(half)])
    return out


def cosine_three(ys):
    n = len(ys)
    if n == 1:
        return list(ys)
    half = n // 2
    even, odd = cosine_three(ys[0::2]), cosine_four(ys[1::2])
    return [even[j] + odd[j] for j in range(half)] + [even[j] - odd[j] for j in reversed(range(half))]


def cosine_four(xs):
    n = len(xs)
    if n == 1:
        return [xs[0] * float(np.cos(np.pi / 4))]
    half = n // 2
    plus, minus = [], []
    for j in range(half):
        c, s = (float(f(np.pi * (2 * j + 1) / (4 * n))) for f in (np.cos, np.sin))
        x, y = xs[j], xs[n - 1 - j]
        plus.append(x * c + y * s)
        minus.append(x * s - y * c if j % 2 == 0 else y * c - x * s)
    c, s = cosine_two(plus), cosine_two(minus)[::-1]
    out = [None] * n
    out[0], out[n - 1] = c[0], s[half - 1]
    for k in range(1, half):
        out[2 * k] = c[k] - s[k - 1]
        out[2 * k - 1] = c[k] + s[k - 1]
    return out


ROOT_HALF = float(np.sqrt(0.5))


def halves(x):
    hi = x.astype(BF16)
    return hi, (x - hi.astype(F32)).astype(BF16)


def times_sy(x, eyw):
    hi, lo = halves(x)
    n = x.shape[1]
    out = jnp.dot(jnp.concatenate([hi, lo], 1), eyw, preferred_element_type=F32)
    return out[:, :n] + out[:, n:]


def sx_times(exw, xs):
    n = xs[0].shape[0]
    rhs = []
    for x in (jnp.concatenate(xs[:2], 1), jnp.concatenate(xs[2:], 1)):
        rhs += list(halves(x))
    out = jnp.dot(exw, jnp.concatenate(rhs, 0), preferred_element_type=F32)
    width = xs[0].shape[1]
    res = []
    for pair in range(2):
        both = out[2 * pair * n:(2 * pair + 1) * n] + out[(2 * pair + 1) * n:(2 * pair + 2) * n]
        res += [both[:, :width], both[:, width:]]
    return res


def lane_id(shape):
    return lax.broadcasted_iota(jnp.int32, shape, 1)


def by_group(pieces, depth):
    group = lane_id(pieces[0].shape) // depth
    out = pieces[0]
    for h in range(1, len(pieces)):
        out = jnp.where(group == h, pieces[h], out)
    return out


def spread(x, depth):
    width = x.shape[1] // 2
    while width >= depth:
        x = x + pltpu.roll(x, width, 1)
        width //= 2
    return x


def pack(col, depth):
    groups = 128 // depth
    size = col.shape[0] // groups
    return by_group([col[h * size:(h + 1) * size] for h in range(groups)], depth)


def unpack(packed, depth):
    groups = 128 // depth
    group = lane_id(packed.shape) // depth
    return jnp.concatenate(
        [spread(jnp.where(group == h, packed, 0.0), depth) for h in range(groups)], 0
    )


def copies_t(kb):
    groups = 128 // kb.shape[0]
    return jnp.concatenate([kb] * groups, 0).T


def rows_from(kbt, depth):
    groups = 128 // depth
    size = kbt.shape[0] // groups
    return by_group([kbt[h * size:(h + 1) * size] for h in range(groups)], depth)


def rows_back(row, depth):
    groups = 128 // depth
    parts = [row] + [pltpu.roll(row, 128 - h * depth, 1) for h in range(1, groups)]
    return jnp.concatenate(parts, 0).T[:depth]


def total(x):
    return jnp.sum(x, 0, keepdims=True)


def sub_sums(ref):
    plus = minus = None
    for s in range(8):
        part = ref[:, s, :]
        if s % 2 == 1:
            plus = part if plus is None else plus + part
        else:
            minus = part if minus is None else minus + part
    return plus + minus, plus - minus


def with_tail(body, tails, size=8):
    width = body.shape[1]
    rows = list(tails)
    if len(rows) < size:
        rows.append(jnp.zeros((size - len(rows), width), F32))
    return jnp.concatenate([body, jnp.concatenate(rows, 0)], 0)


def front_kernel(charge_h, surf_h, eyw_h, exw_h, lxy_h, sx0_h, rimw_h, line_h, base, *rest):
    msgs = rest[:4]
    charge, surf, eyw, exw, lxy, sx0, rimw, line, work, inv, rims, part, first, sems = rest[4:]
    depth, width, height = charge.shape
    tiles = width // 8
    pairs = [(lxy_h, lxy), (surf_h, surf)]
    pairs += [(charge_h.at[:, 8 * i:8 * i + 8, :], charge.at[:, 8 * i:8 * i + 8, :]) for i in range(tiles)]
    pairs += [(eyw_h, eyw), (exw_h, exw), (sx0_h, sx0), (rimw_h, rimw), (line_h, line)]
    copies = [pltpu.make_async_copy(src, dst, sems.at[i]) for i, (src, dst) in enumerate(pairs)]
    for copy in copies:
        copy.start()
    copies[0].wait()
    for k in range(depth):
        inv[k] = 1.0 / (lxy[...] + float(SCREEN + 2.0 - 2.0 * np.cos(np.pi * k / depth)))
    copies[1].wait()

    for i in range(tiles):
        copies[2 + i].wait()
        at = slice(8 * i, 8 * i + 8)
        xs = [charge[z, at, :] for z in range(depth)]
        xs[0] = xs[0] + surf[0, at, :]
        xs[-1] = xs[-1] + surf[1, at, :]
        for k, value in enumerate(cosine_two(xs)):
            work[k, at, :] = value * ROOT_HALF if k == 0 else value
    for copy in copies[2 + tiles:]:
        copy.wait()
    for c in range(0, depth, 4):
        block = work[c:c + 4].reshape(4 * width, height)
        work[c:c + 4] = times_sy(block, eyw[...]).reshape(4, width, height)
    lane = lane_id((width, 128))
    for c in range(0, depth, 4):
        specs = sx_times(exw[...], [work[k] for k in range(c, c + 4)])
        for k, spec in zip(range(c, c + 4), specs):
            inner = spec * inv[k]
            base[k] = inner
            first[k] = spec[0:8]
            part[k] = jnp.sum((inner * sx0[...]).reshape(width // 8, 8, height), 0)
            hi, lo = halves(jnp.where(lane == 0, spec, inner * line[0:1, :]))
            rims[k * width:(k + 1) * width, :] = jnp.concatenate([hi, lo], 1)
    step = 8
    found = jnp.zeros((width, 128), F32)
    for c in range(0, depth, step):
        out = jnp.dot(rims[c * width:(c + step) * width, :], rimw[...], preferred_element_type=F32)
        for k in range(c, c + step):
            one = out[(k - c) * width:(k - c + 1) * width]
            found = jnp.where(lane % depth == k, one, found)
    near, far, own = (spread(jnp.where(lane // depth == g, found, 0.0), depth) for g in range(3))
    row_near, row_far = sub_sums(part)
    own_t = copies_t(first[:, 0, :])
    corner = own_t[0:1]
    row = rows_from(own_t + copies_t(row_near), depth)
    at_zero = (lax.broadcasted_iota(jnp.int32, row.shape, 0) == 0) & (lane_id(row.shape) < depth)
    row = jnp.where(at_zero, 0.0, row)
    col = jnp.where(lax.broadcasted_iota(jnp.int32, own.shape, 0) == 0, 0.0, own + near)
    px = with_tail(row, [corner])
    nx = with_tail(rows_from(copies_t(row_far), depth), [])
    py = with_tail(pack(col, depth), [corner])
    ny = with_tail(pack(far, depth), [])
    for ref, value in zip(msgs, swapped("gx", nx, px) + swapped("gy", ny, py)):
        ref[...] = value


def swapped(axis, after, before):
    even = lax.axis_index(axis) % 2 == 0
    return jnp.where(even, before, after), jnp.where(even, after, before)


def assemble(depth, own, got):
    (nx, px), (ny, py) = swapped("gx", *own[:2]), swapped("gy", *own[2:])
    (from_nx, from_px), (from_ny, from_py) = swapped("gx", *got[:2]), swapped("gy", *got[2:])
    rows, cols = px.shape[0] - 8, py.shape[0] - 8
    row = px[:rows] + from_px[:rows]
    row_n = from_nx[:rows] + nx[:rows]
    col = unpack(py[:cols] + from_py[:cols], depth)
    col_n = unpack(from_ny[:cols] + ny[:cols], depth)
    c00 = px[rows:rows + 1] + from_px[rows:rows + 1] + from_py[cols:cols + 1]
    cx0 = from_nx[rows:rows + 1] + nx[rows:rows + 1] + from_py[cols + 1:cols + 2]
    c0y = from_ny[cols:cols + 1] + ny[cols:cols + 1] + from_px[rows + 1:rows + 2]
    return row, row_n, col, col_n, c00, cx0, c0y


def sizes(rows, cols):
    offs = np.cumsum([0, rows, rows, cols, cols])
    return [slice(int(offs[i]), int(offs[i + 1])) for i in range(4)] + [int(offs[4])]


def unpacked_state(state, rows, cols):
    s = sizes(rows, cols)
    at = s[4]
    return tuple(state[s[i], :] for i in range(4)) + tuple(state[at + i:at + i + 1, :] for i in range(3))


def schur_kernel(depth, want_moments, *refs):
    own, got = [r[...] for r in refs[0:4]], [r[...] for r in refs[4:8]]
    inv2, rowt, colt, crnt = refs[8:12]
    rest = list(refs[12:])
    before = rest.pop(0) if want_moments else None
    state, *outs = rest[:5]
    part, odd_rows, even_rows = rest[-3:]
    row, row_n, col, col_n, c00, cx0, c0y = assemble(depth, own, got)
    rows, cols = row.shape[0], col.shape[0]
    s = sizes(rows, cols)
    for i, piece in enumerate((row, row_n, col, col_n)):
        state[s[i], :] = piece
    state[s[4]:s[4] + 8, :] = jnp.concatenate([c00, cx0, c0y, jnp.zeros((5, 128), F32)], 0)
    sy, sys, g_odd, g_even, d_row = (rowt[i] for i in range(5))
    sx, sxs, h_odd, h_even, d_col = (colt[i] for i in range(5))
    row_p, row_m, col_p, col_m = row + row_n, row - row_n, col + col_n, col - col_n
    odd_rows[...] = row_p * sy
    even_rows[...] = row_m * sy
    col_w = (col_m * sx, col_p * sx)
    odd = lax.broadcasted_iota(jnp.int32, (8, 128), 0) % 2 == 1
    acc = [None, None]
    for r in range(rows):
        table = inv2[r].reshape(cols // 8, 8, 128)
        part[r] = jnp.sum(table * col_w[r % 2].reshape(cols // 8, 8, 128), 0)
        pick = jnp.where(odd, odd_rows[r:r + 1, :], even_rows[r:r + 1, :])
        term = table * pick[None]
        acc[r % 2] = term if acc[r % 2] is None else acc[r % 2] + term
    row_s, row_d = sub_sums(part)
    acc_s = spread((acc[1] + acc[0]).reshape(cols, 128), depth)
    acc_d = spread((acc[1] - acc[0]).reshape(cols, 128), depth)
    diag_o, diag_e = g_odd * row_p, g_even * row_m
    x_near = sy * row_s + (diag_o + diag_e)
    x_far = sy * row_d + (diag_o - diag_e)
    diag_o, diag_e = h_odd * col_p, h_even * col_m
    y_near = sx * acc_s + (diag_o + diag_e)
    y_far = sx * acc_d + (diag_o - diag_e)
    row_img = d_row * row - sy * c00 - sys * c0y - x_near
    col_img = d_col * col - sx * c00 - sxs * cx0 - y_near
    row_end0 = spread(total(sy * row), depth)
    row_end1 = spread(total(sys * row), depth)
    row_end1n = spread(total(sys * row_n), depth)
    col_end0 = total(sx * col)
    col_end1 = total(sxs * col)
    col_end1n = total(sxs * col_n)
    q00 = crnt[0:1, :] * c00 - row_end0 - col_end0
    px = with_tail(row_img, [q00])
    nx = with_tail(-x_far, [-col_end1, -col_end1n])
    py = with_tail(pack(col_img, depth), [q00])
    ny = with_tail(pack(-y_far, depth), [-row_end1, -row_end1n])
    if want_moments:
        row0, _, col0, _, c000, _, _ = unpacked_state(before, rows, cols)
        share = depth / 128.0

        def dot(x, y):
            return total(x[0] * y[0]) + share * (total(x[1] * y[1]) + x[2] * y[2])

        v0, v1 = (row0, col0, c000), (row, col, c00)
        m3 = total(row * row_img - row_n * x_far) + share * (
            total(col * col_img - col_n * y_far) + c00 * q00 - c0y * row_end1 - cx0 * col_end1
        )
        moments = [dot(v0, v0), dot(v0, v1), dot(v1, v1), m3]
        px = with_tail(row_img, [q00, q00, q00, q00] + moments)
        nx = with_tail(-x_far, [-col_end1, -col_end1n, c00, c00] + moments)
    sides = (ny, py) if want_moments else swapped("gy", ny, py)
    for ref, value in zip(outs, swapped("gx", nx, px) + sides):
        ref[...] = value


def cells_from(out, work, spectrum, exw, eyw):
    depth, width, height = work.shape
    for c in range(0, depth, 4):
        for k, cells in zip(range(c, c + 4), sx_times(exw, [spectrum(k) for k in range(c, c + 4)])):
            work[k] = cells
    step = 4
    for c in range(0, depth, step):
        block = work[c:c + step].reshape(step * width, height)
        work[c:c + step] = times_sy(block, eyw).reshape(step, width, height)
    for i in range(width // 8):
        at = slice(8 * i, 8 * i + 8)
        ys = [work[k, at, :] for k in range(depth)]
        for z, value in enumerate(cosine_three([ys[0] * ROOT_HALF] + ys[1:])):
            out[z, at, :] = value


def base_kernel(base, eyw, exw, out, work):
    cells_from(out, work, lambda k: base[k], exw[...], eyw[...])


def extend_kernel(state, eyw, exw, inv, sx0, colw, line, out, work):
    depth, width, height = work.shape
    rows = height * depth // 128
    row, row_n, col, col_n, c00 = unpacked_state(state, rows, width)[:5]
    at_zero = (lax.broadcasted_iota(jnp.int32, row.shape, 0) == 0) & (lane_id(row.shape) < depth)
    row_p = rows_back(row + row_n, depth)
    row_m = rows_back(row - row_n, depth)
    row_full = rows_back(jnp.where(at_zero, c00, row), depth)
    odd = lax.broadcasted_iota(jnp.int32, (8, height), 0) % 2 == 1
    top = lax.broadcasted_iota(jnp.int32, (8, height), 0) == 0
    lane0 = lane_id((width, height)) == 0
    lane = lane_id((width, 256)) % depth
    hi, lo = halves(by_group([col, col_n] + [jnp.zeros_like(col)] * (128 // depth - 2), depth))
    both = jnp.concatenate([hi, lo], 1)
    step = 8
    for c in range(0, depth, step):
        rim = jnp.concatenate([jnp.where(lane == k, both, jnp.zeros_like(both)) for k in range(c, c + step)], 0)
        rim = jnp.dot(rim, colw[...], preferred_element_type=F32)
        for k in range(c, c + step):
            side = rim[(k - c) * width:(k - c + 1) * width]
            pick = jnp.where(odd, row_p[k:k + 1], row_m[k:k + 1])
            pick = jnp.broadcast_to(pick[None], (width // 8, 8, height)).reshape(width, height)
            value = jnp.where(lane0, 1.0, inv[k]) * (sx0[...] * pick + side * line[0:1, :])
            work[k] = value
            work[k, 0:8, :] = jnp.where(top, row_full[k:k + 1], value[0:8])
    cells_from(out, work, lambda k: work[k], exw[...], eyw[...])


def rims_kernel(depth, s0, s1, bx, ax, py, got_bx, got_ax, from_py, ey, ex, cz, czt, out_rows, out_cols):
    packed = py.shape[0] - 8
    rows = bx.shape[0] - 8
    width = packed * 128 // depth
    _, px = swapped("gx", bx[...], ax[...])
    _, from_px = swapped("gx", got_bx[...], got_ax[...])
    v0 = unpacked_state(s0, rows, width)
    v1 = unpacked_state(s1, rows, width)
    v2 = (
        px[:rows, :] + from_px[:rows, :], None,
        unpack(py[:packed, :] + from_py[:packed, :], depth), None,
        px[rows:rows + 1, :] + from_px[rows:rows + 1, :] + from_py[packed:packed + 1, :],
    )
    at_zero = (lax.broadcasted_iota(jnp.int32, (rows, 128), 0) == 0) & (lane_id((rows, 128)) < depth)
    lines = [rows_back(jnp.where(at_zero, v[4], v[0]), depth) for v in (v0, v1, v2)]
    high = lax.Precision.HIGHEST
    lines = jnp.dot(jnp.concatenate(lines, 0), ey[...], precision=high, preferred_element_type=F32)
    lines = jnp.concatenate([lines[i * depth:(i + 1) * depth] for i in range(3)], 1)
    lines = jnp.dot(cz[...], lines, precision=high, preferred_element_type=F32)
    for i in range(3):
        out_rows[i] = lines[:, i * 128:(i + 1) * 128]
    sides = jnp.concatenate([v[2] for v in (v0, v1, v2)], 1)
    sides = jnp.dot(ex[...], sides, precision=high, preferred_element_type=F32)
    sides = jnp.concatenate([sides[:, i * 128:(i + 1) * 128] for i in range(3)], 0)
    sides = jnp.dot(sides, czt[...], precision=high, preferred_element_type=F32)
    for i in range(3):
        out_cols[i] = sides[i * width:(i + 1) * width]


def final_kernel(n_moments, *refs):
    cells_b, cells_0, cells_1, in_rows, in_cols = refs[:5]
    moms = refs[5:5 + n_moments]
    potential_h, residual_h, potential, residual, sems = refs[5 + n_moments:]
    depth, width, height = cells_b.shape
    m = moms[0][...]
    for other in moms[1:]:
        m = m + other[...]
    m = jnp.broadcast_to(jnp.sum(m, 1, keepdims=True), (8, 128))
    m0 = m[4:5]
    n1, n2, n3 = m[5:6] / m0, m[6:7] / m0, m[7:8] / m0
    det = n1 * n3 - n2 * n2
    fine = det > 1e-6 * (n1 * n3)
    safe = jnp.where(fine, det, 1.0)
    c0 = jnp.where(fine, (n3 - n1 * n2) / safe, 1.0 / n1)
    c1 = jnp.where(fine, (n1 * n1 - n2) / safe, 0.0)
    rim_row = in_rows[0] - c0 * in_rows[1] - c1 * in_rows[2]
    rim_col = in_cols[0] - c0 * in_cols[1] - c1 * in_cols[2]
    top = lax.broadcasted_iota(jnp.int32, (8, height), 0) == 0
    lane0 = lane_id((width, height)) == 0
    step = depth // 4
    copies = []

    def send(src, dst, c):
        at = slice(c, c + step)
        copies.append(pltpu.make_async_copy(src.at[at], dst.at[at], sems.at[len(copies)]))
        copies[-1].start()

    for c in range(0, depth, step):
        for z in range(c, c + step):
            potential[z] = cells_b[z] + c0 * cells_0[z] + c1 * cells_1[z]
        send(potential, potential_h, c)
    for c in range(0, depth, step):
        for z in range(c, c + step):
            flat = jnp.where(lane0, rim_col[:, z:z + 1], 0.0)
            residual[z, 8:, :] = flat[8:]
            residual[z, 0:8, :] = jnp.where(top, rim_row[z:z + 1], flat[0:8])
        send(residual, residual_h, c)
    for copy in copies:
        copy.wait()


def shifted(value, axis, by):
    n = lax.axis_size(axis)
    return lax.ppermute(value, axis, [(i, (i + by) % n) for i in range(n)])


def swap(value, axis, odd):
    n = lax.axis_size(axis)
    pairs = [(i, (i + 1) % n) for i in range(odd, n, 2)]
    return lax.ppermute(value, axis, pairs + [(j, i) for i, j in pairs])


def exchange(bx, ax, by, ay):
    return swap(bx, "gx", 1), swap(ax, "gx", 0), swap(by, "gy", 1), swap(ay, "gy", 0)


def pieces_over(value, axis):
    n, stride = lax.axis_size(axis), 1
    while True:
        radix = 4 if n % 4 == 0 else 2 if n % 2 == 0 else n
        parts = [value] + [shifted(value, axis, stride * j) for j in range(1, radix)]
        n, stride = n // radix, stride * radix
        if n == 1:
            return parts
        value = sum(parts[1:], parts[0])


def reduced_x(bx, ax):
    got_bx, got_ax = swap(bx, "gx", 1), swap(ax, "gx", 0)
    if lax.axis_size("gx") == 4:
        parts = [bx, got_ax, shifted(ax, "gx", 2), got_bx]
        parts = [part[-8:] for part in parts]
    else:
        parts = pieces_over(bx[-8:], "gx")
    return parts, got_bx, got_ax


def reduced_y(value):
    if lax.axis_size("gy") == 4:
        return [value, swap(value, "gy", 0), shifted(value, "gy", 2), swap(value, "gy", 1)]
    return pieces_over(value, "gy")


def call(kernel, outs, scratch, in_specs=None, out_specs=None):
    specs = {}
    if in_specs is not None:
        specs["in_specs"] = in_specs
    if out_specs is not None:
        specs["out_specs"] = out_specs
    return pl.pallas_call(
        kernel,
        out_shape=[jax.ShapeDtypeStruct(shape, F32) for shape in outs],
        scratch_shapes=[pltpu.VMEM(s, F32) if isinstance(s, tuple) else s for s in scratch],
        compiler_params=pltpu.CompilerParams(vmem_limit_bytes=48 * 1024 * 1024),
        **specs,
    )


def on_device(charge, surface_charge):
    depth, width, height = charge.shape
    tab = {name: jnp.asarray(value) for name, value in make_tables(depth, width, height).items()}
    rows, packed = height * depth // 128, width * depth // 128
    msgs = [(rows + 8, 128)] * 2 + [(packed + 8, 128)] * 2
    state = (2 * rows + 2 * width + 8, 128)
    block = (depth, width, height)
    anywhere = pl.BlockSpec(memory_space=pltpu.HBM)
    whole = pl.BlockSpec(memory_space=pltpu.VMEM)
    fronts = (charge, surface_charge) + tuple(tab[n] for n in ("eyw", "exw", "lxy", "sx0", "rimw", "line"))
    landing = [pltpu.VMEM(x.shape, x.dtype) for x in fronts]
    fronts = [pltpu.with_memory_space_constraint(x, pltpu.HBM) for x in fronts]
    base, *own = call(
        front_kernel, [block] + msgs,
        landing + [block, block, pltpu.VMEM((depth * width, 2 * height), BF16), (depth, 8, height), (depth, 8, height),
                   pltpu.SemaphoreType.DMA((7 + width // 8,))],
        in_specs=[anywhere] * 8,
    )(*fronts)
    got = exchange(*own)
    cells_b = call(base_kernel, [block], [block])(base, tab["eyw"], tab["exw"])[0]
    *got, cells_b = lax.optimization_barrier((*got, cells_b))
    tables = (tab["inv2"], tab["rowt"], tab["colt"], tab["crnt"])
    scratch = [(rows, 8, 128), (rows, 128), (rows, 128)]
    s0, *own = call(lambda *r: schur_kernel(depth, False, *r), [state] + msgs, scratch)(*own, *got, *tables)
    got = exchange(*own)
    extend = call(extend_kernel, [block], [block])
    backs = tuple(tab[n] for n in ("eyw", "exw", "inv", "sx0", "colw", "line"))
    cells_0 = extend(s0, *backs)[0]
    *got, cells_0 = lax.optimization_barrier((*got, cells_0))
    s1, *own = call(lambda *r: schur_kernel(depth, True, *r), [state] + msgs, scratch)(*own, *got, *tables, s0)
    parts, got_bx, got_ax = reduced_x(*own[:2])
    from_py = shifted(own[2], "gy", 1)
    cells_1 = extend(s1, *backs)[0]
    *parts, cells_1 = lax.optimization_barrier((*parts, cells_1))
    parts = reduced_y(sum(parts[1:], parts[0]))
    rim = call(lambda *r: rims_kernel(depth, *r), [(3, depth, height), (3, width, 128)], [])(
        s0, s1, own[0], own[1], own[3], got_bx, got_ax, from_py, tab["ey"], tab["ex"], tab["cz"], tab["czt"]
    )
    return call(
        lambda *r: final_kernel(len(parts), *r), [block, block], [block, block, pltpu.SemaphoreType.DMA((8,))],
        in_specs=[whole] * (5 + len(parts)), out_specs=[anywhere, anywhere],
    )(cells_b, cells_0, cells_1, *rim, *parts)


def solution(mesh):
    spec = P(None, ("slab", "gx"), "gy")
    return jax.shard_map(
        on_device, mesh=mesh, in_specs=(spec, spec), out_specs=(spec, spec), check_vma=False
    )
```

```python
import numpy as np
import jax
import jax.numpy as jnp
from jax import lax
from jax.experimental import pallas as pl
from jax.experimental.pallas import tpu as pltpu
from jax.sharding import PartitionSpec as P
import ml_dtypes

SCREEN = 0.02
BF16 = jnp.bfloat16
F32 = jnp.float32


def sine_ext(n):
    i = np.arange(n)
    table = np.sqrt(2.0 / n) * np.sin(np.pi * np.outer(i, i) / n)
    table[0, 0] = 1.0
    return table


def split_bf16(table):
    hi = table.astype(np.float32).astype(ml_dtypes.bfloat16)
    lo = (table - hi.astype(np.float64)).astype(np.float32).astype(ml_dtypes.bfloat16)
    return hi, lo


def make_tables(depth, width, height):
    lanes = 128
    groups = lanes // depth
    rows = height // groups
    tab = {}
    hi, lo = split_bf16(sine_ext(height))
    tab["eyw"] = np.block([[hi, lo], [hi, np.zeros_like(lo)]])
    hi, lo = split_bf16(sine_ext(width) * np.sqrt(2.0 / depth))
    half = np.block([[hi, hi], [lo, np.zeros_like(lo)]])
    tab["exw"] = np.block([[half, np.zeros_like(half)], [np.zeros_like(half), half]])
    sign = np.where(np.arange(height) % 2 == 1, 1.0, -1.0)
    unit = (np.arange(height) == 0) * 1.0
    wide = np.zeros((height, lanes))
    for g, values in enumerate((1.0 - unit, sign * (1.0 - unit), unit)):
        wide[:, g * depth:(g + 1) * depth] = values[:, None]
    tab["rimw"] = np.concatenate([wide, wide], 0).astype(ml_dtypes.bfloat16)
    wide[0, :depth] = 1.0
    wide[:, 2 * depth:] = 0.0
    tab["colw"] = np.concatenate([wide.T, wide.T], 0).astype(ml_dtypes.bfloat16)
    tab["ey"], tab["ex"] = sine_ext(height).astype(np.float32), sine_ext(width).astype(np.float32)
    z = np.arange(depth)
    cos = np.cos(np.pi * np.outer(z + 0.5, z) / depth) * np.sqrt(2.0 / depth)
    cos[:, 0] = np.sqrt(1.0 / depth)
    tab["cz"] = cos.astype(np.float32)
    czt = np.zeros((lanes, lanes))
    czt[:depth, :depth] = cos.T
    tab["czt"] = czt.astype(np.float32)
    lz = SCREEN + 2.0 - 2.0 * np.cos(np.pi * z / depth)
    a = np.arange(width)
    b = np.arange(height)
    lx = 2.0 - 2.0 * np.cos(np.pi * a / width)
    ly = 2.0 - 2.0 * np.cos(np.pi * b / height)
    sx = np.sqrt(2.0 / width) * np.sin(np.pi * a / width)
    sy = np.sqrt(2.0 / height) * np.sin(np.pi * b / height)
    sga = np.where(a % 2 == 1, 1.0, -1.0)
    sgb = np.where(b % 2 == 1, 1.0, -1.0)
    inside = (a[:, None] > 0) & (b[None, :] > 0)
    inv = np.where(inside[None], 1.0 / (lz[:, None, None] + lx[None, :, None] + ly[None, None, :]), 0.0)
    tab["lxy"] = np.where(inside, lx[:, None] + ly[None, :], 1e30).astype(np.float32)

    def to_rows(kb):
        return kb.T.reshape(groups, rows, depth).transpose(1, 0, 2).reshape(rows, lanes)

    def to_cols(ka):
        return np.tile(ka.T, (1, groups))

    tab["lxz"] = to_cols(np.where(a > 0, lz[:, None] + lx, 1e30)).astype(np.float32)
    tab["ly"] = to_rows(np.ones((depth, 1)) * np.where(b > 0, ly, 1e30)).astype(np.float32)
    ones = np.ones((depth, 1))
    odd_a, odd_b = sga > 0, sgb > 0
    sx2, sy2 = (sx**2)[None, :, None] * inv, (sy**2)[None, None, :] * inv
    tab["rowt"] = np.stack([
        to_rows(ones * sy),
        to_rows(ones * (sy * sgb)),
        to_rows(sx2[:, odd_a].sum(1)),
        to_rows(sx2[:, ~odd_a].sum(1)),
        to_rows((lz[:, None] + 2.0 + ly) * (b > 0)),
    ]).astype(np.float32)
    tab["colt"] = np.stack([
        to_cols(ones * sx),
        to_cols(ones * (sx * sga)),
        to_cols(sy2[:, :, odd_b].sum(2)),
        to_cols(sy2[:, :, ~odd_b].sum(2)),
        to_cols((lz[:, None] + 2.0 + lx) * (a > 0)),
    ]).astype(np.float32)
    tab["crnt"] = np.tile(np.tile(lz + 4.0, groups)[None], (8, 1)).astype(np.float32)
    line = np.where(b > 0, sy, 1.0)[None]
    tab["line"] = np.tile(line, (8, 1)).astype(np.float32)
    tab["sx0"] = np.tile(sx[:, None], (1, height)).astype(np.float32)
    return tab


def cosine_two(xs):
    n = len(xs)
    if n == 1:
        return list(xs)
    half = n // 2
    out = [None] * n
    out[0::2] = cosine_two([xs[j] + xs[n - 1 - j] for j in range(half)])
    out[1::2] = cosine_four([xs[j] - xs[n - 1 - j] for j in range(half)])
    return out


def cosine_three(ys):
    n = len(ys)
    if n == 1:
        return list(ys)
    half = n // 2
    even, odd = cosine_three(ys[0::2]), cosine_four(ys[1::2])
    return [even[j] + odd[j] for j in range(half)] + [even[j] - odd[j] for j in reversed(range(half))]


def cosine_four(xs):
    n = len(xs)
    if n == 1:
        return [xs[0] * float(np.cos(np.pi / 4))]
    half = n // 2
    plus, minus = [], []
    for j in range(half):
        c, s = (float(f(np.pi * (2 * j + 1) / (4 * n))) for f in (np.cos, np.sin))
        x, y = xs[j], xs[n - 1 - j]
        plus.append(x * c + y * s)
        minus.append(x * s - y * c if j % 2 == 0 else y * c - x * s)
    c, s = cosine_two(plus), cosine_two(minus)[::-1]
    out = [None] * n
    out[0], out[n - 1] = c[0], s[half - 1]
    for k in range(1, half):
        out[2 * k] = c[k] - s[k - 1]
        out[2 * k - 1] = c[k] + s[k - 1]
    return out


ROOT_HALF = float(np.sqrt(0.5))


def halves(x):
    hi = x.astype(BF16)
    return hi, (x - hi.astype(F32)).astype(BF16)


def times_sy(x, eyw):
    hi, lo = halves(x)
    n = x.shape[1]
    out = jnp.dot(jnp.concatenate([hi, lo], 1), eyw, preferred_element_type=F32)
    return out[:, :n] + out[:, n:]


def sx_times(exw, xs):
    n = xs[0].shape[0]
    rhs = []
    for x in (jnp.concatenate(xs[:2], 1), jnp.concatenate(xs[2:], 1)):
        rhs += list(halves(x))
    out = jnp.dot(exw, jnp.concatenate(rhs, 0), preferred_element_type=F32)
    width = xs[0].shape[1]
    res = []
    for pair in range(2):
        both = out[2 * pair * n:(2 * pair + 1) * n] + out[(2 * pair + 1) * n:(2 * pair + 2) * n]
        res += [both[:, :width], both[:, width:]]
    return res


def lane_id(shape):
    return lax.broadcasted_iota(jnp.int32, shape, 1)


def by_group(pieces, depth):
    group = lane_id(pieces[0].shape) // depth
    out = pieces[0]
    for h in range(1, len(pieces)):
        out = jnp.where(group == h, pieces[h], out)
    return out


def spread(x, depth):
    width = x.shape[1] // 2
    while width >= depth:
        x = x + pltpu.roll(x, width, 1)
        width //= 2
    return x


def pack(col, depth):
    groups = 128 // depth
    size = col.shape[0] // groups
    return by_group([col[h * size:(h + 1) * size] for h in range(groups)], depth)


def unpack(packed, depth):
    groups = 128 // depth
    group = lane_id(packed.shape) // depth
    return jnp.concatenate(
        [spread(jnp.where(group == h, packed, 0.0), depth) for h in range(groups)], 0
    )


def copies_t(kb):
    groups = 128 // kb.shape[0]
    return jnp.concatenate([kb] * groups, 0).T


def rows_from(kbt, depth):
    groups = 128 // depth
    size = kbt.shape[0] // groups
    return by_group([kbt[h * size:(h + 1) * size] for h in range(groups)], depth)


def rows_back(row, depth):
    groups = 128 // depth
    parts = [row] + [pltpu.roll(row, 128 - h * depth, 1) for h in range(1, groups)]
    return jnp.concatenate(parts, 0).T[:depth]


def total(x):
    return jnp.sum(x, 0, keepdims=True)


def sub_sums(ref):
    plus = minus = None
    for s in range(8):
        part = ref[:, s, :]
        if s % 2 == 1:
            plus = part if plus is None else plus + part
        else:
            minus = part if minus is None else minus + part
    return plus + minus, plus - minus


def with_tail(body, tails, size=8):
    width = body.shape[1]
    rows = list(tails)
    if len(rows) < size:
        rows.append(jnp.zeros((size - len(rows), width), F32))
    return jnp.concatenate([body, jnp.concatenate(rows, 0)], 0)


def front_kernel(charge_h, surf_h, eyw_h, exw_h, lxy_h, sx0_h, line_h, base, inv, rims, *rest):
    msgs = rest[:2]
    charge, surf, eyw, exw, lxy, sx0, line, work, part, first, sems = rest[2:]
    depth, width, height = charge.shape
    tiles = width // 8
    pairs = [(lxy_h, lxy), (surf_h, surf)]
    pairs += [(charge_h.at[:, 8 * i:8 * i + 8, :], charge.at[:, 8 * i:8 * i + 8, :]) for i in range(tiles)]
    pairs += [(eyw_h, eyw), (exw_h, exw), (sx0_h, sx0), (line_h, line)]
    copies = [pltpu.make_async_copy(src, dst, sems.at[i]) for i, (src, dst) in enumerate(pairs)]
    for copy in copies:
        copy.start()
    copies[0].wait()
    for k in range(depth):
        inv[k] = 1.0 / (lxy[...] + float(SCREEN + 2.0 - 2.0 * np.cos(np.pi * k / depth)))
    copies[1].wait()

    for i in range(tiles):
        copies[2 + i].wait()
        at = slice(8 * i, 8 * i + 8)
        xs = [charge[z, at, :] for z in range(depth)]
        xs[0] = xs[0] + surf[0, at, :]
        xs[-1] = xs[-1] + surf[1, at, :]
        for k, value in enumerate(cosine_two(xs)):
            work[k, at, :] = value * ROOT_HALF if k == 0 else value
    for copy in copies[2 + tiles:]:
        copy.wait()
    for c in range(0, depth, 4):
        block = work[c:c + 4].reshape(4 * width, height)
        work[c:c + 4] = times_sy(block, eyw[...]).reshape(4, width, height)
    lane = lane_id((width, 128))
    for c in range(0, depth, 4):
        specs = sx_times(exw[...], [work[k] for k in range(c, c + 4)])
        for k, spec in zip(range(c, c + 4), specs):
            inner = spec * inv[k]
            base[k] = inner
            first[k] = spec[0:8]
            part[k] = jnp.sum((inner * sx0[...]).reshape(width // 8, 8, height), 0)
            hi, lo = halves(jnp.where(lane == 0, spec, inner * line[0:1, :]))
            rims[k * width:(k + 1) * width, :] = jnp.concatenate([hi, lo], 1)
    row_near, row_far = sub_sums(part)
    own_t = copies_t(first[:, 0, :])
    corner = own_t[0:1]
    row = rows_from(own_t + copies_t(row_near), depth)
    at_zero = (lax.broadcasted_iota(jnp.int32, row.shape, 0) == 0) & (lane_id(row.shape) < depth)
    row = jnp.where(at_zero, 0.0, row)
    px = with_tail(row, [corner])
    nx = with_tail(rows_from(copies_t(row_far), depth), [])
    for ref, value in zip(msgs, swapped("gx", nx, px)):
        ref[...] = value


def sides_kernel(depth, rims, rimw, bx, ax, by, ay):
    width = rims.shape[0] // depth
    lane = lane_id((width, 128))
    step = 8
    found = jnp.zeros((width, 128), F32)
    for c in range(0, depth, step):
        out = jnp.dot(rims[c * width:(c + step) * width, :], rimw[...], preferred_element_type=F32)
        for k in range(c, c + step):
            one = out[(k - c) * width:(k - c + 1) * width]
            found = jnp.where(lane % depth == k, one, found)
    near, far, own = (spread(jnp.where(lane // depth == g, found, 0.0), depth) for g in range(3))
    _, px = swapped("gx", bx[...], ax[...])
    corner = px[px.shape[0] - 8:px.shape[0] - 7]
    col = jnp.where(lax.broadcasted_iota(jnp.int32, own.shape, 0) == 0, 0.0, own + near)
    py = with_tail(pack(col, depth), [corner])
    ny = with_tail(pack(far, depth), [])
    for ref, value in zip((by, ay), swapped("gy", ny, py)):
        ref[...] = value


def swapped(axis, after, before):
    even = lax.axis_index(axis) % 2 == 0
    return jnp.where(even, before, after), jnp.where(even, after, before)


def assemble(depth, own, got):
    (nx, px), (ny, py) = swapped("gx", *own[:2]), swapped("gy", *own[2:])
    (from_nx, from_px), (from_ny, from_py) = swapped("gx", *got[:2]), swapped("gy", *got[2:])
    rows, cols = px.shape[0] - 8, py.shape[0] - 8
    row = px[:rows] + from_px[:rows]
    row_n = from_nx[:rows] + nx[:rows]
    col = unpack(py[:cols] + from_py[:cols], depth)
    col_n = unpack(from_ny[:cols] + ny[:cols], depth)
    c00 = px[rows:rows + 1] + from_px[rows:rows + 1] + from_py[cols:cols + 1]
    cx0 = from_nx[rows:rows + 1] + nx[rows:rows + 1] + from_py[cols + 1:cols + 2]
    c0y = from_ny[cols:cols + 1] + ny[cols:cols + 1] + from_px[rows + 1:rows + 2]
    return row, row_n, col, col_n, c00, cx0, c0y


def sizes(rows, cols):
    offs = np.cumsum([0, rows, rows, cols, cols])
    return [slice(int(offs[i]), int(offs[i + 1])) for i in range(4)] + [int(offs[4])]


def unpacked_state(state, rows, cols):
    s = sizes(rows, cols)
    at = s[4]
    return tuple(state[s[i], :] for i in range(4)) + tuple(state[at + i:at + i + 1, :] for i in range(3))


def schur_kernel(depth, want_moments, *refs):
    own, got = [r[...] for r in refs[0:4]], [r[...] for r in refs[4:8]]
    inv2, rowt, colt, crnt = refs[8:12]
    rest = list(refs[12:])
    before = rest.pop(0) if want_moments else None
    state, *outs = rest[:5]
    part, odd_rows, even_rows = rest[-3:]
    row, row_n, col, col_n, c00, cx0, c0y = assemble(depth, own, got)
    rows, cols = row.shape[0], col.shape[0]
    s = sizes(rows, cols)
    for i, piece in enumerate((row, row_n, col, col_n)):
        state[s[i], :] = piece
    state[s[4]:s[4] + 8, :] = jnp.concatenate([c00, cx0, c0y, jnp.zeros((5, 128), F32)], 0)
    sy, sys, g_odd, g_even, d_row = (rowt[i] for i in range(5))
    sx, sxs, h_odd, h_even, d_col = (colt[i] for i in range(5))
    row_p, row_m, col_p, col_m = row + row_n, row - row_n, col + col_n, col - col_n
    odd_rows[...] = row_p * sy
    even_rows[...] = row_m * sy
    col_w = (col_m * sx, col_p * sx)
    odd = lax.broadcasted_iota(jnp.int32, (8, 128), 0) % 2 == 1
    acc = [None, None]
    for r in range(rows):
        table = inv2[r].reshape(cols // 8, 8, 128)
        part[r] = jnp.sum(table * col_w[r % 2].reshape(cols // 8, 8, 128), 0)
        pick = jnp.where(odd, odd_rows[r:r + 1, :], even_rows[r:r + 1, :])
        term = table * pick[None]
        acc[r % 2] = term if acc[r % 2] is None else acc[r % 2] + term
    row_s, row_d = sub_sums(part)
    acc_s = spread((acc[1] + acc[0]).reshape(cols, 128), depth)
    acc_d = spread((acc[1] - acc[0]).reshape(cols, 128), depth)
    diag_o, diag_e = g_odd * row_p, g_even * row_m
    x_near = sy * row_s + (diag_o + diag_e)
    x_far = sy * row_d + (diag_o - diag_e)
    diag_o, diag_e = h_odd * col_p, h_even * col_m
    y_near = sx * acc_s + (diag_o + diag_e)
    y_far = sx * acc_d + (diag_o - diag_e)
    row_img = d_row * row - sy * c00 - sys * c0y - x_near
    col_img = d_col * col - sx * c00 - sxs * cx0 - y_near
    row_end0 = spread(total(sy * row), depth)
    row_end1 = spread(total(sys * row), depth)
    row_end1n = spread(total(sys * row_n), depth)
    col_end0 = total(sx * col)
    col_end1 = total(sxs * col)
    col_end1n = total(sxs * col_n)
    q00 = crnt[0:1, :] * c00 - row_end0 - col_end0
    px = with_tail(row_img, [q00])
    nx = with_tail(-x_far, [-col_end1, -col_end1n])
    py = with_tail(pack(col_img, depth), [q00])
    ny = with_tail(pack(-y_far, depth), [-row_end1, -row_end1n])
    if want_moments:
        row0, _, col0, _, c000, _, _ = unpacked_state(before, rows, cols)
        share = depth / 128.0

        def dot(x, y):
            return total(x[0] * y[0]) + share * (total(x[1] * y[1]) + x[2] * y[2])

        v0, v1 = (row0, col0, c000), (row, col, c00)
        m3 = total(row * row_img - row_n * x_far) + share * (
            total(col * col_img - col_n * y_far) + c00 * q00 - c0y * row_end1 - cx0 * col_end1
        )
        moments = [dot(v0, v0), dot(v0, v1), dot(v1, v1), m3]
        px = with_tail(row_img, [q00, q00, q00, q00] + moments)
        nx = with_tail(-x_far, [-col_end1, -col_end1n, c00, c00] + moments)
    sides = (ny, py) if want_moments else swapped("gy", ny, py)
    for ref, value in zip(outs, swapped("gx", nx, px) + sides):
        ref[...] = value


def cells_from(out, work, spectrum, exw, eyw):
    depth, width, height = work.shape
    for c in range(0, depth, 4):
        for k, cells in zip(range(c, c + 4), sx_times(exw, [spectrum(k) for k in range(c, c + 4)])):
            work[k] = cells
    step = 4
    for c in range(0, depth, step):
        block = work[c:c + step].reshape(step * width, height)
        work[c:c + step] = times_sy(block, eyw).reshape(step, width, height)
    for i in range(width // 8):
        at = slice(8 * i, 8 * i + 8)
        ys = [work[k, at, :] for k in range(depth)]
        for z, value in enumerate(cosine_three([ys[0] * ROOT_HALF] + ys[1:])):
            out[z, at, :] = value


def base_kernel(base, eyw, exw, lxz, ly, out, inv2, work):
    for r in range(inv2.shape[0]):
        inv2[r] = 1.0 / (lxz[...] + ly[r:r + 1, :])
    cells_from(out, work, lambda k: base[k], exw[...], eyw[...])


def extend_kernel(state, eyw, exw, inv, sx0, colw, line, out, work):
    depth, width, height = work.shape
    rows = height * depth // 128
    row, row_n, col, col_n, c00 = unpacked_state(state, rows, width)[:5]
    at_zero = (lax.broadcasted_iota(jnp.int32, row.shape, 0) == 0) & (lane_id(row.shape) < depth)
    row_p = rows_back(row + row_n, depth)
    row_m = rows_back(row - row_n, depth)
    row_full = rows_back(jnp.where(at_zero, c00, row), depth)
    odd = lax.broadcasted_iota(jnp.int32, (8, height), 0) % 2 == 1
    top = lax.broadcasted_iota(jnp.int32, (8, height), 0) == 0
    lane0 = lane_id((width, height)) == 0
    lane = lane_id((width, 256)) % depth
    hi, lo = halves(by_group([col, col_n] + [jnp.zeros_like(col)] * (128 // depth - 2), depth))
    both = jnp.concatenate([hi, lo], 1)
    step = 8
    for c in range(0, depth, step):
        rim = jnp.concatenate([jnp.where(lane == k, both, jnp.zeros_like(both)) for k in range(c, c + step)], 0)
        rim = jnp.dot(rim, colw[...], preferred_element_type=F32)
        for k in range(c, c + step):
            side = rim[(k - c) * width:(k - c + 1) * width]
            pick = jnp.where(odd, row_p[k:k + 1], row_m[k:k + 1])
            pick = jnp.broadcast_to(pick[None], (width // 8, 8, height)).reshape(width, height)
            value = jnp.where(lane0, 1.0, inv[k]) * (sx0[...] * pick + side * line[0:1, :])
            work[k] = value
            work[k, 0:8, :] = jnp.where(top, row_full[k:k + 1], value[0:8])
    cells_from(out, work, lambda k: work[k], exw[...], eyw[...])


def rims_kernel(depth, s0, s1, bx, ax, py, got_bx, got_ax, from_py, ey, ex, cz, czt, out_rows, out_cols):
    packed = py.shape[0] - 8
    rows = bx.shape[0] - 8
    width = packed * 128 // depth
    _, px = swapped("gx", bx[...], ax[...])
    _, from_px = swapped("gx", got_bx[...], got_ax[...])
    v0 = unpacked_state(s0, rows, width)
    v1 = unpacked_state(s1, rows, width)
    v2 = (
        px[:rows, :] + from_px[:rows, :], None,
        unpack(py[:packed, :] + from_py[:packed, :], depth), None,
        px[rows:rows + 1, :] + from_px[rows:rows + 1, :] + from_py[packed:packed + 1, :],
    )
    at_zero = (lax.broadcasted_iota(jnp.int32, (rows, 128), 0) == 0) & (lane_id((rows, 128)) < depth)
    lines = [rows_back(jnp.where(at_zero, v[4], v[0]), depth) for v in (v0, v1, v2)]
    high = lax.Precision.HIGHEST
    lines = jnp.dot(jnp.concatenate(lines, 0), ey[...], precision=high, preferred_element_type=F32)
    lines = jnp.concatenate([lines[i * depth:(i + 1) * depth] for i in range(3)], 1)
    lines = jnp.dot(cz[...], lines, precision=high, preferred_element_type=F32)
    for i in range(3):
        out_rows[i] = lines[:, i * 128:(i + 1) * 128]
    sides = jnp.concatenate([v[2] for v in (v0, v1, v2)], 1)
    sides = jnp.dot(ex[...], sides, precision=high, preferred_element_type=F32)
    sides = jnp.concatenate([sides[:, i * 128:(i + 1) * 128] for i in range(3)], 0)
    sides = jnp.dot(sides, czt[...], precision=high, preferred_element_type=F32)
    for i in range(3):
        out_cols[i] = sides[i * width:(i + 1) * width]


def final_kernel(n_moments, *refs):
    cells_b, cells_0, cells_1, in_rows, in_cols = refs[:5]
    moms = refs[5:5 + n_moments]
    potential_h, residual_h, potential, residual, sems = refs[5 + n_moments:]
    depth, width, height = cells_b.shape
    m = moms[0][...]
    for other in moms[1:]:
        m = m + other[...]
    m = jnp.broadcast_to(jnp.sum(m, 1, keepdims=True), (8, 128))
    m0 = m[4:5]
    n1, n2, n3 = m[5:6] / m0, m[6:7] / m0, m[7:8] / m0
    det = n1 * n3 - n2 * n2
    fine = det > 1e-6 * (n1 * n3)
    safe = jnp.where(fine, det, 1.0)
    c0 = jnp.where(fine, (n3 - n1 * n2) / safe, 1.0 / n1)
    c1 = jnp.where(fine, (n1 * n1 - n2) / safe, 0.0)
    rim_row = in_rows[0] - c0 * in_rows[1] - c1 * in_rows[2]
    rim_col = in_cols[0] - c0 * in_cols[1] - c1 * in_cols[2]
    top = lax.broadcasted_iota(jnp.int32, (8, height), 0) == 0
    lane0 = lane_id((width, height)) == 0
    step = depth // 4
    copies = []

    def send(src, dst, c):
        at = slice(c, c + step)
        copies.append(pltpu.make_async_copy(src.at[at], dst.at[at], sems.at[len(copies)]))
        copies[-1].start()

    for c in range(0, depth, step):
        for z in range(c, c + step):
            potential[z] = cells_b[z] + c0 * cells_0[z] + c1 * cells_1[z]
        send(potential, potential_h, c)
    for c in range(0, depth, step):
        for z in range(c, c + step):
            flat = jnp.where(lane0, rim_col[:, z:z + 1], 0.0)
            residual[z, 8:, :] = flat[8:]
            residual[z, 0:8, :] = jnp.where(top, rim_row[z:z + 1], flat[0:8])
        send(residual, residual_h, c)
    for copy in copies:
        copy.wait()


def shifted(value, axis, by):
    n = lax.axis_size(axis)
    return lax.ppermute(value, axis, [(i, (i + by) % n) for i in range(n)])


def swap(value, axis, odd):
    n = lax.axis_size(axis)
    pairs = [(i, (i + 1) % n) for i in range(odd, n, 2)]
    return lax.ppermute(value, axis, pairs + [(j, i) for i, j in pairs])


def exchange(bx, ax, by, ay):
    return swap(bx, "gx", 1), swap(ax, "gx", 0), swap(by, "gy", 1), swap(ay, "gy", 0)


def pieces_over(value, axis):
    n, stride = lax.axis_size(axis), 1
    while True:
        radix = 4 if n % 4 == 0 else 2 if n % 2 == 0 else n
        parts = [value] + [shifted(value, axis, stride * j) for j in range(1, radix)]
        n, stride = n // radix, stride * radix
        if n == 1:
            return parts
        value = sum(parts[1:], parts[0])


def reduced_x(bx, ax):
    got_bx, got_ax = swap(bx, "gx", 1), swap(ax, "gx", 0)
    if lax.axis_size("gx") == 4:
        parts = [bx, got_ax, shifted(ax, "gx", 2), got_bx]
        parts = [part[-8:] for part in parts]
    else:
        parts = pieces_over(bx[-8:], "gx")
    return parts, got_bx, got_ax


def reduced_y(value):
    if lax.axis_size("gy") == 4:
        return [value, swap(value, "gy", 0), shifted(value, "gy", 2), swap(value, "gy", 1)]
    return pieces_over(value, "gy")


def call(kernel, outs, scratch, in_specs=None, out_specs=None):
    specs = {}
    if in_specs is not None:
        specs["in_specs"] = in_specs
    if out_specs is not None:
        specs["out_specs"] = out_specs
    return pl.pallas_call(
        kernel,
        out_shape=[jax.ShapeDtypeStruct(o, F32) if isinstance(o, tuple) else o for o in outs],
        scratch_shapes=[pltpu.VMEM(s, F32) if isinstance(s, tuple) else s for s in scratch],
        compiler_params=pltpu.CompilerParams(vmem_limit_bytes=48 * 1024 * 1024),
        **specs,
    )


def on_device(charge, surface_charge):
    depth, width, height = charge.shape
    tab = {name: jnp.asarray(value) for name, value in make_tables(depth, width, height).items()}
    rows, packed = height * depth // 128, width * depth // 128
    msgs = [(rows + 8, 128)] * 2 + [(packed + 8, 128)] * 2
    state = (2 * rows + 2 * width + 8, 128)
    block = (depth, width, height)
    anywhere = pl.BlockSpec(memory_space=pltpu.HBM)
    whole = pl.BlockSpec(memory_space=pltpu.VMEM)
    fronts = (charge, surface_charge) + tuple(tab[n] for n in ("eyw", "exw", "lxy", "sx0", "line"))
    landing = [pltpu.VMEM(x.shape, x.dtype) for x in fronts]
    fronts = [pltpu.with_memory_space_constraint(x, pltpu.HBM) for x in fronts]
    base, inv, rims, *own = call(
        front_kernel, [block, block, jax.ShapeDtypeStruct((depth * width, 2 * height), BF16)] + msgs[:2],
        landing + [block, (depth, 8, height), (depth, 8, height), pltpu.SemaphoreType.DMA((6 + width // 8,))],
        in_specs=[anywhere] * 7,
    )(*fronts)
    own += call(lambda *r: sides_kernel(depth, *r), msgs[2:], [])(rims, tab["rimw"], *own)
    got = exchange(*own)
    cells_b, inv2 = call(base_kernel, [block, (rows, width, 128)], [block])(
        base, tab["eyw"], tab["exw"], tab["lxz"], tab["ly"]
    )
    *got, cells_b = lax.optimization_barrier((*got, cells_b))
    tables = (inv2, tab["rowt"], tab["colt"], tab["crnt"])
    scratch = [(rows, 8, 128), (rows, 128), (rows, 128)]
    s0, *own = call(lambda *r: schur_kernel(depth, False, *r), [state] + msgs, scratch)(*own, *got, *tables)
    got = exchange(*own)
    extend = call(extend_kernel, [block], [block])
    backs = (tab["eyw"], tab["exw"], inv, tab["sx0"], tab["colw"], tab["line"])
    cells_0 = extend(s0, *backs)[0]
    *got, cells_0 = lax.optimization_barrier((*got, cells_0))
    s1, *own = call(lambda *r: schur_kernel(depth, True, *r), [state] + msgs, scratch)(*own, *got, *tables, s0)
    parts, got_bx, got_ax = reduced_x(*own[:2])
    from_py = shifted(own[2], "gy", 1)
    cells_1 = extend(s1, *backs)[0]
    *parts, cells_1 = lax.optimization_barrier((*parts, cells_1))
    parts = reduced_y(sum(parts[1:], parts[0]))
    rim = call(lambda *r: rims_kernel(depth, *r), [(3, depth, height), (3, width, 128)], [])(
        s0, s1, own[0], own[1], own[3], got_bx, got_ax, from_py, tab["ey"], tab["ex"], tab["cz"], tab["czt"]
    )
    return call(
        lambda *r: final_kernel(len(parts), *r), [block, block], [block, block, pltpu.SemaphoreType.DMA((8,))],
        in_specs=[whole] * (5 + len(parts)), out_specs=[anywhere, anywhere],
    )(cells_b, cells_0, cells_1, *rim, *parts)


def solution(mesh):
    spec = P(None, ("slab", "gx"), "gy")
    return jax.shard_map(
        on_device, mesh=mesh, in_specs=(spec, spec), out_specs=(spec, spec), check_vma=False
    )
```

```python
import numpy as np
import jax
import jax.numpy as jnp
from jax import lax
from jax.experimental import pallas as pl
from jax.experimental.pallas import tpu as pltpu
from jax.sharding import PartitionSpec as P
import ml_dtypes

SCREEN = 0.02
BF16 = jnp.bfloat16
F32 = jnp.float32


def sine_ext(n):
    i = np.arange(n)
    table = np.sqrt(2.0 / n) * np.sin(np.pi * np.outer(i, i) / n)
    table[0, 0] = 1.0
    return table


def split_bf16(table):
    hi = table.astype(np.float32).astype(ml_dtypes.bfloat16)
    lo = (table - hi.astype(np.float64)).astype(np.float32).astype(ml_dtypes.bfloat16)
    return hi, lo


def make_tables(depth, width, height):
    lanes = 128
    groups = lanes // depth
    rows = height // groups
    tab = {}
    hi, lo = split_bf16(sine_ext(height))
    tab["eyw"] = np.block([[hi, lo], [hi, np.zeros_like(lo)]])
    hi, lo = split_bf16(sine_ext(width) * np.sqrt(2.0 / depth))
    half = np.block([[hi, hi], [lo, np.zeros_like(lo)]])
    tab["exw"] = np.block([[half, np.zeros_like(half)], [np.zeros_like(half), half]])
    sign = np.where(np.arange(height) % 2 == 1, 1.0, -1.0)
    unit = (np.arange(height) == 0) * 1.0
    wide = np.zeros((height, lanes))
    for g, values in enumerate((1.0 - unit, sign * (1.0 - unit), unit)):
        wide[:, g * depth:(g + 1) * depth] = values[:, None]
    tab["rimw"] = np.concatenate([wide, wide], 0).astype(ml_dtypes.bfloat16)
    wide[0, :depth] = 1.0
    wide[:, 2 * depth:] = 0.0
    tab["colw"] = np.concatenate([wide.T, wide.T], 0).astype(ml_dtypes.bfloat16)
    tab["ey"], tab["ex"] = sine_ext(height).astype(np.float32), sine_ext(width).astype(np.float32)
    z = np.arange(depth)
    cos = np.cos(np.pi * np.outer(z + 0.5, z) / depth) * np.sqrt(2.0 / depth)
    cos[:, 0] = np.sqrt(1.0 / depth)
    tab["cz"] = cos.astype(np.float32)
    czt = np.zeros((lanes, lanes))
    czt[:depth, :depth] = cos.T
    tab["czt"] = czt.astype(np.float32)
    lz = SCREEN + 2.0 - 2.0 * np.cos(np.pi * z / depth)
    a = np.arange(width)
    b = np.arange(height)
    lx = 2.0 - 2.0 * np.cos(np.pi * a / width)
    ly = 2.0 - 2.0 * np.cos(np.pi * b / height)
    sx = np.sqrt(2.0 / width) * np.sin(np.pi * a / width)
    sy = np.sqrt(2.0 / height) * np.sin(np.pi * b / height)
    sga = np.where(a % 2 == 1, 1.0, -1.0)
    sgb = np.where(b % 2 == 1, 1.0, -1.0)
    inside = (a[:, None] > 0) & (b[None, :] > 0)
    inv = np.where(inside[None], 1.0 / (lz[:, None, None] + lx[None, :, None] + ly[None, None, :]), 0.0)
    tab["lxy"] = np.where(inside, lx[:, None] + ly[None, :], 1e30).astype(np.float32)

    def to_rows(kb):
        return kb.T.reshape(groups, rows, depth).transpose(1, 0, 2).reshape(rows, lanes)

    def to_cols(ka):
        return np.tile(ka.T, (1, groups))

    tab["lxz"] = to_cols(np.where(a > 0, lz[:, None] + lx, 1e30)).astype(np.float32)
    tab["ly"] = to_rows(np.ones((depth, 1)) * np.where(b > 0, ly, 1e30)).astype(np.float32)
    ones = np.ones((depth, 1))
    odd_a, odd_b = sga > 0, sgb > 0
    sx2, sy2 = (sx**2)[None, :, None] * inv, (sy**2)[None, None, :] * inv
    tab["rowt"] = np.stack([
        to_rows(ones * sy),
        to_rows(ones * (sy * sgb)),
        to_rows(sx2[:, odd_a].sum(1)),
        to_rows(sx2[:, ~odd_a].sum(1)),
        to_rows((lz[:, None] + 2.0 + ly) * (b > 0)),
    ]).astype(np.float32)
    tab["colt"] = np.stack([
        to_cols(ones * sx),
        to_cols(ones * (sx * sga)),
        to_cols(sy2[:, :, odd_b].sum(2)),
        to_cols(sy2[:, :, ~odd_b].sum(2)),
        to_cols((lz[:, None] + 2.0 + lx) * (a > 0)),
    ]).astype(np.float32)
    tab["crnt"] = np.tile(np.tile(lz + 4.0, groups)[None], (8, 1)).astype(np.float32)
    line = np.where(b > 0, sy, 1.0)[None]
    tab["line"] = np.tile(line, (8, 1)).astype(np.float32)
    tab["sx0"] = np.tile(sx[:, None], (1, height)).astype(np.float32)
    return tab


def cosine_two(xs):
    n = len(xs)
    if n == 1:
        return list(xs)
    half = n // 2
    out = [None] * n
    out[0::2] = cosine_two([xs[j] + xs[n - 1 - j] for j in range(half)])
    out[1::2] = cosine_four([xs[j] - xs[n - 1 - j] for j in range(half)])
    return out


def cosine_three(ys):
    n = len(ys)
    if n == 1:
        return list(ys)
    half = n // 2
    even, odd = cosine_three(ys[0::2]), cosine_four(ys[1::2])
    return [even[j] + odd[j] for j in range(half)] + [even[j] - odd[j] for j in reversed(range(half))]


def cosine_four(xs):
    n = len(xs)
    if n == 1:
        return [xs[0] * float(np.cos(np.pi / 4))]
    half = n // 2
    plus, minus = [], []
    for j in range(half):
        c, s = (float(f(np.pi * (2 * j + 1) / (4 * n))) for f in (np.cos, np.sin))
        x, y = xs[j], xs[n - 1 - j]
        plus.append(x * c + y * s)
        minus.append(x * s - y * c if j % 2 == 0 else y * c - x * s)
    c, s = cosine_two(plus), cosine_two(minus)[::-1]
    out = [None] * n
    out[0], out[n - 1] = c[0], s[half - 1]
    for k in range(1, half):
        out[2 * k] = c[k] - s[k - 1]
        out[2 * k - 1] = c[k] + s[k - 1]
    return out


ROOT_HALF = float(np.sqrt(0.5))


def halves(x):
    hi = x.astype(BF16)
    return hi, (x - hi.astype(F32)).astype(BF16)


def times_sy(x, eyw):
    hi, lo = halves(x)
    n = x.shape[1]
    out = jnp.dot(jnp.concatenate([hi, lo], 1), eyw, preferred_element_type=F32)
    return out[:, :n] + out[:, n:]


def sx_times(exw, xs):
    n = xs[0].shape[0]
    rhs = []
    for x in (jnp.concatenate(xs[:2], 1), jnp.concatenate(xs[2:], 1)):
        rhs += list(halves(x))
    out = jnp.dot(exw, jnp.concatenate(rhs, 0), preferred_element_type=F32)
    width = xs[0].shape[1]
    res = []
    for pair in range(2):
        both = out[2 * pair * n:(2 * pair + 1) * n] + out[(2 * pair + 1) * n:(2 * pair + 2) * n]
        res += [both[:, :width], both[:, width:]]
    return res


def lane_id(shape):
    return lax.broadcasted_iota(jnp.int32, shape, 1)


def by_group(pieces, depth):
    group = lane_id(pieces[0].shape) // depth
    out = pieces[0]
    for h in range(1, len(pieces)):
        out = jnp.where(group == h, pieces[h], out)
    return out


def spread(x, depth):
    width = x.shape[1] // 2
    while width >= depth:
        x = x + pltpu.roll(x, width, 1)
        width //= 2
    return x


def pack(col, depth):
    groups = 128 // depth
    size = col.shape[0] // groups
    return by_group([col[h * size:(h + 1) * size] for h in range(groups)], depth)


def unpack(packed, depth):
    groups = 128 // depth
    group = lane_id(packed.shape) // depth
    return jnp.concatenate(
        [spread(jnp.where(group == h, packed, 0.0), depth) for h in range(groups)], 0
    )


def copies_t(kb):
    groups = 128 // kb.shape[0]
    return jnp.concatenate([kb] * groups, 0).T


def rows_from(kbt, depth):
    groups = 128 // depth
    size = kbt.shape[0] // groups
    return by_group([kbt[h * size:(h + 1) * size] for h in range(groups)], depth)


def rows_back(row, depth):
    groups = 128 // depth
    parts = [row] + [pltpu.roll(row, 128 - h * depth, 1) for h in range(1, groups)]
    return jnp.concatenate(parts, 0).T[:depth]


def total(x):
    return jnp.sum(x, 0, keepdims=True)


def sub_sums(ref):
    plus = minus = None
    for s in range(8):
        part = ref[:, s, :]
        if s % 2 == 1:
            plus = part if plus is None else plus + part
        else:
            minus = part if minus is None else minus + part
    return plus + minus, plus - minus


def with_tail(body, tails, size=8):
    width = body.shape[1]
    rows = list(tails)
    if len(rows) < size:
        rows.append(jnp.zeros((size - len(rows), width), F32))
    return jnp.concatenate([body, jnp.concatenate(rows, 0)], 0)


def front_kernel(charge_h, surf_h, eyw_h, exw_h, lxy_h, sx0_h, line_h, base, inv, rims, *rest):
    msgs = rest[:2]
    charge, surf, eyw, exw, lxy, sx0, line, work, part, first, sems = rest[2:]
    depth, width, height = charge.shape
    tiles = width // 8
    pairs = [(lxy_h, lxy), (surf_h, surf)]
    pairs += [(charge_h.at[:, 8 * i:8 * i + 8, :], charge.at[:, 8 * i:8 * i + 8, :]) for i in range(tiles)]
    pairs += [(eyw_h, eyw), (exw_h, exw), (sx0_h, sx0), (line_h, line)]
    copies = [pltpu.make_async_copy(src, dst, sems.at[i]) for i, (src, dst) in enumerate(pairs)]
    for copy in copies:
        copy.start()
    copies[0].wait()
    for k in range(depth):
        inv[k] = 1.0 / (lxy[...] + float(SCREEN + 2.0 - 2.0 * np.cos(np.pi * k / depth)))
    copies[1].wait()

    for i in range(tiles):
        copies[2 + i].wait()
        at = slice(8 * i, 8 * i + 8)
        xs = [charge[z, at, :] for z in range(depth)]
        xs[0] = xs[0] + surf[0, at, :]
        xs[-1] = xs[-1] + surf[1, at, :]
        for k, value in enumerate(cosine_two(xs)):
            work[k, at, :] = value * ROOT_HALF if k == 0 else value
    for copy in copies[2 + tiles:]:
        copy.wait()
    for c in range(0, depth, 4):
        block = work[c:c + 4].reshape(4 * width, height)
        work[c:c + 4] = times_sy(block, eyw[...]).reshape(4, width, height)
    lane = lane_id((width, 128))
    for c in range(0, depth, 4):
        specs = sx_times(exw[...], [work[k] for k in range(c, c + 4)])
        for k, spec in zip(range(c, c + 4), specs):
            inner = spec * inv[k]
            base[k] = inner
            first[k] = spec[0:8]
            part[k] = jnp.sum((inner * sx0[...]).reshape(width // 8, 8, height), 0)
            hi, lo = halves(jnp.where(lane == 0, spec, inner * line[0:1, :]))
            rims[k * width:(k + 1) * width, :] = jnp.concatenate([hi, lo], 1)
    row_near, row_far = sub_sums(part)
    own_t = copies_t(first[:, 0, :])
    corner = own_t[0:1]
    row = rows_from(own_t + copies_t(row_near), depth)
    at_zero = (lax.broadcasted_iota(jnp.int32, row.shape, 0) == 0) & (lane_id(row.shape) < depth)
    row = jnp.where(at_zero, 0.0, row)
    px = with_tail(row, [corner])
    nx = with_tail(rows_from(copies_t(row_far), depth), [])
    for ref, value in zip(msgs, swapped("gx", nx, px)):
        ref[...] = value


def sides_kernel(depth, rims, rimw, bx, ax, by, ay):
    width = rims.shape[0] // depth
    lane = lane_id((width, 128))
    step = 8
    found = jnp.zeros((width, 128), F32)
    for c in range(0, depth, step):
        out = jnp.dot(rims[c * width:(c + step) * width, :], rimw[...], preferred_element_type=F32)
        for k in range(c, c + step):
            one = out[(k - c) * width:(k - c + 1) * width]
            found = jnp.where(lane % depth == k, one, found)
    near, far, own = (spread(jnp.where(lane // depth == g, found, 0.0), depth) for g in range(3))
    _, px = swapped("gx", bx[...], ax[...])
    corner = px[px.shape[0] - 8:px.shape[0] - 7]
    col = jnp.where(lax.broadcasted_iota(jnp.int32, own.shape, 0) == 0, 0.0, own + near)
    py = with_tail(pack(col, depth), [corner])
    ny = with_tail(pack(far, depth), [])
    for ref, value in zip((by, ay), swapped("gy", ny, py)):
        ref[...] = value


def swapped(axis, after, before):
    even = lax.axis_index(axis) % 2 == 0
    return jnp.where(even, before, after), jnp.where(even, after, before)


def assemble(depth, own, got):
    (nx, px), (ny, py) = swapped("gx", *own[:2]), swapped("gy", *own[2:])
    (from_nx, from_px), (from_ny, from_py) = swapped("gx", *got[:2]), swapped("gy", *got[2:])
    rows, cols = px.shape[0] - 8, py.shape[0] - 8
    row = px[:rows] + from_px[:rows]
    row_n = from_nx[:rows] + nx[:rows]
    col = unpack(py[:cols] + from_py[:cols], depth)
    col_n = unpack(from_ny[:cols] + ny[:cols], depth)
    c00 = px[rows:rows + 1] + from_px[rows:rows + 1] + from_py[cols:cols + 1]
    cx0 = from_nx[rows:rows + 1] + nx[rows:rows + 1] + from_py[cols + 1:cols + 2]
    c0y = from_ny[cols:cols + 1] + ny[cols:cols + 1] + from_px[rows + 1:rows + 2]
    return row, row_n, col, col_n, c00, cx0, c0y


def sizes(rows, cols):
    offs = np.cumsum([0, rows, rows, cols, cols])
    return [slice(int(offs[i]), int(offs[i + 1])) for i in range(4)] + [int(offs[4])]


def unpacked_state(state, rows, cols):
    s = sizes(rows, cols)
    at = s[4]
    return tuple(state[s[i], :] for i in range(4)) + tuple(state[at + i:at + i + 1, :] for i in range(3))


def schur_kernel(depth, mode, *refs):
    inv2, rowt, colt, crnt = refs[:4]
    rest = list(refs[4:])
    part, odd_rows, even_rows = rest[-3:]
    with_rows, with_cols, want_moments = mode != "cols", mode != "rows", mode == "last"
    if mode == "cols":
        state, *outs = rest[:3]
        cols = inv2.shape[1]
        rows = inv2.shape[0]
        row, row_n, col, col_n, c00, cx0, c0y = unpacked_state(state, rows, cols)
    else:
        own, got = [r[...] for r in rest[0:4]], [r[...] for r in rest[4:8]]
        rest = rest[8:]
        before = rest.pop(0) if want_moments else None
        state, *outs = rest[:-3]
        row, row_n, col, col_n, c00, cx0, c0y = assemble(depth, own, got)
        rows, cols = row.shape[0], col.shape[0]
        s = sizes(rows, cols)
        for i, piece in enumerate((row, row_n, col, col_n)):
            state[s[i], :] = piece
        state[s[4]:s[4] + 8, :] = jnp.concatenate([c00, cx0, c0y, jnp.zeros((5, 128), F32)], 0)
    sy, sys, g_odd, g_even, d_row = (rowt[i] for i in range(5))
    sx, sxs, h_odd, h_even, d_col = (colt[i] for i in range(5))
    row_p, row_m, col_p, col_m = row + row_n, row - row_n, col + col_n, col - col_n
    if with_cols:
        odd_rows[...] = row_p * sy
        even_rows[...] = row_m * sy
    col_w = (col_m * sx, col_p * sx)
    odd = lax.broadcasted_iota(jnp.int32, (8, 128), 0) % 2 == 1
    acc = [None, None]
    for r in range(rows):
        table = inv2[r].reshape(cols // 8, 8, 128)
        if with_rows:
            part[r] = jnp.sum(table * col_w[r % 2].reshape(cols // 8, 8, 128), 0)
        if with_cols:
            pick = jnp.where(odd, odd_rows[r:r + 1, :], even_rows[r:r + 1, :])
            term = table * pick[None]
            acc[r % 2] = term if acc[r % 2] is None else acc[r % 2] + term
    if with_rows:
        row_s, row_d = sub_sums(part)
        diag_o, diag_e = g_odd * row_p, g_even * row_m
        x_near = sy * row_s + (diag_o + diag_e)
        x_far = sy * row_d + (diag_o - diag_e)
        row_img = d_row * row - sy * c00 - sys * c0y - x_near
    if with_cols:
        acc_s = spread((acc[1] + acc[0]).reshape(cols, 128), depth)
        acc_d = spread((acc[1] - acc[0]).reshape(cols, 128), depth)
        diag_o, diag_e = h_odd * col_p, h_even * col_m
        y_near = sx * acc_s + (diag_o + diag_e)
        y_far = sx * acc_d + (diag_o - diag_e)
        col_img = d_col * col - sx * c00 - sxs * cx0 - y_near
    row_end0 = spread(total(sy * row), depth)
    row_end1 = spread(total(sys * row), depth)
    row_end1n = spread(total(sys * row_n), depth)
    col_end0 = total(sx * col)
    col_end1 = total(sxs * col)
    col_end1n = total(sxs * col_n)
    q00 = crnt[0:1, :] * c00 - row_end0 - col_end0
    if mode == "rows":
        px = with_tail(row_img, [q00])
        nx = with_tail(-x_far, [-col_end1, -col_end1n])
        values = swapped("gx", nx, px)
    if with_cols:
        py = with_tail(pack(col_img, depth), [q00])
        ny = with_tail(pack(-y_far, depth), [-row_end1, -row_end1n])
        values = swapped("gy", ny, py)
    if want_moments:
        row0, _, col0, _, c000, _, _ = unpacked_state(before, rows, cols)
        share = depth / 128.0

        def dot(x, y):
            return total(x[0] * y[0]) + share * (total(x[1] * y[1]) + x[2] * y[2])

        v0, v1 = (row0, col0, c000), (row, col, c00)
        m3 = total(row * row_img - row_n * x_far) + share * (
            total(col * col_img - col_n * y_far) + c00 * q00 - c0y * row_end1 - cx0 * col_end1
        )
        moments = [dot(v0, v0), dot(v0, v1), dot(v1, v1), m3]
        px = with_tail(row_img, [q00, q00, q00, q00] + moments)
        nx = with_tail(-x_far, [-col_end1, -col_end1n, c00, c00] + moments)
        values = swapped("gx", nx, px) + (ny, py)
    for ref, value in zip(outs, values):
        ref[...] = value


def cells_from(out, work, spectrum, exw, eyw):
    depth, width, height = work.shape
    for c in range(0, depth, 4):
        for k, cells in zip(range(c, c + 4), sx_times(exw, [spectrum(k) for k in range(c, c + 4)])):
            work[k] = cells
    step = 4
    for c in range(0, depth, step):
        block = work[c:c + step].reshape(step * width, height)
        work[c:c + step] = times_sy(block, eyw).reshape(step, width, height)
    for i in range(width // 8):
        at = slice(8 * i, 8 * i + 8)
        ys = [work[k, at, :] for k in range(depth)]
        for z, value in enumerate(cosine_three([ys[0] * ROOT_HALF] + ys[1:])):
            out[z, at, :] = value


def base_kernel(base, eyw, exw, lxz, ly, out, inv2, work):
    for r in range(inv2.shape[0]):
        inv2[r] = 1.0 / (lxz[...] + ly[r:r + 1, :])
    cells_from(out, work, lambda k: base[k], exw[...], eyw[...])


def extend_kernel(state, eyw, exw, inv, sx0, colw, line, out, work):
    depth, width, height = work.shape
    rows = height * depth // 128
    row, row_n, col, col_n, c00 = unpacked_state(state, rows, width)[:5]
    at_zero = (lax.broadcasted_iota(jnp.int32, row.shape, 0) == 0) & (lane_id(row.shape) < depth)
    row_p = rows_back(row + row_n, depth)
    row_m = rows_back(row - row_n, depth)
    row_full = rows_back(jnp.where(at_zero, c00, row), depth)
    odd = lax.broadcasted_iota(jnp.int32, (8, height), 0) % 2 == 1
    top = lax.broadcasted_iota(jnp.int32, (8, height), 0) == 0
    lane0 = lane_id((width, height)) == 0
    lane = lane_id((width, 256)) % depth
    hi, lo = halves(by_group([col, col_n] + [jnp.zeros_like(col)] * (128 // depth - 2), depth))
    both = jnp.concatenate([hi, lo], 1)
    step = 8
    for c in range(0, depth, step):
        rim = jnp.concatenate([jnp.where(lane == k, both, jnp.zeros_like(both)) for k in range(c, c + step)], 0)
        rim = jnp.dot(rim, colw[...], preferred_element_type=F32)
        for k in range(c, c + step):
            side = rim[(k - c) * width:(k - c + 1) * width]
            pick = jnp.where(odd, row_p[k:k + 1], row_m[k:k + 1])
            pick = jnp.broadcast_to(pick[None], (width // 8, 8, height)).reshape(width, height)
            value = jnp.where(lane0, 1.0, inv[k]) * (sx0[...] * pick + side * line[0:1, :])
            work[k] = value
            work[k, 0:8, :] = jnp.where(top, row_full[k:k + 1], value[0:8])
    cells_from(out, work, lambda k: work[k], exw[...], eyw[...])


def rims_kernel(depth, s0, s1, bx, ax, py, got_bx, got_ax, from_py, ey, ex, cz, czt, out_rows, out_cols):
    packed = py.shape[0] - 8
    rows = bx.shape[0] - 8
    width = packed * 128 // depth
    _, px = swapped("gx", bx[...], ax[...])
    _, from_px = swapped("gx", got_bx[...], got_ax[...])
    v0 = unpacked_state(s0, rows, width)
    v1 = unpacked_state(s1, rows, width)
    v2 = (
        px[:rows, :] + from_px[:rows, :], None,
        unpack(py[:packed, :] + from_py[:packed, :], depth), None,
        px[rows:rows + 1, :] + from_px[rows:rows + 1, :] + from_py[packed:packed + 1, :],
    )
    at_zero = (lax.broadcasted_iota(jnp.int32, (rows, 128), 0) == 0) & (lane_id((rows, 128)) < depth)
    lines = [rows_back(jnp.where(at_zero, v[4], v[0]), depth) for v in (v0, v1, v2)]
    high = lax.Precision.HIGHEST
    lines = jnp.dot(jnp.concatenate(lines, 0), ey[...], precision=high, preferred_element_type=F32)
    lines = jnp.concatenate([lines[i * depth:(i + 1) * depth] for i in range(3)], 1)
    lines = jnp.dot(cz[...], lines, precision=high, preferred_element_type=F32)
    for i in range(3):
        out_rows[i] = lines[:, i * 128:(i + 1) * 128]
    sides = jnp.concatenate([v[2] for v in (v0, v1, v2)], 1)
    sides = jnp.dot(ex[...], sides, precision=high, preferred_element_type=F32)
    sides = jnp.concatenate([sides[:, i * 128:(i + 1) * 128] for i in range(3)], 0)
    sides = jnp.dot(sides, czt[...], precision=high, preferred_element_type=F32)
    for i in range(3):
        out_cols[i] = sides[i * width:(i + 1) * width]


def final_kernel(n_moments, *refs):
    cells_b, cells_0, cells_1, in_rows, in_cols = refs[:5]
    moms = refs[5:5 + n_moments]
    potential_h, residual_h, potential, residual, sems = refs[5 + n_moments:]
    depth, width, height = cells_b.shape
    m = moms[0][...]
    for other in moms[1:]:
        m = m + other[...]
    m = jnp.broadcast_to(jnp.sum(m, 1, keepdims=True), (8, 128))
    m0 = m[4:5]
    n1, n2, n3 = m[5:6] / m0, m[6:7] / m0, m[7:8] / m0
    det = n1 * n3 - n2 * n2
    fine = det > 1e-6 * (n1 * n3)
    safe = jnp.where(fine, det, 1.0)
    c0 = jnp.where(fine, (n3 - n1 * n2) / safe, 1.0 / n1)
    c1 = jnp.where(fine, (n1 * n1 - n2) / safe, 0.0)
    rim_row = in_rows[0] - c0 * in_rows[1] - c1 * in_rows[2]
    rim_col = in_cols[0] - c0 * in_cols[1] - c1 * in_cols[2]
    top = lax.broadcasted_iota(jnp.int32, (8, height), 0) == 0
    lane0 = lane_id((width, height)) == 0
    step = depth // 4
    copies = []

    def send(src, dst, c):
        at = slice(c, c + step)
        copies.append(pltpu.make_async_copy(src.at[at], dst.at[at], sems.at[len(copies)]))
        copies[-1].start()

    for c in range(0, depth, step):
        for z in range(c, c + step):
            potential[z] = cells_b[z] + c0 * cells_0[z] + c1 * cells_1[z]
        send(potential, potential_h, c)
    for c in range(0, depth, step):
        for z in range(c, c + step):
            flat = jnp.where(lane0, rim_col[:, z:z + 1], 0.0)
            residual[z, 8:, :] = flat[8:]
            residual[z, 0:8, :] = jnp.where(top, rim_row[z:z + 1], flat[0:8])
        send(residual, residual_h, c)
    for copy in copies:
        copy.wait()


def shifted(value, axis, by):
    n = lax.axis_size(axis)
    return lax.ppermute(value, axis, [(i, (i + by) % n) for i in range(n)])


def swap(value, axis, odd):
    n = lax.axis_size(axis)
    pairs = [(i, (i + 1) % n) for i in range(odd, n, 2)]
    return lax.ppermute(value, axis, pairs + [(j, i) for i, j in pairs])


def exchange(bx, ax, by, ay):
    return swap(bx, "gx", 1), swap(ax, "gx", 0), swap(by, "gy", 1), swap(ay, "gy", 0)


def pieces_over(value, axis):
    n, stride = lax.axis_size(axis), 1
    while True:
        radix = 4 if n % 4 == 0 else 2 if n % 2 == 0 else n
        parts = [value] + [shifted(value, axis, stride * j) for j in range(1, radix)]
        n, stride = n // radix, stride * radix
        if n == 1:
            return parts
        value = sum(parts[1:], parts[0])


def reduced_x(bx, ax):
    got_bx, got_ax = swap(bx, "gx", 1), swap(ax, "gx", 0)
    if lax.axis_size("gx") == 4:
        parts = [bx, got_ax, shifted(ax, "gx", 2), got_bx]
        parts = [part[-8:] for part in parts]
    else:
        parts = pieces_over(bx[-8:], "gx")
    return parts, got_bx, got_ax


def reduced_y(value):
    if lax.axis_size("gy") == 4:
        return [value, swap(value, "gy", 0), shifted(value, "gy", 2), swap(value, "gy", 1)]
    return pieces_over(value, "gy")


def call(kernel, outs, scratch, in_specs=None, out_specs=None):
    specs = {}
    if in_specs is not None:
        specs["in_specs"] = in_specs
    if out_specs is not None:
        specs["out_specs"] = out_specs
    return pl.pallas_call(
        kernel,
        out_shape=[jax.ShapeDtypeStruct(o, F32) if isinstance(o, tuple) else o for o in outs],
        scratch_shapes=[pltpu.VMEM(s, F32) if isinstance(s, tuple) else s for s in scratch],
        compiler_params=pltpu.CompilerParams(vmem_limit_bytes=48 * 1024 * 1024),
        **specs,
    )


def on_device(charge, surface_charge):
    depth, width, height = charge.shape
    tab = {name: jnp.asarray(value) for name, value in make_tables(depth, width, height).items()}
    rows, packed = height * depth // 128, width * depth // 128
    msgs = [(rows + 8, 128)] * 2 + [(packed + 8, 128)] * 2
    state = (2 * rows + 2 * width + 8, 128)
    block = (depth, width, height)
    anywhere = pl.BlockSpec(memory_space=pltpu.HBM)
    whole = pl.BlockSpec(memory_space=pltpu.VMEM)
    fronts = (charge, surface_charge) + tuple(tab[n] for n in ("eyw", "exw", "lxy", "sx0", "line"))
    landing = [pltpu.VMEM(x.shape, x.dtype) for x in fronts]
    fronts = [pltpu.with_memory_space_constraint(x, pltpu.HBM) for x in fronts]
    base, inv, rims, *own = call(
        front_kernel, [block, block, jax.ShapeDtypeStruct((depth * width, 2 * height), BF16)] + msgs[:2],
        landing + [block, (depth, 8, height), (depth, 8, height), pltpu.SemaphoreType.DMA((6 + width // 8,))],
        in_specs=[anywhere] * 7,
    )(*fronts)
    own += call(lambda *r: sides_kernel(depth, *r), msgs[2:], [])(rims, tab["rimw"], *own)
    got = exchange(*own)
    cells_b, inv2 = call(base_kernel, [block, (rows, width, 128)], [block])(
        base, tab["eyw"], tab["exw"], tab["lxz"], tab["ly"]
    )
    *got, cells_b = lax.optimization_barrier((*got, cells_b))
    tables = (inv2, tab["rowt"], tab["colt"], tab["crnt"])
    scratch = [(rows, 8, 128), (rows, 128), (rows, 128)]
    s0, *own = call(lambda *r: schur_kernel(depth, "rows", *r), [state] + msgs[:2], scratch)(*tables, *own, *got)
    own += call(lambda *r: schur_kernel(depth, "cols", *r), msgs[2:], scratch)(*tables, s0)
    got = exchange(*own)
    extend = call(extend_kernel, [block], [block])
    backs = (tab["eyw"], tab["exw"], inv, tab["sx0"], tab["colw"], tab["line"])
    cells_0 = extend(s0, *backs)[0]
    *got, cells_0 = lax.optimization_barrier((*got, cells_0))
    s1, *own = call(lambda *r: schur_kernel(depth, "last", *r), [state] + msgs, scratch)(*tables, *own, *got, s0)
    parts, got_bx, got_ax = reduced_x(*own[:2])
    from_py = shifted(own[2], "gy", 1)
    cells_1 = extend(s1, *backs)[0]
    *parts, cells_1 = lax.optimization_barrier((*parts, cells_1))
    parts = reduced_y(sum(parts[1:], parts[0]))
    rim = call(lambda *r: rims_kernel(depth, *r), [(3, depth, height), (3, width, 128)], [])(
        s0, s1, own[0], own[1], own[3], got_bx, got_ax, from_py, tab["ey"], tab["ex"], tab["cz"], tab["czt"]
    )
    return call(
        lambda *r: final_kernel(len(parts), *r), [block, block], [block, block, pltpu.SemaphoreType.DMA((8,))],
        in_specs=[whole] * (5 + len(parts)), out_specs=[anywhere, anywhere],
    )(cells_b, cells_0, cells_1, *rim, *parts)


def solution(mesh):
    spec = P(None, ("slab", "gx"), "gy")
    return jax.shard_map(
        on_device, mesh=mesh, in_specs=(spec, spec), out_specs=(spec, spec), check_vma=False
    )
```
